32 devices in a mesh: clip: 2 (over y), wide: 8 (over z, core), tp: 2 (over x).
Axes of the slice: x: 2, y: 2, z: 4, core: 2. Of those that a mesh axis runs over, the one named last changes fastest.
Arguments:
- frames_a: bfloat16 [4, 16, 256, 1024], P('clip', 'wide'), may hold values from -6 to 6
- frames_b: bfloat16 [4, 16, 64, 1024], P('clip', 'wide'), may hold values from -6 to 6
- actions_a: int32 [4, 16], P('clip', 'wide'), may hold values from 0 to 7
- actions_b: int32 [4, 16], P('clip', 'wide'), may hold values from 0 to 7
- action_table: bfloat16 [8, 1024], replicated, may hold values from -3 to 3
- gain_space: float32 [1024], replicated, may hold values from 0.5 to 1.5
- space_qkv: bfloat16 [3, 1024, 1024], P(None, None, 'tp'), may hold values from -0.1875 to 0.1875
- space_out: bfloat16 [1024, 1024], P('tp'), may hold values from -0.5 to 0.5
- gain_time: float32 [1024], replicated, may hold values from 0.5 to 1.5
- time_qkv: bfloat16 [3, 1024, 1024], P(None, None, 'tp'), may hold values from -0.1875 to 0.1875
- time_out: bfloat16 [1024, 1024], P('tp'), may hold values from -0.25 to 0.25
- gain_ffn: float32 [1024], replicated, may hold values from 0.5 to 1.5
- ffn_up: bfloat16 [1024, 4096], P(None, 'tp'), may hold values from -0.1875 to 0.1875
- ffn_down: bfloat16 [4096, 1024], P('tp'), may hold values from -0.09375 to 0.09375
- cot_a: bfloat16 [4, 16, 256, 1024], P('clip', 'wide'), may hold values from -6 to 6
- cot_b: bfloat16 [4, 16, 64, 1024], P('clip', 'wide'), may hold values from -6 to 6
Outputs:
- out_a: bfloat16 [4, 16, 256, 1024], P('clip', 'wide')
- out_b: bfloat16 [4, 16, 64, 1024], P('clip', 'wide')
- d_frames_a: bfloat16 [4, 16, 256, 1024], P('clip', 'wide')
- d_frames_b: bfloat16 [4, 16, 64, 1024], P('clip', 'wide')
- d_action_table: float32 [8, 1024], P(None, 'wide')
- d_gain_space: float32 [1024], P('wide')
- d_space_qkv: float32 [3, 1024, 1024], P(None, 'wide', 'tp')
- d_space_out: float32 [1024, 1024], P('tp', 'wide')
- d_gain_time: float32 [1024], P('wide')
- d_time_qkv: float32 [3, 1024, 1024], P(None, 'wide', 'tp')
- d_time_out: float32 [1024, 1024], P('tp', 'wide')
- d_gain_ffn: float32 [1024], P('wide')
- d_ffn_up: float32 [1024, 4096], P('wide', 'tp')
- d_ffn_down: float32 [4096, 1024], P('tp', 'wide')
The draws below stay inside these ranges and needn't reach their ends.
All inputs are finite; a program needn't handle non-finite values.
Results may differ from the reference program's by a relative error of at most 0.03.
Values may be sent and summed in bfloat16 or wider, within the bound.
No kernel may reach another device: no remote copies, remote signals or barrier semaphores. Data moves between devices by JAX's collectives and lax.ppermute only.
A program may use at most 192 MiB of HBM per device.

```python
import jax
import jax.numpy as jnp
from jax import lax

D = 1024
HEADS = 16
HEAD = 64
FF = 4096
ACTIONS = 8
F = 16
GA = 256
GB = 64
CLIPS_A = 4
CLIPS_B = 4


def plant(array, key, low, high):
    dims = array.shape
    spot = [jax.random.randint(jax.random.fold_in(key, axis), (), 0, dims[axis]) for axis in range(len(dims))]
    array = array.at[tuple(spot)].set(low)
    longest = dims.index(max(dims))
    spot[longest] = (spot[longest] + 1) % dims[longest]
    return array.at[tuple(spot)].set(high)


def raised(result, stream_key, source, target, parts, factor):
    owner, partner = [(jnp.arange(result.shape[axis_at]) // (result.shape[axis_at] // parts)).reshape([-1 if axis == axis_at else 1 for axis in range(result.ndim)]) for axis_at in (source, target)]
    chosen = jax.random.permutation(stream_key, parts)[partner]
    strong = (owner == chosen) | (owner == (partner + parts // 2) % parts)
    return jnp.where(strong, factor * result, result)


def levels(key, shape, pieces, least, largest):
    def one(dim, parts):
        draws = jax.random.uniform(jax.random.fold_in(jax.random.fold_in(key, 6), dim), (parts,), jnp.float32, least / len(pieces), largest / len(pieces))
        return jnp.repeat(jnp.exp(draws), shape[dim] // parts).reshape((-1,) + (1,) * (len(shape) - dim - 1))

    factor_of = one(*pieces[0])
    for cut in pieces[1:]:
        factor_of = factor_of * one(*cut)
    return factor_of


def normal_values(stream_key, shape, scale, most, shards=(), held_as=jnp.bfloat16):
    values = jax.random.normal(stream_key, shape, jnp.float32) * scale
    if len(shards) > 0:
        values = levels(stream_key, shape, shards, -0.22, 0.18) * values
    return jnp.clip(values, min=-most, max=most).astype(held_as)


def heavy_noise(stream_key, dims, width, limit, cuts, heavy, dtype=jnp.bfloat16):
    result = width * jax.random.normal(stream_key, dims, jnp.float32)
    if cuts:
        result = result * levels(stream_key, dims, cuts, -0.22, 0.18)
    return jnp.clip(raised(result, jax.random.fold_in(stream_key, 3), *heavy), -limit, limit).astype(dtype)


def setup_inputs(seed: int = 0) -> dict:
    splits = jax.random.split(jax.random.key(seed), 17)
    frames_a = normal_values(splits[0], (CLIPS_A, F, GA, D), 1.0, 6.0, ((0, 2), (1, 8)))
    frames_b = normal_values(splits[1], (CLIPS_B, F, GB, D), 1.0, 6.0, ((0, 2), (1, 8)))
    actions_a = plant(jax.random.randint(splits[2], (CLIPS_A, F), 0, ACTIONS), jax.random.fold_in(splits[2], 1), 0, ACTIONS - 1).astype(jnp.int32)
    actions_b = plant(jax.random.randint(splits[3], (CLIPS_B, F), 0, ACTIONS), jax.random.fold_in(splits[3], 1), 0, ACTIONS - 1).astype(jnp.int32)
    action_table = normal_values(splits[4], (ACTIONS, D), 0.5, 3.0)
    gain_space = jnp.clip(1.0 + 0.1 * jax.random.normal(splits[5], (D,), jnp.float32), 0.5, 1.5)
    space_qkv = normal_values(splits[6], (3, D, D), D ** -0.5, 0.1875, ((2, 2),))
    space_out = normal_values(splits[7], (D, D), (D // 8) ** -0.5, 0.5, ((0, 2),))
    gain_time = jnp.clip(1.0 + 0.1 * jax.random.normal(splits[8], (D,), jnp.float32), 0.5, 1.5)
    time_qkv = normal_values(splits[9], (3, D, D), D ** -0.5, 0.1875, ((2, 2),))
    time_out = normal_values(splits[10], (D, D), (D // 2) ** -0.5, 0.25, ((0, 2),))
    gain_ffn = jnp.clip(1.0 + 0.1 * jax.random.normal(splits[11], (D,), jnp.float32), 0.5, 1.5)
    ffn_up = normal_values(splits[12], (D, FF), D ** -0.5, 0.1875, ((1, 2),))
    ffn_down = normal_values(splits[13], (FF, D), FF ** -0.5, 0.09375, ((0, 2),))
    cot_a = heavy_noise(splits[14], (CLIPS_A, F, GA, D), 1.0, 6.0, ((0, 2), (1, 8)), (1, 3, 8, 2.0))
    cot_b = heavy_noise(splits[15], (CLIPS_B, F, GB, D), 1.0, 6.0, ((0, 2), (1, 8)), (1, 3, 8, 2.0))
    return {"frames_a": frames_a, "frames_b": frames_b, "actions_a": actions_a, "actions_b": actions_b, "action_table": action_table, "gain_space": gain_space, "space_qkv": space_qkv, "space_out": space_out, "gain_time": gain_time, "time_qkv": time_qkv, "time_out": time_out, "gain_ffn": gain_ffn, "ffn_up": ffn_up, "ffn_down": ffn_down, "cot_a": cot_a, "cot_b": cot_b}


@jax.custom_vjp
def low(v):
    return lax.optimization_barrier(v.astype(jnp.bfloat16)).astype(jnp.float32)

@jax.custom_vjp
def low_back(v):
    return v

def low_keep(v):
    return (low(v), None)

def low_pass(kept, grad):
    return (grad,)

def back_keep(v):
    return (v, None)

def back_low(kept, grad):
    return (low(grad),)
low.defvjp(low_keep, low_pass)
low_back.defvjp(back_keep, back_low)

def layer_norm(values, gain_vec):
    centered = values - lax.optimization_barrier(jnp.mean(values, -1, keepdims=True))
    spread = lax.optimization_barrier(jnp.mean(centered * centered, -1, keepdims=True))
    return centered * lax.rsqrt(spread + 1e-05) * gain_vec

def attention(normed, weight_qkv, weight_out, causal):
    projected = jnp.einsum('nlpd,tde->tnlpe', normed, weight_qkv, precision=lax.Precision.HIGHEST)
    projected = low_back(low(projected))
    projected = projected.reshape(projected.shape[:4] + (HEADS, HEAD))
    scores = jnp.einsum('nqphe,nkphe->nphqk', projected[0], projected[1], precision=lax.Precision.HIGHEST) * HEAD ** (-0.5)
    scores = low_back(scores)
    if causal:
        length = scores.shape[-1]
        allowed = jnp.arange(length)[:, None] >= jnp.arange(length)[None, :]
        scores = jnp.where(allowed, scores, -1e+30)
    shifted = jnp.exp(scores - lax.optimization_barrier(jnp.max(scores, -1, keepdims=True)))
    attn_probs = low(shifted / lax.optimization_barrier(jnp.sum(shifted, -1, keepdims=True)))
    head_out = jnp.einsum('nphqk,nkphe->nqphe', attn_probs, projected[2], precision=lax.Precision.HIGHEST)
    head_out = low_back(low(head_out)).reshape(normed.shape)
    return low_back(jnp.einsum('nlpe,ed->nlpd', head_out, weight_out, precision=lax.Precision.HIGHEST))

def clip_forward(clip_frames, clip_actions, params):
    table_rows, gain_space, space_qkv, space_out, gain_time, time_qkv, time_out, gain_ffn, ffn_up, ffn_down = params
    started = clip_frames + table_rows[clip_actions][:, None, :]
    normed = low(layer_norm(started, gain_space))[:, :, None, :]
    middle = low_back(low(started + attention(normed, space_qkv, space_out, False)[:, :, 0, :]))
    normed = low(layer_norm(middle, gain_time))[None]
    latest = low_back(low(middle + attention(normed, time_qkv, time_out, True)[0]))
    normed = low(layer_norm(latest, gain_ffn))
    hidden = low_back(jnp.einsum('fgd,de->fge', normed, ffn_up, precision=lax.Precision.HIGHEST))
    gelu_out = low(jax.nn.gelu(hidden, approximate=True))
    return latest + low_back(jnp.einsum('fge,ed->fgd', gelu_out, ffn_down, precision=lax.Precision.HIGHEST))

def forward(first_frames, second_frames, first_actions, second_actions, params):
    clip_step = jax.checkpoint(clip_forward)

    def run_clip(clip_pair):
        return clip_step(clip_pair[0], clip_pair[1], params)
    return (lax.map(run_clip, (first_frames, first_actions)), lax.map(run_clip, (second_frames, second_actions)))

def widen(array_in):
    return array_in.astype(jnp.float32)

def reference(frames_a, frames_b, actions_a, actions_b, action_table, gain_space, space_qkv, space_out, gain_time, time_qkv, time_out, gain_ffn, ffn_up, ffn_down, cot_a, cot_b):
    params = (widen(action_table), widen(gain_space), widen(space_qkv), widen(space_out), widen(gain_time), widen(time_qkv), widen(time_out), widen(gain_ffn), widen(ffn_up), widen(ffn_down))

    def whole_block(first_frames, second_frames, weights):
        return forward(first_frames, second_frames, actions_a, actions_b, weights)
    outputs, pullback = jax.vjp(whole_block, widen(frames_a), widen(frames_b), params)
    grad_first, grad_second, grad_weights = pullback((widen(cot_a), widen(cot_b)))
    return (outputs[0].astype(jnp.bfloat16), outputs[1].astype(jnp.bfloat16), grad_first.astype(jnp.bfloat16), grad_second.astype(jnp.bfloat16), grad_weights[0], grad_weights[1], grad_weights[2], grad_weights[3], grad_weights[4], grad_weights[5], grad_weights[6], grad_weights[7], grad_weights[8], grad_weights[9])
```

```python
from functools import partial

import jax
import jax.numpy as jnp
from jax import lax
from jax.experimental import pallas as pl
from jax.experimental.pallas import tpu as pltpu
from jax.sharding import PartitionSpec as P

HEAD = 64
PAIR = 2 * HEAD
BF = jnp.bfloat16
F32 = jnp.float32


def group_mask(kind, rows, length):
    if kind is None:
        return None
    name, size = kind
    query = lax.broadcasted_iota(jnp.int32, (rows, length), 0) & (length - 1)
    key = lax.broadcasted_iota(jnp.int32, (rows, length), 1)
    shift = size.bit_length() - 1
    same = (query >> shift) == (key >> shift)
    if name == "causal":
        same = same & (key <= query)
    return same


def head_factors(value):
    lane = lax.broadcasted_iota(jnp.int32, (1, PAIR), 1)
    first = jnp.where(lane < HEAD, value, 0.0).astype(BF)
    second = jnp.where(lane < HEAD, 0.0, value).astype(BF)
    return first, second


def dot_t(a, b):
    return lax.dot_general(a, b, (((1,), (1,)), ((), ())), preferred_element_type=F32)


def dot_n(a, b):
    return lax.dot_general(a, b, (((1,), (0,)), ((), ())), preferred_element_type=F32)


def dot_l(a, b):
    return lax.dot_general(a, b, (((0,), (0,)), ((), ())), preferred_element_type=F32)


def attend_kernel(groups, p_ref, o_ref, l_ref):
    first, second = head_factors(1.0)
    q_first, q_second = head_factors(HEAD**-0.5)
    left = lax.broadcasted_iota(jnp.int32, (1, PAIR), 1) < HEAD
    for start, length, kind in groups:
        rows = slice(start, start + length)
        query, key, value = (p_ref[i, rows, :] for i in range(3))
        outs, logs = [], []
        for q_part, v_part in ((q_first, first), (q_second, second)):
            scores = dot_t(query * q_part, key)
            mask = group_mask(kind, length, length)
            if mask is not None:
                scores = jnp.where(mask, scores, -1e30)
            largest = jnp.max(scores, -1, keepdims=True)
            shifted = jnp.exp(scores - largest)
            total = jnp.sum(shifted, -1, keepdims=True)
            soft = (shifted / total).astype(BF)
            outs.append(dot_n(soft, value * v_part))
            logs.append(largest + jnp.log(total))
        o_ref[rows, :] = (outs[0] + outs[1]).astype(BF)
        l_ref[rows, :] = jnp.where(left, logs[0], logs[1])


def attend_back_kernel(groups, p_ref, d_ref, l_ref, o_ref):
    first, second = head_factors(1.0)
    scale = HEAD**-0.5
    for start, length, kind in groups:
        rows = slice(start, start + length)
        query, key, value = (p_ref[i, rows, :] for i in range(3))
        d_out = d_ref[rows, :]
        d_query = d_key = d_value = None
        for index, part in enumerate((first, second)):
            q_part, d_part, k_part = query * part, d_out * part, key * part
            scores = dot_t(q_part, key) * scale
            soft = jnp.exp(scores - l_ref[rows, index * HEAD : index * HEAD + 1])
            mask = group_mask(kind, length, length)
            if mask is not None:
                soft = jnp.where(mask, soft, 0.0)
            d_soft = dot_t(d_part, value)
            row_dot = jnp.sum(soft * d_soft, -1, keepdims=True)
            d_scores = (soft * (d_soft - row_dot)).astype(BF)
            terms = (dot_n(d_scores, k_part), dot_l(d_scores, q_part), dot_l(soft.astype(BF), d_part))
            if index == 0:
                d_query, d_key, d_value = terms
            else:
                d_query, d_key, d_value = d_query + terms[0], d_key + terms[1], d_value + terms[2]
        o_ref[0, rows, :] = (d_query * scale).astype(BF)
        o_ref[1, rows, :] = (d_key * scale).astype(BF)
        o_ref[2, rows, :] = d_value.astype(BF)


def attend(projected, groups):
    _, rows, width = projected.shape
    return pl.pallas_call(
        partial(attend_kernel, groups),
        grid=(width // PAIR,),
        in_specs=[pl.BlockSpec((3, rows, PAIR), lambda h: (0, 0, h))],
        out_specs=[pl.BlockSpec((rows, PAIR), lambda h: (0, h))] * 2,
        out_shape=[
            jax.ShapeDtypeStruct((rows, width), BF),
            jax.ShapeDtypeStruct((rows, width), F32),
        ],
        cost_estimate=pl.CostEstimate(
            flops=4 * rows * 512 * width, bytes_accessed=12 * rows * width, transcendentals=rows * 256 * width // HEAD
        ),
        name="attend",
    )(projected)


def attend_back(projected, d_heads, logs, groups):
    _, rows, width = projected.shape
    return pl.pallas_call(
        partial(attend_back_kernel, groups),
        grid=(width // PAIR,),
        in_specs=[
            pl.BlockSpec((3, rows, PAIR), lambda h: (0, 0, h)),
            pl.BlockSpec((rows, PAIR), lambda h: (0, h)),
            pl.BlockSpec((rows, PAIR), lambda h: (0, h)),
        ],
        out_specs=pl.BlockSpec((3, rows, PAIR), lambda h: (0, 0, h)),
        out_shape=jax.ShapeDtypeStruct(projected.shape, BF),
        cost_estimate=pl.CostEstimate(
            flops=10 * rows * 512 * width, bytes_accessed=18 * rows * width, transcendentals=rows * 256 * width // HEAD
        ),
        name="attend_back",
    )(projected, d_heads, logs)


def frame_groups(first_frames, first_grid, second_frames, second_grid):
    groups = [(i * first_grid, first_grid, None) for i in range(first_frames)]
    base = first_frames * first_grid
    if second_frames % 2 == 0:
        groups += [
            (base + i * second_grid, 2 * second_grid, ("block", second_grid))
            for i in range(0, second_frames, 2)
        ]
    else:
        groups += [(base + i * second_grid, second_grid, None) for i in range(second_frames)]
    return tuple(groups)


def clip_groups(rows, frames):
    size = 128
    while rows % size:
        size //= 2
    return tuple((i, size, ("causal", frames)) for i in range(0, rows, size))


def swap(value, axis, size, step=1):
    return lax.ppermute(value, axis, [(i, i ^ step) for i in range(size)])


def flip(bit):
    return 1 - bit


def take(value, index, axis):
    return lax.dynamic_index_in_dim(value, index, axis, keepdims=False)


def fetch_other(weight, sizes, clip_bit, core_bit):
    rows = weight.shape[-2]
    quarter = rows // 4
    lead = (0,) * (weight.ndim - 2)

    def put(whole, piece, clip_at, core_at):
        return lax.dynamic_update_slice(whole, piece, (*lead, (2 * clip_at + core_at) * quarter, 0))

    mine = lax.dynamic_slice_in_dim(weight, (2 * clip_bit + core_bit) * quarter, quarter, weight.ndim - 2)
    from_x = swap(mine, "tp", sizes["tp"])
    from_y = swap(from_x, "clip", sizes["clip"])
    core_x = swap(from_x, "wide", sizes["wide"])
    core_y = swap(from_y, "wide", sizes["wide"])
    whole = jnp.zeros_like(weight)
    whole = put(whole, from_x, clip_bit, core_bit)
    whole = put(whole, from_y, flip(clip_bit), core_bit)
    whole = put(whole, core_x, clip_bit, flip(core_bit))
    return put(whole, core_y, flip(clip_bit), flip(core_bit))


def halves(value, index, axis):
    size = value.shape[axis] // 2
    return (
        lax.dynamic_slice_in_dim(value, index * size, size, axis),
        lax.dynamic_slice_in_dim(value, flip(index) * size, size, axis),
    )


def reduce_grad(left, own, other, sizes, bits, x_first):
    clip_bit, core_bit, z_index = bits
    n, depth = left.shape
    cuts = depth // sizes["wide"]
    stacks = sizes["wide"] // 2
    split = left.reshape(n, stacks, 2, cuts)
    keep_left = take(split, core_bit, 2).reshape(n, stacks * cuts)
    send_left = take(split, flip(core_bit), 2).reshape(n, stacks * cuts)

    def product(a, b):
        return jnp.einsum("nd,ntk->dtk", a, b, preferred_element_type=F32)

    own_keep, own_send = halves(own, clip_bit, 2)
    other_keep, other_send = halves(other, clip_bit, 2)

    def core_sum(b):
        return product(keep_left, b) + swap(product(send_left, b).astype(BF), "wide", sizes["wide"]).astype(F32)

    def x_swap(v):
        return swap(v.astype(BF), "tp", sizes["tp"]).astype(F32)

    def y_swap(v):
        return swap(v.astype(BF), "clip", sizes["clip"]).astype(F32)

    if x_first:
        keep = core_sum(own_keep) + x_swap(core_sum(other_keep))
        send = core_sum(own_send) + x_swap(core_sum(other_send))
        total = keep + y_swap(send)
    else:
        keep_own = core_sum(own_keep) + y_swap(core_sum(own_send))
        keep_other = core_sum(other_keep) + y_swap(core_sum(other_send))
        total = keep_own + x_swap(keep_other)
    for step in range(2, sizes["clip"].bit_length()):
        total = total + swap(total.astype(BF), "clip", sizes["clip"], 1 << (step - 1)).astype(F32)
    blocks = total.astype(BF).reshape((stacks, cuts) + total.shape[1:])
    result = take(total.reshape(blocks.shape), z_index, 0)
    for step in range(1, stacks):
        result = result + swap(take(blocks, z_index ^ step, 0), "wide", sizes["wide"], 2 * step).astype(F32)
    low = result.astype(BF)
    partner = swap(low, "clip", sizes["clip"])
    lower = jnp.where(clip_bit == 0, low, partner)
    upper = jnp.where(clip_bit == 0, partner, low)
    return jnp.concatenate([lower, upper], 2).astype(F32)


def reduce_small(rows, sizes, bits):
    clip_bit, core_bit, z_index = bits
    stacks = sizes["wide"] // 2
    count, depth = rows.shape
    blocks = rows.reshape(count, stacks, 2, depth // sizes["wide"]).transpose(1, 2, 0, 3)
    total = take(blocks, core_bit, 1) + swap(take(blocks, flip(core_bit), 1), "wide", sizes["wide"])
    total = total + swap(total, "tp", sizes["tp"])
    step = 1
    while step < sizes["clip"]:
        total = total + swap(total, "clip", sizes["clip"], step)
        step *= 2
    result = take(total, z_index, 0)
    for step in range(1, stacks):
        result = result + swap(take(total, z_index ^ step, 0), "wide", sizes["wide"], 2 * step)
    return result


def norm_stats(values):
    mean = jnp.mean(values, -1, keepdims=True)
    centered = values - mean
    spread = jnp.mean(centered * centered, -1, keepdims=True)
    return mean, lax.rsqrt(spread + 1e-05)


def norm_apply(values, gain, stats):
    return ((values - stats[0]) * stats[1] * gain).astype(BF)


def norm_back(values, gain, stats, d_normed):
    normal = (values - stats[0]) * stats[1]
    d_gain = jnp.sum(d_normed * normal, 0)
    scaled = d_normed * gain
    mean_first = jnp.mean(scaled, -1, keepdims=True)
    mean_second = jnp.mean(scaled * normal, -1, keepdims=True)
    return (scaled - mean_first - normal * mean_second) * stats[1], d_gain


def project(normed, weight):
    return jnp.einsum("nd,tde->tne", normed, weight, preferred_element_type=F32).astype(BF)


def mix(a, b):
    return jnp.dot(a, b, preferred_element_type=F32)


def gelu_parts(hidden):
    root = (2.0 / jnp.pi) ** 0.5
    square = hidden * hidden
    curve = jnp.tanh(root * (hidden + 0.044715 * square * hidden))
    slope = 0.5 * (1.0 + curve) + 0.5 * hidden * (1.0 - curve * curve) * root * (1.0 + 3 * 0.044715 * square)
    return 0.5 * hidden * (1.0 + curve), slope


def per_device(
    sizes,
    frames_a,
    frames_b,
    actions_a,
    actions_b,
    action_table,
    gain_space,
    space_qkv,
    space_out,
    gain_time,
    time_qkv,
    time_out,
    gain_ffn,
    ffn_up,
    ffn_down,
    cot_a,
    cot_b,
):
    n_wide = sizes["wide"]
    tp_index = lax.axis_index("tp")
    clip_bit = lax.axis_index("clip") % 2
    wide_index = lax.axis_index("wide")
    bits = (clip_bit, wide_index % 2, wide_index // 2)
    core_bit = bits[1]
    _, n_frames, grid_a, width = frames_a.shape
    grid_b = frames_b.shape[2]
    rows_a = n_frames * grid_a
    rows_b = n_frames * grid_b
    spots_a, spots_b = grid_a // n_wide, grid_b // n_wide
    spots = spots_a + spots_b
    all_frames = n_frames * n_wide
    rows = rows_a + rows_b

    def pick(value):
        return take(value, tp_index, 0)

    def to_grid(rows_in):
        first = rows_in[:rows_a].reshape(n_frames, n_wide, spots_a, width)
        second = rows_in[rows_a:].reshape(n_frames, n_wide, spots_b, width)
        packed = jnp.concatenate([first, second], 2).transpose(1, 0, 2, 3)
        moved = lax.all_to_all(packed, "wide", split_axis=0, concat_axis=0, tiled=True)
        return moved.reshape(all_frames, spots, width).transpose(1, 0, 2).reshape(rows, width)

    def to_frames(rows_in):
        packed = rows_in.reshape(spots, n_wide, n_frames, width).transpose(1, 2, 0, 3)
        moved = lax.all_to_all(packed, "wide", split_axis=0, concat_axis=0, tiled=True)
        first = moved[:, :, :spots_a].transpose(1, 0, 2, 3).reshape(rows_a, width)
        second = moved[:, :, spots_a:].transpose(1, 0, 2, 3).reshape(rows_b, width)
        return jnp.concatenate([first, second])

    def both_clips(rows_in):
        partner = swap(rows_in, "tp", sizes["tp"])
        pair = jnp.stack(
            [jnp.where(tp_index == 0, rows_in, partner), jnp.where(tp_index == 0, partner, rows_in)]
        )
        return (
            pair[:, :rows_a].reshape(2, n_frames, grid_a, width),
            pair[:, rows_a:].reshape(2, n_frames, grid_b, width),
        )

    other = {}
    names = ("space_qkv", "space_out", "time_qkv", "time_out", "ffn_up", "ffn_down")
    mine = dict(zip(names, (space_qkv, space_out, time_qkv, time_out, ffn_up, ffn_down)))
    for name in names:
        other[name] = fetch_other(mine[name], sizes, clip_bit, core_bit)

    space_groups = frame_groups(n_frames, grid_a, n_frames, grid_b)
    time_groups = clip_groups(rows, all_frames)

    cot = to_grid(jnp.concatenate([pick(cot_a).reshape(rows_a, width), pick(cot_b).reshape(rows_b, width)]))

    codes = lax.broadcasted_iota(jnp.int32, (1, action_table.shape[0]), 1)
    acts = jnp.concatenate([pick(actions_a), pick(actions_b)])
    one_hot = (acts[:, None] == codes).astype(F32)
    shifts = jnp.dot(one_hot, action_table.astype(F32), precision=lax.Precision.HIGHEST)
    started = jnp.concatenate(
        [
            (pick(frames_a).astype(F32) + shifts[:n_frames, None, :]).reshape(rows_a, width),
            (pick(frames_b).astype(F32) + shifts[n_frames:, None, :]).reshape(rows_b, width),
        ]
    )

    def branch(stream, gain, name, groups):
        stats = norm_stats(stream)
        normed = norm_apply(stream, gain, stats)
        kept = []
        total = stream
        for side in (mine, other):
            projected = project(normed, side[name + "_qkv"])
            heads, logs = attend(projected, groups)
            total = total + mix(heads, side[name + "_out"])
            kept.append((projected, heads, logs))
        return total.astype(BF), (stats, normed, kept)

    def branch_back(d_stream, stream, gain, name, groups, saved, x_first):
        stats, normed, kept = saved
        d_normed = 0.0
        d_projected = []
        for side, (projected, heads, logs) in zip((mine, other), kept):
            d_heads = dot_t(d_stream, side[name + "_out"]).astype(BF)
            piece = attend_back(projected, d_heads, logs, groups)
            d_projected.append(piece.transpose(1, 0, 2))
            d_normed = d_normed + jnp.einsum(
                "tne,tde->nd", piece, side[name + "_qkv"], preferred_element_type=F32
            )
        grad_out = reduce_grad(
            d_stream, kept[0][1][:, None, :], kept[1][1][:, None, :], sizes, bits, not x_first
        )
        grad_qkv = reduce_grad(normed, d_projected[0], d_projected[1], sizes, bits, x_first)
        d_values, d_gain = norm_back(stream, gain, stats, d_normed)
        return d_stream.astype(F32) + d_values, d_gain, grad_qkv.transpose(1, 0, 2), grad_out[:, 0, :].T

    middle, space_saved = branch(started, gain_space, "space", space_groups)
    middle = to_grid(middle).astype(F32)
    latest, time_saved = branch(middle, gain_time, "time", time_groups)
    latest = latest.astype(F32)
    ffn_stats = norm_stats(latest)
    normed_ffn = norm_apply(latest, gain_ffn, ffn_stats)
    total = latest
    d_normed_ffn = 0.0
    gelus, d_hiddens = [], []
    for side in (mine, other):
        hidden = mix(normed_ffn, side["ffn_up"])
        gelu, slope = gelu_parts(hidden)
        gelu = gelu.astype(BF)
        d_hidden = (dot_t(cot, side["ffn_down"]) * slope).astype(BF)
        d_normed_ffn = d_normed_ffn + dot_t(d_hidden, side["ffn_up"])
        total = total + mix(gelu, side["ffn_down"])
        gelus.append(gelu[:, None, :])
        d_hiddens.append(d_hidden[:, None, :])
    out_a, out_b = both_clips(to_frames(total.astype(BF)))
    grad_down = reduce_grad(cot, gelus[0], gelus[1], sizes, bits, False)
    grad_up = reduce_grad(normed_ffn, d_hiddens[0], d_hiddens[1], sizes, bits, True)
    d_values, d_gain_ffn = norm_back(latest, gain_ffn, ffn_stats, d_normed_ffn)
    d_latest = (cot.astype(F32) + d_values).astype(BF)
    d_middle, d_gain_time, grad_time_qkv, grad_time_out = branch_back(
        d_latest, middle, gain_time, "time", time_groups, time_saved, True
    )
    d_middle = to_frames(d_middle.astype(BF))
    d_started, d_gain_space, grad_space_qkv, grad_space_out = branch_back(
        d_middle, started, gain_space, "space", space_groups, space_saved, True
    )
    d_frames_a, d_frames_b = both_clips(d_started.astype(BF))
    frame_sums = jnp.concatenate(
        [
            jnp.sum(d_started[:rows_a].reshape(n_frames, grid_a, width), 1),
            jnp.sum(d_started[rows_a:].reshape(n_frames, grid_b, width), 1),
        ]
    )
    d_table = jnp.einsum("fa,fd->ad", one_hot, frame_sums, precision=lax.Precision.HIGHEST)
    small = reduce_small(
        jnp.concatenate([d_table, d_gain_space[None], d_gain_time[None], d_gain_ffn[None]]), sizes, bits
    )
    n_codes = action_table.shape[0]
    return (
        out_a,
        out_b,
        d_frames_a,
        d_frames_b,
        small[:n_codes],
        small[n_codes],
        grad_space_qkv,
        grad_space_out,
        small[n_codes + 1],
        grad_time_qkv,
        grad_time_out,
        small[n_codes + 2],
        grad_up[:, 0, :],
        grad_down[:, 0, :].T,
    )


def solution(mesh):
    sizes = dict(mesh.shape)
    return jax.shard_map(
        partial(per_device, sizes),
        mesh=mesh,
        in_specs=(
            P("clip", "wide", None, None),
            P("clip", "wide", None, None),
            P("clip", "wide"),
            P("clip", "wide"),
            P(),
            P(),
            P(None, None, "tp"),
            P("tp", None),
            P(),
            P(None, None, "tp"),
            P("tp", None),
            P(),
            P(None, "tp"),
            P("tp", None),
            P("clip", "wide", None, None),
            P("clip", "wide", None, None),
        ),
        out_specs=(
            P("clip", "wide", None, None),
            P("clip", "wide", None, None),
            P("clip", "wide", None, None),
            P("clip", "wide", None, None),
            P(None, "wide"),
            P("wide"),
            P(None, "wide", "tp"),
            P("tp", "wide"),
            P("wide"),
            P(None, "wide", "tp"),
            P("tp", "wide"),
            P("wide"),
            P("wide", "tp"),
            P("tp", "wide"),
        ),
        check_vma=False,
    )
```

```python
from functools import partial

import jax
import jax.numpy as jnp
from jax import lax
from jax.experimental import pallas as pl
from jax.experimental.pallas import tpu as pltpu
from jax.sharding import PartitionSpec as P

HEAD = 64
PAIR = 2 * HEAD
BLOCK = 2 * PAIR
BF = jnp.bfloat16
F32 = jnp.float32
LIMIT = 60 * 2**20


def dot_n(a, b):
    return lax.dot_general(a, b, (((1,), (0,)), ((), ())), preferred_element_type=F32)


def dot_t(a, b):
    return lax.dot_general(a, b, (((1,), (1,)), ((), ())), preferred_element_type=F32)


def shape_of(*dims, dtype=BF):
    return jax.ShapeDtypeStruct(dims, dtype)


def whole(*dims):
    return pl.BlockSpec(dims, lambda *_: (0,) * len(dims))


def any_spec():
    return pl.BlockSpec(memory_space=pl.ANY)


def params():
    return pltpu.CompilerParams(vmem_limit_bytes=LIMIT)


def cost(micros):
    return pl.CostEstimate(flops=int(micros * 4e9), bytes_accessed=2**20, transcendentals=0)


def group_mask(kind, length):
    if kind is None:
        return None
    name, size, inner = kind
    key = lax.broadcasted_iota(jnp.int32, (length, length), 0)
    query = lax.broadcasted_iota(jnp.int32, (length, length), 1)
    if name == "block":
        shift = size.bit_length() - 1
        return (query >> shift) == (key >> shift)
    shift = inner.bit_length() - 1
    return ((query & (inner - 1)) == (key & (inner - 1))) & ((key >> shift) <= (query >> shift))


def head_masks(value):
    lane = lax.broadcasted_iota(jnp.int32, (1, PAIR), 1)
    return (
        jnp.where(lane < HEAD, value, 0.0).astype(BF),
        jnp.where(lane < HEAD, 0.0, value).astype(BF),
    )


def attend_block(groups, proj_ref, heads_ref, logs_ref):
    scaled = head_masks(HEAD**-0.5)
    masks = {kind: group_mask(kind, length) for _, length, kind in groups}
    for pair in range(2):
        cols = slice(pair * PAIR, (pair + 1) * PAIR)
        for start, length, kind in groups:
            rows = slice(start, start + length)
            query, key, value = (proj_ref[i, rows, cols] for i in range(3))
            value_t = value.T
            outs = []
            for h in range(2):
                scores = dot_t(key * scaled[h], query)
                if kind is not None:
                    scores = jnp.where(masks[kind], scores, -1e30)
                largest = jnp.max(scores, 0, keepdims=True)
                shifted = jnp.exp(scores - largest)
                total = jnp.sum(shifted, 0, keepdims=True)
                out = dot_n(value_t[h * HEAD : (h + 1) * HEAD], shifted.astype(BF))
                outs.append(out * (1.0 / total))
                if logs_ref is not None:
                    logs_ref[2 * pair + h : 2 * pair + h + 1, rows] = largest + jnp.log(total)
            heads_ref[rows, cols] = jnp.concatenate(outs, 0).T.astype(BF)


def attend_back_block(groups, proj_ref, d_ref, logs_ref, o_ref):
    scale = HEAD**-0.5
    scaled = head_masks(scale)
    parts = head_masks(1.0)
    masks = {kind: group_mask(kind, length) for _, length, kind in groups}
    for pair in range(2):
        cols = slice(pair * PAIR, (pair + 1) * PAIR)
        for start, length, kind in groups:
            rows = slice(start, start + length)
            query, key, value = (proj_ref[i, rows, cols] for i in range(3))
            d_out = d_ref[rows, cols]
            key_t = key.T
            d_key = d_value = None
            d_query = []
            for h in range(2):
                soft = jnp.exp(
                    dot_t(key * scaled[h], query) - logs_ref[2 * pair + h : 2 * pair + h + 1, rows]
                )
                if kind is not None:
                    soft = jnp.where(masks[kind], soft, 0.0)
                d_soft = dot_t(value * parts[h], d_out)
                row_dot = jnp.sum(soft * d_soft, 0, keepdims=True)
                d_scores = (soft * (d_soft - row_dot)).astype(BF)
                key_term = dot_n(d_scores, query * parts[h])
                value_term = dot_n(soft.astype(BF), d_out * parts[h])
                d_key = key_term if h == 0 else d_key + key_term
                d_value = value_term if h == 0 else d_value + value_term
                d_query.append(dot_n(key_t[h * HEAD : (h + 1) * HEAD], d_scores))
            o_ref[0, rows, cols] = (jnp.concatenate(d_query, 0).T * scale).astype(BF)
            o_ref[1, rows, cols] = (d_key * scale).astype(BF)
            o_ref[2, rows, cols] = d_value.astype(BF)


def row_chunks(rows, size=64):
    return [slice(i, i + size) for i in range(0, rows, size)]


def norm_parts(values):
    centered = values - jnp.mean(values, -1, keepdims=True)
    inverse = lax.rsqrt(jnp.mean(centered * centered, -1, keepdims=True) + 1e-05)
    return centered * inverse, inverse


def project_block(normed_ref, weight, proj_ref):
    for i in range(3):
        proj_ref[i] = dot_n(normed_ref[...], weight(i)).astype(BF)


def space_kernel(groups, full, _, fa_ref, fb_ref, shift_ref, gain_ref, w_ref, *refs):
    if full:
        heads_ref, proj_ref, logs_ref, started_ref, normed_ref = refs
        proj, logs = proj_ref.at[0], logs_ref.at[0]
    else:
        heads_ref, proj, normed_ref = refs
        logs = None
    _, frames, grid_a, _ = fa_ref.shape
    grid_b = fb_ref.shape[2]

    @pl.when(pl.program_id(0) == 0)
    def _():
        gain = gain_ref[...]
        base = 0
        for frame_ref, grid, first in ((fa_ref, grid_a, 0), (fb_ref, grid_b, frames)):
            for f in range(frames):
                move = shift_ref[0, first + f : first + f + 1, :]
                for rows in row_chunks(grid):
                    values = frame_ref[0, f, rows, :].astype(F32) + move
                    out = slice(base + rows.start, base + rows.stop)
                    if full:
                        started_ref[out, :] = values
                    normed_ref[out, :] = (norm_parts(values)[0] * gain).astype(BF)
                base += grid

    project_block(normed_ref, lambda i: w_ref[i], proj)
    attend_block(groups, proj, heads_ref.at[0], logs)


def space_heads(clip, frames_a, frames_b, shifts, gain, qkv, groups, full):
    _, frames, grid_a, depth = frames_a.shape
    grid_b = frames_b.shape[2]
    rows = frames * (grid_a + grid_b)
    blocks = qkv.shape[2] // BLOCK

    def chosen(*dims):
        return pl.BlockSpec((1, *dims), lambda s, c: (c[0],) + (0,) * len(dims))

    heads = (pl.BlockSpec((1, rows, BLOCK), lambda s, c: (s, 0, 0)), shape_of(blocks, rows, BLOCK))
    if full:
        outs = [
            heads,
            (pl.BlockSpec((1, 3, rows, BLOCK), lambda s, c: (s, 0, 0, 0)), shape_of(blocks, 3, rows, BLOCK)),
            (pl.BlockSpec((1, 8, rows), lambda s, c: (s, 0, 0)), shape_of(blocks, 8, rows, dtype=F32)),
            (whole(rows, depth), shape_of(rows, depth, dtype=F32)),
            (whole(rows, depth), shape_of(rows, depth)),
        ]
        scratch = []
    else:
        outs = [heads]
        scratch = [pltpu.VMEM((3, rows, BLOCK), BF), pltpu.VMEM((rows, depth), BF)]
    return pl.pallas_call(
        partial(space_kernel, groups, full),
        grid_spec=pltpu.PrefetchScalarGridSpec(
            num_scalar_prefetch=1,
            grid=(blocks,),
            in_specs=[
                chosen(frames, grid_a, depth),
                chosen(frames, grid_b, depth),
                chosen(2 * frames, depth),
                whole(1, depth),
                pl.BlockSpec((3, depth, BLOCK), lambda s, c: (0, 0, s)),
            ],
            out_specs=[o[0] for o in outs],
            scratch_shapes=scratch,
        ),
        out_shape=[o[1] for o in outs],
        compiler_params=params(),
        cost_estimate=cost(12),
        name="space_own" if full else "space_partner",
    )(clip, frames_a, frames_b, shifts, gain, qkv)


def stream_weights(own_qkv, own_out, qkv_slots, out_slots, wq, wo, sems, step, steps, first=0):
    def start(index, slot):
        for s in range(steps):

            @pl.when(index == s)
            def _(s=s):
                if s + first < 2:
                    cols = pl.ds((s + first) * BLOCK, BLOCK)
                    pltpu.make_async_copy(own_qkv.at[:, :, cols], wq.at[slot], sems.at[slot, 0]).start()
                    if wo is not None:
                        pltpu.make_async_copy(own_out.at[cols, :], wo.at[slot], sems.at[slot, 1]).start()
                else:
                    for i in range(2):
                        part = 2 * (s + first - 2) + i
                        cols = pl.ds(i * PAIR, PAIR)
                        pltpu.make_async_copy(
                            qkv_slots[part].at[0:3], wq.at[slot, :, :, cols], sems.at[slot, 0]
                        ).start()
                        if wo is None:
                            continue
                        if out_slots is not None:
                            pltpu.make_async_copy(
                                out_slots[part], wo.at[slot, cols, :], sems.at[slot, 1]
                            ).start()
                            continue
                        for j in range(wo.shape[2] // PAIR):
                            place = pl.ds(j * PAIR, PAIR)
                            pltpu.make_async_copy(
                                qkv_slots[part].at[3, place, :], wo.at[slot, cols, place], sems.at[slot, 1]
                            ).start()

    slot = step % 2

    @pl.when(step == 0)
    def _():
        start(step, slot)

    @pl.when(step + 1 < steps)
    def _():
        start(step + 1, 1 - slot)

    pltpu.make_async_copy(wq.at[slot], wq.at[slot], sems.at[slot, 0]).wait()
    if wo is not None:
        pltpu.make_async_copy(wo.at[slot], wo.at[slot], sems.at[slot, 1]).wait()
    return slot


def rest_kernel(groups, normed_ref, q0, q1, q2, q3, heads_ref, proj_ref, logs_ref, wq, sems):
    slot = stream_weights(None, None, (q0, q1, q2, q3), None, wq, None, sems, pl.program_id(0), 2, 2)
    project_block(normed_ref, lambda i: wq[slot, i], proj_ref.at[0])
    attend_block(groups, proj_ref.at[0], heads_ref.at[0], logs_ref.at[0])


def space_rest(normed, qkv_slots, groups):
    rows, depth = normed.shape
    return pl.pallas_call(
        partial(rest_kernel, groups),
        grid=(2,),
        in_specs=[whole(rows, depth)] + [any_spec()] * 4,
        out_specs=[
            pl.BlockSpec((1, rows, BLOCK), lambda s: (s, 0, 0)),
            pl.BlockSpec((1, 3, rows, BLOCK), lambda s: (s, 0, 0, 0)),
            pl.BlockSpec((1, 8, rows), lambda s: (s, 0, 0)),
        ],
        out_shape=[
            shape_of(2, rows, BLOCK),
            shape_of(2, 3, rows, BLOCK),
            shape_of(2, 8, rows, dtype=F32),
        ],
        scratch_shapes=[pltpu.VMEM((2, 3, depth, BLOCK), BF), pltpu.SemaphoreType.DMA((2, 2))],
        compiler_params=params(),
        cost_estimate=cost(12),
        name="space_rest",
    )(normed, *qkv_slots)


def out_kernel(bits_ref, stream_ref, own_ref, other_ref, w_ref, o0, o1, o2, o3, mid_ref, assembled):
    clip_bit, core_bit = bits_ref[0], bits_ref[1]
    for i, piece in enumerate((o0, o1, o2, o3)):
        place = 2 * (clip_bit if i < 2 else 1 - clip_bit) + (core_bit if i % 2 == 0 else 1 - core_bit)
        assembled[pl.ds(pl.multiple_of(place * PAIR, PAIR), PAIR), :] = piece[...]
    total = stream_ref[...]
    for b in range(own_ref.shape[0]):
        cols = slice(b * BLOCK, (b + 1) * BLOCK)
        total = total + dot_n(own_ref[b], w_ref[cols, :]) + dot_n(other_ref[b], assembled[cols, :])
    mid_ref[...] = total.astype(BF)


def space_mix(bits, started, own, other, weight, out_slots):
    rows, depth = started.shape
    half = weight.shape[0]
    return pl.pallas_call(
        out_kernel,
        grid_spec=pltpu.PrefetchScalarGridSpec(
            num_scalar_prefetch=1,
            grid=(1,),
            in_specs=[whole(rows, depth), whole(*own.shape), whole(*other.shape), whole(half, depth)]
            + [whole(half // 4, depth)] * 4,
            out_specs=whole(rows, depth),
            scratch_shapes=[pltpu.VMEM((half, depth), BF)],
        ),
        out_shape=shape_of(rows, depth),
        compiler_params=params(),
        cost_estimate=cost(6),
        name="space_mix",
    )(bits, started, own, other, weight, *out_slots)


def time_kernel(groups, mid_ref, gain_ref, wq_any, wo_any, q0, q1, q2, q3,
                late_ref, normed_ref, heads_ref, proj_ref, logs_ref, acc, wq, wo, sems):
    step = pl.program_id(0)
    rows = mid_ref.shape[0]

    @pl.when(step == 0)
    def _():
        gain = gain_ref[...]
        for chunk in row_chunks(rows):
            values = mid_ref[chunk, :].astype(F32)
            acc[chunk, :] = values
            normed_ref[chunk, :] = (norm_parts(values)[0] * gain).astype(BF)

    slot = stream_weights(wq_any, wo_any, (q0, q1, q2, q3), None, wq, wo, sems, step, 4)
    project_block(normed_ref, lambda i: wq[slot, i], proj_ref.at[0])
    attend_block(groups, proj_ref.at[0], heads_ref.at[0], logs_ref.at[0])
    acc[...] += dot_n(heads_ref[0], wo[slot])

    @pl.when(step == 3)
    def _():
        late_ref[...] = acc[...].astype(BF)


def time_forward(middle, gain, qkv, out, slots, groups):
    rows, depth = middle.shape
    return pl.pallas_call(
        partial(time_kernel, groups),
        grid=(4,),
        in_specs=[whole(rows, depth), whole(1, depth)] + [any_spec()] * 6,
        out_specs=[
            whole(rows, depth),
            whole(rows, depth),
            pl.BlockSpec((1, rows, BLOCK), lambda s: (s, 0, 0)),
            pl.BlockSpec((1, 3, rows, BLOCK), lambda s: (s, 0, 0, 0)),
            pl.BlockSpec((1, 8, rows), lambda s: (s, 0, 0)),
        ],
        out_shape=[
            shape_of(rows, depth),
            shape_of(rows, depth),
            shape_of(4, rows, BLOCK),
            shape_of(4, 3, rows, BLOCK),
            shape_of(4, 8, rows, dtype=F32),
        ],
        scratch_shapes=[
            pltpu.VMEM((rows, depth), F32),
            pltpu.VMEM((2, 3, depth, BLOCK), BF),
            pltpu.VMEM((2, BLOCK, depth), BF),
            pltpu.SemaphoreType.DMA((2, 2)),
        ],
        compiler_params=params(),
        cost_estimate=cost(29),
        name="time_forward",
    )(middle, gain, qkv, out, *slots)


def gelu_parts(hidden):
    root = 0.7978845608028654
    square = hidden * hidden
    curve = jnp.tanh(hidden * (root + (root * 0.044715) * square))
    half = 0.5 + 0.5 * curve
    slope = half + hidden * (half * (1.0 - curve)) * (root + (3 * 0.044715 * root) * square)
    return hidden * half, slope


def norm_back_rows(values, gain, d_normed):
    normal, inverse = norm_parts(values)
    scaled = d_normed * gain
    mean_first = jnp.mean(scaled, -1, keepdims=True)
    mean_second = jnp.mean(scaled * normal, -1, keepdims=True)
    return (scaled - mean_first - normal * mean_second) * inverse, d_normed * normal


def ffn_kernel(late_ref, cot_ref, gain_ref, up_any, down_any, u0, u1, u2, u3, d0, d1, d2, d3,
               out_ref, d_late_ref, normed_ref, gelu_ref, d_hidden_ref, d_gain_ref, total, d_normed, wu, wd, sems):
    step = pl.program_id(0)
    rows, depth = late_ref.shape
    width = wu.shape[2]
    steps = 8

    @pl.when(step == 0)
    def _():
        gain = gain_ref[...]
        for chunk in row_chunks(rows):
            values = late_ref[chunk, :].astype(F32)
            total[chunk, :] = values
            d_normed[chunk, :] = jnp.zeros_like(values)
            normed_ref[chunk, :] = (norm_parts(values)[0] * gain).astype(BF)

    def start(index, slot):
        for s in range(steps):

            @pl.when(index == s)
            def _(s=s):
                cols = pl.ds(s * width, width)
                up = up_any.at[:, cols] if s < 4 else (u0, u1, u2, u3)[s - 4]
                down = down_any.at[cols, :] if s < 4 else (d0, d1, d2, d3)[s - 4]
                pltpu.make_async_copy(up, wu.at[slot], sems.at[slot, 0]).start()
                pltpu.make_async_copy(down, wd.at[slot], sems.at[slot, 1]).start()

    slot = step % 2

    @pl.when(step == 0)
    def _():
        start(step, slot)

    @pl.when(step + 1 < steps)
    def _():
        start(step + 1, 1 - slot)

    pltpu.make_async_copy(wu.at[slot], wu.at[slot], sems.at[slot, 0]).wait()
    pltpu.make_async_copy(wd.at[slot], wd.at[slot], sems.at[slot, 1]).wait()
    for chunk in row_chunks(rows, rows // 2):
        gelu, slope = gelu_parts(dot_n(normed_ref[chunk, :], wu[slot]))
        gelu = gelu.astype(BF)
        gelu_ref[0, 0, chunk, :] = gelu
        d_hidden = (dot_t(cot_ref[chunk, :], wd[slot]) * slope).astype(BF)
        d_hidden_ref[0, 0, chunk, :] = d_hidden
        total[chunk, :] += dot_n(gelu, wd[slot])
        d_normed[chunk, :] += dot_t(d_hidden, wu[slot])

    @pl.when(step == steps - 1)
    def _():
        gain = gain_ref[...]
        d_gain = jnp.zeros_like(gain)
        for chunk in row_chunks(rows):
            out_ref[chunk, :] = total[chunk, :].astype(BF)
            back, d_gain_rows = norm_back_rows(late_ref[chunk, :].astype(F32), gain, d_normed[chunk, :])
            d_late_ref[chunk, :] = (cot_ref[chunk, :].astype(F32) + back).astype(BF)
            d_gain = d_gain + jnp.sum(d_gain_rows, 0, keepdims=True)
        d_gain_ref[...] = d_gain


def feed_forward(latest, cot, gain, up, down, up_slots, down_slots):
    rows, depth = latest.shape
    width = up.shape[1] // 4
    stream = pl.BlockSpec((1, 1, rows, width), lambda s: (s, 0, 0, 0))
    return pl.pallas_call(
        ffn_kernel,
        grid=(8,),
        in_specs=[whole(rows, depth), whole(rows, depth), whole(1, depth)] + [any_spec()] * 10,
        out_specs=[whole(rows, depth), whole(rows, depth), whole(rows, depth), stream, stream, whole(1, depth)],
        out_shape=[
            shape_of(rows, depth),
            shape_of(rows, depth),
            shape_of(rows, depth),
            shape_of(8, 1, rows, width),
            shape_of(8, 1, rows, width),
            shape_of(1, depth, dtype=F32),
        ],
        scratch_shapes=[
            pltpu.VMEM((rows, depth), F32),
            pltpu.VMEM((rows, depth), F32),
            pltpu.VMEM((2, depth, width), BF),
            pltpu.VMEM((2, width, depth), BF),
            pltpu.SemaphoreType.DMA((2, 2)),
        ],
        compiler_params=params(),
        cost_estimate=cost(34),
        name="feed_forward",
    )(latest, cot, gain, up, down, *up_slots, *down_slots)


def back_kernel(groups, segments, sums, final, packed, offset, dy_ref, proj_any, logs_any, *refs):
    if final:
        stream_ref, gain_ref, partial_ref, q0, q1, q2, q3 = refs[:7]
        refs = refs[7:]
        out_slots = None
        if not packed:
            out_slots, refs = refs[:4], refs[4:]
        own, slots = (None, None), ((q0, q1, q2, q3), out_slots)
        d_stream_ref, d_proj_ref, d_gain_ref, sums_ref, d_normed = refs[:5]
        first = 2
    else:
        own, slots = refs[:2], (None, None)
        d_normed, d_proj_ref = refs[2:4]
        first = 0
    d_heads, proj, logs, wq, wo, sems, more = refs[-7:]
    step = pl.program_id(0)

    def start(index, slot):
        pltpu.make_async_copy(proj_any.at[index + offset], proj.at[slot], more.at[slot, 0]).start()
        pltpu.make_async_copy(logs_any.at[index + offset], logs.at[slot], more.at[slot, 1]).start()

    slot = step % 2

    @pl.when(step == 0)
    def _():
        start(step, slot)
        start(step + 1, 1 - slot)

    slot = stream_weights(*own, *slots, wq, wo, sems, step, 2, first)
    d_heads[...] = dot_t(dy_ref[...], wo[slot]).astype(BF)
    pltpu.make_async_copy(proj.at[slot], proj.at[slot], more.at[slot, 0]).wait()
    pltpu.make_async_copy(logs.at[slot], logs.at[slot], more.at[slot, 1]).wait()
    attend_back_block(groups, proj.at[slot], d_heads, logs.at[slot], d_proj_ref.at[0])
    term = (
        dot_t(d_proj_ref[0, 0], wq[slot, 0])
        + dot_t(d_proj_ref[0, 1], wq[slot, 1])
        + dot_t(d_proj_ref[0, 2], wq[slot, 2])
    )

    @pl.when(step == 0)
    def _():
        d_normed[...] = term + partial_ref[...] if final else term

    @pl.when(step > 0)
    def _():
        d_normed[...] += term

    if not final:
        return

    @pl.when(step == 1)
    def _():
        gain = gain_ref[...]
        d_gain = jnp.zeros_like(gain)
        for index, (begin, count) in enumerate(segments):
            summed = jnp.zeros_like(gain)
            for piece in row_chunks(count):
                chunk = slice(begin + piece.start, begin + piece.stop)
                back, d_gain_rows = norm_back_rows(stream_ref[chunk, :].astype(F32), gain, d_normed[chunk, :])
                d_values = dy_ref[chunk, :].astype(F32) + back
                d_stream_ref[chunk, :] = d_values.astype(BF)
                d_gain = d_gain + jnp.sum(d_gain_rows, 0, keepdims=True)
                if sums:
                    summed = summed + jnp.sum(d_values, 0, keepdims=True)
            if sums:
                sums_ref[index : index + 1, :] = summed
        d_gain_ref[...] = d_gain
        if not sums:
            sums_ref[...] = jnp.zeros_like(sums_ref)


def branch_back(name, dy, proj, logs, offset, weights, groups, tail=None, segments=(), sums=False):
    rows, depth = dy.shape
    final = tail is not None
    if final:
        slots = [piece for group in weights for piece in group]
        others = [*tail, *slots]
        specs = [whole(rows, depth), whole(1, depth), whole(rows, depth)] + [any_spec()] * len(slots)
        outs = [
            (whole(rows, depth), shape_of(rows, depth)),
            (pl.BlockSpec((1, 3, rows, BLOCK), lambda s: (s, 0, 0, 0)), shape_of(2, 3, rows, BLOCK)),
            (whole(1, depth), shape_of(1, depth, dtype=F32)),
            (whole(8, depth), shape_of(8, depth, dtype=F32)),
        ]
        scratch = [pltpu.VMEM((rows, depth), F32)]
    else:
        others = list(weights)
        specs = [any_spec()] * 2
        outs = [
            (whole(rows, depth), shape_of(rows, depth, dtype=F32)),
            (pl.BlockSpec((1, 3, rows, BLOCK), lambda s: (s, 0, 0, 0)), shape_of(2, 3, rows, BLOCK)),
        ]
        scratch = []
    return pl.pallas_call(
        partial(back_kernel, groups, segments, sums, final, len(weights) == 1, offset),
        grid=(2,),
        in_specs=[whole(rows, depth), any_spec(), any_spec()] + specs,
        out_specs=[o[0] for o in outs],
        out_shape=[o[1] for o in outs],
        scratch_shapes=scratch
        + [
            pltpu.VMEM((rows, BLOCK), BF),
            pltpu.VMEM((2, 3, rows, BLOCK), BF),
            pltpu.VMEM((2, 8, rows), F32),
            pltpu.VMEM((2, 3, depth, BLOCK), BF),
            pltpu.VMEM((2, BLOCK, depth), BF),
            pltpu.SemaphoreType.DMA((2, 2)),
            pltpu.SemaphoreType.DMA((2, 2)),
        ],
        compiler_params=params(),
        cost_estimate=cost(21 if final else 18),
        name=name,
    )(dy, proj, logs, *others)


def grad_kernel(chunk, y_first, lefts, bits_ref, *refs):
    count = len(lefts)
    n_left = max(lefts) + 1
    left_refs, own_refs, other_refs = refs[:n_left], refs[n_left : n_left + count], refs[n_left + count : n_left + 2 * count]
    send_ref, keep_ref, turned = refs[n_left + 2 * count :]
    step = pl.program_id(0)
    core_bit, z_index = bits_ref[1], bits_ref[2]
    stacks = send_ref.shape[2]
    cut = send_ref.shape[3]

    @pl.when(step == 0)
    def _():
        for n, left_ref in enumerate(left_refs):
            for j in range(stacks):
                start = pl.multiple_of((z_index ^ j) * 2 * cut, 2 * cut)
                both = left_ref[:, pl.ds(start, 2 * cut)].T
                rows = slice(j * cut, (j + 1) * cut)
                for core in range(2):

                    @pl.when(core_bit == core)
                    def _(core=core, both=both, rows=rows, n=n):
                        turned[n, 1, rows, :] = both[core * cut : (core + 1) * cut]
                        turned[n, 0, rows, :] = both[(1 - core) * cut : (2 - core) * cut]

    def fill(side, half, out_ref):
        matrix = 0
        for n, own_ref, other_ref in zip(lefts, own_refs, other_refs):
            source = own_ref if half == 0 else other_ref
            span = source.shape[3]
            for t in range(source.shape[1]):
                for b in range(source.shape[0]):
                    block = dot_n(turned[n, side], source[b, t]).astype(BF)
                    for i in range(span // chunk):
                        index = b * (span // chunk) + i
                        if half == 1:
                            index = index ^ core_bit
                        lanes = pl.ds(pl.multiple_of((2 * matrix + index) * chunk, chunk), chunk)
                        for j in range(stacks):
                            out_ref[0, 0, j, :, lanes] = block[
                                j * cut : (j + 1) * cut, i * chunk : (i + 1) * chunk
                            ]
                matrix += 1

    for g in range(8):

        @pl.when(step == g)
        def _(g=g):
            first, second = g // 2 % 2, g % 2
            fill(g // 4, second if y_first else first, send_ref if g < 4 else keep_ref)


def grad_product(bits, left_arrays, terms, chunk, y_first, sizes, micros):
    rows, depth = left_arrays[0].shape
    stacks = sizes["wide"] // 2
    cut = depth // sizes["wide"]
    columns = 2 * sum(term[4] for term in terms) * chunk

    def y_flip(g):
        return g % 4 // 2 if y_first else g % 2

    def own_index(g, b):
        flip = y_flip(g)
        if not y_first:
            flip = jnp.where(g % 4 // 2 == 0, flip, 1)
        return b[0] ^ flip

    def other_index(g, b):
        flip = y_flip(g)
        if not y_first:
            flip = jnp.where(g % 4 // 2 == 1, flip, 0)
        return flip

    def half_spec(value, index, first_part, parts):
        array, at = value
        lead = 2 * chunk // array.shape[3]
        return pl.BlockSpec(
            (lead, parts, *array.shape[2:]),
            lambda g, b: (2 * at + index(g, b), first_part // parts, 0, 0),
        )

    block = (1, 1, stacks, cut, columns)
    return pl.pallas_call(
        partial(grad_kernel, chunk, y_first, [term[0] for term in terms]),
        grid_spec=pltpu.PrefetchScalarGridSpec(
            num_scalar_prefetch=1,
            grid=(8,),
            in_specs=[whole(rows, depth)] * len(left_arrays)
            + [half_spec(term[1], own_index, *term[3:]) for term in terms]
            + [half_spec(term[2], other_index, *term[3:]) for term in terms],
            out_specs=[
                pl.BlockSpec(block, lambda g, b: (jnp.minimum(g, 3) // 2, jnp.minimum(g, 3) % 2, 0, 0, 0)),
                pl.BlockSpec(
                    block, lambda g, b: (jnp.maximum(g - 4, 0) // 2, jnp.maximum(g - 4, 0) % 2, 0, 0, 0)
                ),
            ],
            scratch_shapes=[pltpu.VMEM((len(left_arrays), 2, stacks * cut, rows), BF)],
        ),
        out_shape=[shape_of(2, 2, stacks, cut, columns)] * 2,
        compiler_params=params(),
        cost_estimate=cost(micros),
        name="grad_product",
    )(bits, *left_arrays, *[term[1][0] for term in terms], *[term[2][0] for term in terms])


def swap(value, axis, sizes, step=1):
    return lax.ppermute(value, axis, [(i, i ^ step) for i in range(sizes[axis])])


def after(value, *others):
    return lax.optimization_barrier((value, *others))[0]


def wide(value):
    return value.astype(F32)


class Moves:
    def __init__(self, sizes):
        self.sizes = sizes
        self.tp = lax.axis_index("tp")
        self.clip = lax.axis_index("clip")
        self.clip_bit = self.clip % 2
        place = lax.axis_index("wide")
        self.core_bit = place % 2
        self.z = place // 2
        self.bits = jnp.stack([self.clip_bit, self.core_bit, self.z]).astype(jnp.int32)

    def quarter(self, weight, axis):
        size = weight.shape[axis] // 4
        return lax.dynamic_slice_in_dim(weight, (2 * self.clip_bit + self.core_bit) * size, size, axis)

    def spread(self, from_x):
        from_y = swap(from_x, "clip", self.sizes)
        return (from_x, swap(from_x, "wide", self.sizes), from_y, swap(from_y, "wide", self.sizes))

    def spread_core(self, from_x, from_y):
        return (from_x, swap(from_x, "wide", self.sizes), from_y, swap(from_y, "wide", self.sizes))

    def reduction(self, product, y_first):
        return Reduction(self, *product, y_first)

    def take(self, value, index, axis):
        return lax.dynamic_index_in_dim(value, index, axis, keepdims=False)

    def small_first(self, rows):
        count, depth = rows.shape
        wide_size = self.sizes["wide"]
        blocks = rows.reshape(count, wide_size // 2, 2, depth // wide_size).transpose(1, 2, 0, 3)
        other = swap(self.take(blocks, 1 - self.core_bit, 1), "wide", self.sizes)
        return self.take(blocks, self.core_bit, 1), other

    def small_last(self, total):
        result = self.take(total, self.z, 0)
        for j in range(1, self.sizes["wide"] // 2):
            result = result + swap(self.take(total, self.z ^ j, 0), "wide", self.sizes, 2 * j)
        return result


class Reduction:
    def __init__(self, moves, send, keep, y_first):
        self.moves, self.sizes, self.keep = moves, moves.sizes, keep
        self.axes = ("clip", "tp") if y_first else ("tp", "clip")
        self.got = swap(send, "wide", self.sizes)

    def second(self, *deps):
        self.leaving = (wide(self.keep[1]) + wide(self.got[1])).astype(BF)
        if deps:
            self.leaving = after(self.leaving, *deps)
        self.arrived = swap(self.leaving, self.axes[0], self.sizes)
        return self.leaving

    def third(self, *deps):
        total = wide(self.keep[0]) + wide(self.got[0]) + wide(self.arrived)
        self.leaving = total[1].astype(BF)
        if deps:
            self.leaving = after(self.leaving, *deps)
        self.mine = total[0].astype(BF)
        self.arrived = swap(self.leaving, self.axes[1], self.sizes)
        return self.leaving

    def sum(self, *deps):
        if deps:
            self.mine = after(self.mine, *deps)
        total = wide(self.mine) + wide(self.arrived)
        step = 2
        while step < self.sizes["clip"]:
            total = total + wide(swap(total.astype(BF), "clip", self.sizes, step))
            step *= 2
        self.total = total.astype(BF)
        return self.total


class Pair:
    def __init__(self, moves, one, two):
        self.moves, self.sizes, self.one, self.two = moves, moves.sizes, one, two

    def fourth(self, *deps):
        one, two = self.one.total, self.two.total
        if deps:
            one = after(one, *deps)
        low = jnp.stack([one, two], 1)
        self.mine = low[0]
        self.pieces = [swap(low[j], "wide", self.sizes, 2 * j) for j in range(1, low.shape[0])]
        return low

    def fifth(self, *deps):
        result = wide(after(self.mine, *deps) if deps else self.mine)
        for piece in self.pieces:
            result = result + wide(piece)
        self.mine = result.astype(BF)
        self.arrived = swap(self.mine, "clip", self.sizes)
        return self.mine

    def halves(self, which, matrix, count):
        first = self.moves.clip_bit == 0
        columns = self.mine.shape[2] // count
        part = slice(matrix * columns, (matrix + 1) * columns)
        mine, arrived = self.mine[which, :, part], self.arrived[which, :, part]
        return jnp.concatenate(
            [wide(jnp.where(first, mine, arrived)), wide(jnp.where(first, arrived, mine))], -1
        )


def frame_groups(frames, grid_a, grid_b):
    groups = [(i * grid_a, grid_a, None) for i in range(frames)]
    base = frames * grid_a
    if frames % 2 == 0:
        groups += [(base + i * grid_b, 2 * grid_b, ("block", grid_b, 1)) for i in range(0, frames, 2)]
    else:
        groups += [(base + i * grid_b, grid_b, None) for i in range(frames)]
    return tuple(groups)


def per_device(
    sizes,
    frames_a,
    frames_b,
    actions_a,
    actions_b,
    action_table,
    gain_space,
    space_qkv,
    space_out,
    gain_time,
    time_qkv,
    time_out,
    gain_ffn,
    ffn_up,
    ffn_down,
    cot_a,
    cot_b,
):
    moves = Moves(sizes)
    n_wide = sizes["wide"]
    _, n_frames, grid_a, depth = frames_a.shape
    grid_b = frames_b.shape[2]
    rows_a, rows_b = n_frames * grid_a, n_frames * grid_b
    rows = rows_a + rows_b
    spots_a, spots_b = grid_a // n_wide, grid_b // n_wide
    spots = spots_a + spots_b
    all_frames = n_frames * n_wide
    inner = 8 if spots % 8 == 0 else 4
    gain_space, gain_time, gain_ffn = (g[None] for g in (gain_space, gain_time, gain_ffn))

    def exchange(packed):
        return lax.all_to_all(packed, "wide", split_axis=0, concat_axis=0, tiled=True)

    def pack_grid(first, second):
        first = first.reshape(n_frames, n_wide, spots_a, depth)
        second = second.reshape(n_frames, n_wide, spots_b, depth)
        return jnp.concatenate([first, second], 2).transpose(1, 0, 2, 3)

    def unpack_grid(moved):
        moved = moved.reshape(all_frames, spots // inner, inner, depth)
        return moved.transpose(1, 0, 2, 3).reshape(rows, depth)

    def pack_frames(rows_in):
        packed = rows_in.reshape(spots // inner, n_wide, n_frames, inner, depth)
        return packed.transpose(1, 2, 0, 3, 4).reshape(n_wide, n_frames, spots, depth)

    def unpack_frames(moved):
        first = moved[:, :, :spots_a].transpose(1, 0, 2, 3).reshape(rows_a, depth)
        second = moved[:, :, spots_a:].transpose(1, 0, 2, 3).reshape(rows_b, depth)
        return jnp.concatenate([first, second])

    def both_clips(mine, partner):
        low = moves.tp == 0
        pair = jnp.stack([jnp.where(low, mine, partner), jnp.where(low, partner, mine)])
        return (
            pair[:, :rows_a].reshape(2, n_frames, grid_a, depth),
            pair[:, rows_a:].reshape(2, n_frames, grid_b, depth),
        )

    def pick(value):
        return lax.dynamic_index_in_dim(value, moves.tp, 0, keepdims=False)

    space_groups = frame_groups(n_frames, grid_a, grid_b)
    group = inner * all_frames
    time_groups = tuple((i, group, ("causal", all_frames, inner)) for i in range(0, rows, group))
    codes = jnp.arange(action_table.shape[0])
    acts = jnp.concatenate([actions_a, actions_b], 1)
    one_hot = (acts[:, :, None] == codes).astype(F32)
    shifts = jnp.einsum("cfa,ad->cfd", one_hot, action_table.astype(F32), precision=lax.Precision.HIGHEST)

    clip = moves.tp[None].astype(jnp.int32)
    n_codes = action_table.shape[0]

    def from_x(weight, axis, *deps):
        piece = moves.quarter(weight, axis)
        return swap(after(piece, *deps) if deps else piece, "tp", sizes)

    def from_y(value, *deps):
        return swap(after(value, *deps) if deps else value, "clip", sizes)

    def cores(value, *deps):
        return swap(after(value, *deps) if deps else value, "wide", sizes)

    so_x = from_x(space_out, 0)
    cot_moved = exchange(pack_grid(pick(cot_a), pick(cot_b)))
    (partner_heads,) = space_heads(
        1 - clip, frames_a, frames_b, shifts, gain_space, space_qkv, space_groups, False
    )
    heads_other = swap(partner_heads, "tp", sizes)
    so_y = from_y(so_x, partner_heads)
    heads_own, proj_own, logs_own, started, normed_space = space_heads(
        clip, frames_a, frames_b, shifts, gain_space, space_qkv, space_groups, True
    )
    so_slots = (so_x, cores(so_x, heads_own), so_y, cores(so_y, heads_own))
    middle = space_mix(moves.bits, started, heads_own, heads_other, space_out, so_slots)
    packed = pack_grid(middle[:rows_a], middle[rows_a:])
    middle = exchange(packed)

    out_piece = moves.quarter(time_out, 0)
    out_piece = out_piece.reshape(PAIR, -1, PAIR).transpose(1, 0, 2).reshape(1, -1, PAIR)
    time_piece = jnp.concatenate([moves.quarter(time_qkv, 2), out_piece])
    time_x = swap(after(time_piece, heads_own), "tp", sizes)
    up_x = from_x(ffn_up, 1, heads_own)
    time_y = from_y(time_x)
    time_slots = (time_x, cores(time_x), time_y, cores(time_y))
    down_x = from_x(ffn_down, 0, time_x)
    up_y = from_y(up_x, time_x)
    down_y = from_y(down_x)
    sq_x = from_x(space_qkv, 2, down_x)
    latest, normed_time, heads_time, proj_time, logs_time = time_forward(
        unpack_grid(middle), gain_time, time_qkv, time_out, time_slots, time_groups
    )
    middle = unpack_grid(middle)
    up_slots = (up_x, cores(up_x, latest), up_y, cores(up_y, latest))
    down_slots = (down_x, cores(down_x, latest), down_y, cores(down_y, latest))
    cot = unpack_grid(cot_moved)
    out, d_latest, normed_ffn, gelu, d_hidden, d_gain_ffn = feed_forward(
        latest, cot, gain_ffn, ffn_up, ffn_down, up_slots, down_slots
    )
    out_packed = pack_frames(out)
    out_moved = exchange(out_packed)
    sq_y = from_y(sq_x, out_packed)

    def product(left_arrays, terms, chunk, y_first, micros):
        return moves.reduction(
            grad_product(moves.bits, left_arrays, terms, chunk, y_first, sizes, micros), y_first
        )

    chunk = ffn_up.shape[1] // 4
    up = product([after(normed_ffn, out_packed)], [(0, (d_hidden, 0), (d_hidden, 1), 0, 1)], chunk, False, 15)
    down = product([after(cot, up.keep)], [(0, (gelu, 0), (gelu, 1), 0, 1)], chunk, True, 15)
    gate = up.second(down.keep)
    partial_time, d_proj_own = branch_back(
        "time_back", after(d_latest, gate), proj_time, logs_time, 0, (time_qkv, time_out), time_groups
    )
    sq_slots = (sq_x, cores(sq_x, partial_time), sq_y, cores(sq_y, partial_time))
    gate = down.second(partial_time)
    d_middle, d_proj_rest, d_gain_time, _ = branch_back(
        "time_back_end", d_latest, proj_time, logs_time, 2, (time_slots,), time_groups,
        (middle, gain_time, after(partial_time, gate, out_moved)), ((0, rows),),
    )
    packed = pack_frames(d_middle)
    d_middle = exchange(packed)
    gate = up.third(packed)
    heads_time = heads_time[:, None]
    own, rest = (d_proj_own, 0), (d_proj_rest, 0)
    time_one = product([after(normed_time, gate)], [(0, own, rest, 0, 2)], PAIR, False, 10)
    out_rows = unpack_frames(after(out_moved, time_one.keep))
    out_partner = swap(out_rows, "tp", sizes)
    time_two = product(
        [normed_time, after(d_latest, time_one.keep)],
        [(0, own, rest, 2, 1), (1, (heads_time, 0), (heads_time, 1), 0, 1)],
        PAIR, True, 10,
    )
    gate = time_one.second(time_two.keep)
    heads_rest, proj_rest, logs_rest = space_rest(after(normed_space, gate), sq_slots, space_groups)
    gate = down.third(heads_rest)
    gate2 = time_two.second(heads_rest)
    d_middle = unpack_frames(d_middle)
    d_middle = after(d_middle, gate, gate2)
    partial_space, d_proj_own = branch_back(
        "space_back", d_middle, proj_own, logs_own, 0, (space_qkv, space_out), space_groups
    )
    out_a, out_b = both_clips(out_rows, after(out_partner, partial_space))
    gate = time_one.third(partial_space)
    gate2 = time_two.third(gate)
    segments = tuple((i * grid_a, grid_a) for i in range(n_frames)) + tuple(
        (rows_a + i * grid_b, grid_b) for i in range(n_frames)
    )
    d_started, d_proj_rest, d_gain_space, frame_sums = branch_back(
        "space_back_end", d_middle, proj_rest, logs_rest, 0, (sq_slots, so_slots), space_groups,
        (started, gain_space, after(partial_space, gate, gate2, out_a, out_b)), segments, True,
    )
    own, rest = (d_proj_own, 0), (d_proj_rest, 0)
    gates = [r.sum(d_started) for r in (up, down, time_one, time_two)]
    ffn, time = Pair(moves, up, down), Pair(moves, time_one, time_two)
    gates = [ffn.fourth(*gates)]
    gates += [time.fourth(*gates)]
    d_table = jnp.einsum(
        "fa,fd->ad", pick(one_hot), frame_sums[: 2 * n_frames], precision=lax.Precision.HIGHEST
    )
    small, small_other = moves.small_first(jnp.concatenate([d_table, d_gain_space, d_gain_time, d_gain_ffn]))
    started_partner = swap(d_started, "tp", sizes)
    space_two = product(
        [after(normed_space, *gates, small), d_middle],
        [(0, own, rest, 2, 1), (1, (heads_own[:, None], 0), (heads_rest[:, None], 0), 0, 1)],
        PAIR, True, 10,
    )
    small = small + after(small_other, space_two.keep)
    small_other = swap(small, "tp", sizes)
    space_one = product([after(normed_space, space_two.keep, small)], [(0, own, rest, 0, 2)], PAIR, False, 10)
    gate = space_two.second(space_one.keep)
    small = small + after(small_other, gate)
    d_frames_a, d_frames_b = both_clips(d_started, after(started_partner, gate))
    gate = space_one.second(d_frames_a, d_frames_b)
    step = 1
    while step < sizes["clip"]:
        small = small + swap(small, "clip", sizes, step)
        step *= 2
    gate = ffn.fifth(gate)
    gate = time.fifth(gate, small)
    gate = space_two.third(gate)
    gate = space_one.third(gate)
    small = moves.small_last(after(small, gate))
    space_two.sum(small), space_one.sum()
    space = Pair(moves, space_one, space_two)
    space.fourth()
    space.fifth()

    def qkv(pair):
        return jnp.stack([pair.halves(0, 0, 2), pair.halves(0, 1, 2), pair.halves(1, 0, 2)])

    return (
        out_a,
        out_b,
        d_frames_a,
        d_frames_b,
        small[:n_codes],
        small[n_codes],
        qkv(space),
        space.halves(1, 1, 2).T,
        small[n_codes + 1],
        qkv(time),
        time.halves(1, 1, 2).T,
        small[n_codes + 2],
        ffn.halves(0, 0, 1),
        ffn.halves(1, 0, 1).T,
    )


def solution(mesh):
    sizes = dict(mesh.shape)
    return jax.shard_map(
        partial(per_device, sizes),
        mesh=mesh,
        in_specs=(
            P("clip", "wide", None, None),
            P("clip", "wide", None, None),
            P("clip", "wide"),
            P("clip", "wide"),
            P(),
            P(),
            P(None, None, "tp"),
            P("tp", None),
            P(),
            P(None, None, "tp"),
            P("tp", None),
            P(),
            P(None, "tp"),
            P("tp", None),
            P("clip", "wide", None, None),
            P("clip", "wide", None, None),
        ),
        out_specs=(
            P("clip", "wide", None, None),
            P("clip", "wide", None, None),
            P("clip", "wide", None, None),
            P("clip", "wide", None, None),
            P(None, "wide"),
            P("wide"),
            P(None, "wide", "tp"),
            P("tp", "wide"),
            P("wide"),
            P(None, "wide", "tp"),
            P("tp", "wide"),
            P("wide"),
            P("wide", "tp"),
            P("tp", "wide"),
        ),
        check_vma=False,
    )
```

```python
from functools import partial

import jax
import jax.numpy as jnp
from jax import lax
from jax.experimental import pallas as pl
from jax.experimental.pallas import tpu as pltpu
from jax.sharding import PartitionSpec as P

HEAD = 64
PAIR = 2 * HEAD
BLOCK = 2 * PAIR
BF = jnp.bfloat16
F32 = jnp.float32
LIMIT = 60 * 2**20


def dot_n(a, b):
    return lax.dot_general(a, b, (((1,), (0,)), ((), ())), preferred_element_type=F32)


def dot_t(a, b):
    return lax.dot_general(a, b, (((1,), (1,)), ((), ())), preferred_element_type=F32)


def shape_of(*dims, dtype=BF):
    return jax.ShapeDtypeStruct(dims, dtype)


def whole(*dims):
    return pl.BlockSpec(dims, lambda *_: (0,) * len(dims))


def any_spec():
    return pl.BlockSpec(memory_space=pl.ANY)


def params():
    return pltpu.CompilerParams(vmem_limit_bytes=LIMIT)


MICROS = {'space_partner': 1.2, 'space_own': 1.2, 'space_mix': 1.2, 'space_rest': 0.9985, 'time_forward': 44.8106, 'feed_forward': 4.9837, 'time_back': 11.3339, 'time_back_end': 0.852, 'space_back': 6.0811, 'space_back_end': 30.4331, 'grad_up': 12.841, 'grad_down': 0.5749, 'time_one': 0.1151, 'time_two': 0.6269, 'space_two': 0.3517, 'space_one': 1.624, 'pause0': 1.2, 'pause1': 1.2, 'pause2': 1.2, 'pause3': 1.2, 'pause4': 5.9164, 'pause5': 3.5109, 'pause6': 2.6464, 'pause7': 12.3069, 'pause8': 160.0718, 'pause9': 0.8432}


def cost(name):
    return pl.CostEstimate(flops=int(MICROS[name] * 1e9), bytes_accessed=2**20, transcendentals=0)


def group_mask(kind, length):
    if kind is None:
        return None
    name, size, inner = kind
    key = lax.broadcasted_iota(jnp.int32, (length, length), 0)
    query = lax.broadcasted_iota(jnp.int32, (length, length), 1)
    if name == "block":
        shift = size.bit_length() - 1
        return (query >> shift) == (key >> shift)
    shift = inner.bit_length() - 1
    return ((query & (inner - 1)) == (key & (inner - 1))) & ((key >> shift) <= (query >> shift))


def head_masks(value):
    lane = lax.broadcasted_iota(jnp.int32, (1, PAIR), 1)
    return (
        jnp.where(lane < HEAD, value, 0.0).astype(BF),
        jnp.where(lane < HEAD, 0.0, value).astype(BF),
    )


def attend_block(groups, proj_ref, heads_ref, logs_ref):
    scaled = head_masks(HEAD**-0.5)
    masks = {kind: group_mask(kind, length) for _, length, kind in groups}
    for pair in range(2):
        cols = slice(pair * PAIR, (pair + 1) * PAIR)
        for start, length, kind in groups:
            rows = slice(start, start + length)
            query, key, value = (proj_ref[i, rows, cols] for i in range(3))
            value_t = value.T
            outs = []
            for h in range(2):
                scores = dot_t(key * scaled[h], query)
                if kind is not None:
                    scores = jnp.where(masks[kind], scores, -1e30)
                largest = jnp.max(scores, 0, keepdims=True)
                shifted = jnp.exp(scores - largest)
                total = jnp.sum(shifted, 0, keepdims=True)
                out = dot_n(value_t[h * HEAD : (h + 1) * HEAD], shifted.astype(BF))
                outs.append(out * (1.0 / total))
                if logs_ref is not None:
                    logs_ref[2 * pair + h : 2 * pair + h + 1, rows] = largest + jnp.log(total)
            heads_ref[rows, cols] = jnp.concatenate(outs, 0).T.astype(BF)


def attend_back_block(groups, proj_ref, d_ref, logs_ref, o_ref):
    scale = HEAD**-0.5
    scaled = head_masks(scale)
    parts = head_masks(1.0)
    masks = {kind: group_mask(kind, length) for _, length, kind in groups}
    for pair in range(2):
        cols = slice(pair * PAIR, (pair + 1) * PAIR)
        for start, length, kind in groups:
            rows = slice(start, start + length)
            query, key, value = (proj_ref[i, rows, cols] for i in range(3))
            d_out = d_ref[rows, cols]
            key_t = key.T
            d_key = d_value = None
            d_query = []
            for h in range(2):
                soft = jnp.exp(
                    dot_t(key * scaled[h], query) - logs_ref[2 * pair + h : 2 * pair + h + 1, rows]
                )
                if kind is not None:
                    soft = jnp.where(masks[kind], soft, 0.0)
                d_soft = dot_t(value * parts[h], d_out)
                row_dot = jnp.sum(soft * d_soft, 0, keepdims=True)
                d_scores = (soft * (d_soft - row_dot)).astype(BF)
                key_term = dot_n(d_scores, query * parts[h])
                value_term = dot_n(soft.astype(BF), d_out * parts[h])
                d_key = key_term if h == 0 else d_key + key_term
                d_value = value_term if h == 0 else d_value + value_term
                d_query.append(dot_n(key_t[h * HEAD : (h + 1) * HEAD], d_scores))
            o_ref[0, rows, cols] = (jnp.concatenate(d_query, 0).T * scale).astype(BF)
            o_ref[1, rows, cols] = (d_key * scale).astype(BF)
            o_ref[2, rows, cols] = d_value.astype(BF)


def row_chunks(rows, size=64):
    return [slice(i, i + size) for i in range(0, rows, size)]


def norm_parts(values):
    centered = values - jnp.mean(values, -1, keepdims=True)
    inverse = lax.rsqrt(jnp.mean(centered * centered, -1, keepdims=True) + 1e-05)
    return centered * inverse, inverse


def project_block(normed_ref, weight, proj_ref):
    for i in range(3):
        proj_ref[i] = dot_n(normed_ref[...], weight(i)).astype(BF)


def space_kernel(groups, full, _, fa_ref, fb_ref, shift_ref, gain_ref, w_ref, *refs):
    if full:
        heads_ref, proj_ref, logs_ref, started_ref, normed_ref = refs
        proj, logs = proj_ref.at[0], logs_ref.at[0]
    else:
        heads_ref, proj, normed_ref = refs
        logs = None
    _, frames, grid_a, _ = fa_ref.shape
    grid_b = fb_ref.shape[2]

    @pl.when(pl.program_id(0) == 0)
    def _():
        gain = gain_ref[...]
        base = 0
        for frame_ref, grid, first in ((fa_ref, grid_a, 0), (fb_ref, grid_b, frames)):
            for f in range(frames):
                move = shift_ref[0, first + f : first + f + 1, :]
                for rows in row_chunks(grid):
                    values = frame_ref[0, f, rows, :].astype(F32) + move
                    out = slice(base + rows.start, base + rows.stop)
                    if full:
                        started_ref[out, :] = values
                    normed_ref[out, :] = (norm_parts(values)[0] * gain).astype(BF)
                base += grid

    project_block(normed_ref, lambda i: w_ref[i], proj)
    attend_block(groups, proj, heads_ref.at[0], logs)


def space_heads(clip, frames_a, frames_b, shifts, gain, qkv, groups, full):
    _, frames, grid_a, depth = frames_a.shape
    grid_b = frames_b.shape[2]
    rows = frames * (grid_a + grid_b)
    blocks = qkv.shape[2] // BLOCK

    def chosen(*dims):
        return pl.BlockSpec((1, *dims), lambda s, c: (c[0],) + (0,) * len(dims))

    heads = (pl.BlockSpec((1, rows, BLOCK), lambda s, c: (s, 0, 0)), shape_of(blocks, rows, BLOCK))
    if full:
        outs = [
            heads,
            (pl.BlockSpec((1, 3, rows, BLOCK), lambda s, c: (s, 0, 0, 0)), shape_of(blocks, 3, rows, BLOCK)),
            (pl.BlockSpec((1, 8, rows), lambda s, c: (s, 0, 0)), shape_of(blocks, 8, rows, dtype=F32)),
            (whole(rows, depth), shape_of(rows, depth, dtype=F32)),
            (whole(rows, depth), shape_of(rows, depth)),
        ]
        scratch = []
    else:
        outs = [heads]
        scratch = [pltpu.VMEM((3, rows, BLOCK), BF), pltpu.VMEM((rows, depth), BF)]
    return pl.pallas_call(
        partial(space_kernel, groups, full),
        grid_spec=pltpu.PrefetchScalarGridSpec(
            num_scalar_prefetch=1,
            grid=(blocks,),
            in_specs=[
                chosen(frames, grid_a, depth),
                chosen(frames, grid_b, depth),
                chosen(2 * frames, depth),
                whole(1, depth),
                pl.BlockSpec((3, depth, BLOCK), lambda s, c: (0, 0, s)),
            ],
            out_specs=[o[0] for o in outs],
            scratch_shapes=scratch,
        ),
        out_shape=[o[1] for o in outs],
        compiler_params=params(),
        cost_estimate=cost("space_own" if full else "space_partner"),
        name="space_own" if full else "space_partner",
    )(clip, frames_a, frames_b, shifts, gain, qkv)


def stream_weights(own_qkv, own_out, qkv_slots, out_slots, wq, wo, sems, step, steps, first=0):
    def start(index, slot):
        for s in range(steps):

            @pl.when(index == s)
            def _(s=s):
                if s + first < 2:
                    cols = pl.ds((s + first) * BLOCK, BLOCK)
                    pltpu.make_async_copy(own_qkv.at[:, :, cols], wq.at[slot], sems.at[slot, 0]).start()
                    if wo is not None:
                        pltpu.make_async_copy(own_out.at[cols, :], wo.at[slot], sems.at[slot, 1]).start()
                else:
                    for i in range(2):
                        part = 2 * (s + first - 2) + i
                        cols = pl.ds(i * PAIR, PAIR)
                        pltpu.make_async_copy(
                            qkv_slots[part].at[0:3], wq.at[slot, :, :, cols], sems.at[slot, 0]
                        ).start()
                        if wo is None:
                            continue
                        if out_slots is not None:
                            pltpu.make_async_copy(
                                out_slots[part], wo.at[slot, cols, :], sems.at[slot, 1]
                            ).start()
                            continue
                        for j in range(wo.shape[2] // PAIR):
                            place = pl.ds(j * PAIR, PAIR)
                            pltpu.make_async_copy(
                                qkv_slots[part].at[3, place, :], wo.at[slot, cols, place], sems.at[slot, 1]
                            ).start()

    slot = step % 2

    @pl.when(step == 0)
    def _():
        start(step, slot)

    @pl.when(step + 1 < steps)
    def _():
        start(step + 1, 1 - slot)

    pltpu.make_async_copy(wq.at[slot], wq.at[slot], sems.at[slot, 0]).wait()
    if wo is not None:
        pltpu.make_async_copy(wo.at[slot], wo.at[slot], sems.at[slot, 1]).wait()
    return slot


def rest_kernel(groups, normed_ref, q0, q1, q2, q3, heads_ref, proj_ref, logs_ref, wq, sems):
    slot = stream_weights(None, None, (q0, q1, q2, q3), None, wq, None, sems, pl.program_id(0), 2, 2)
    project_block(normed_ref, lambda i: wq[slot, i], proj_ref.at[0])
    attend_block(groups, proj_ref.at[0], heads_ref.at[0], logs_ref.at[0])


def space_rest(normed, qkv_slots, groups):
    rows, depth = normed.shape
    return pl.pallas_call(
        partial(rest_kernel, groups),
        grid=(2,),
        in_specs=[whole(rows, depth)] + [any_spec()] * 4,
        out_specs=[
            pl.BlockSpec((1, rows, BLOCK), lambda s: (s, 0, 0)),
            pl.BlockSpec((1, 3, rows, BLOCK), lambda s: (s, 0, 0, 0)),
            pl.BlockSpec((1, 8, rows), lambda s: (s, 0, 0)),
        ],
        out_shape=[
            shape_of(2, rows, BLOCK),
            shape_of(2, 3, rows, BLOCK),
            shape_of(2, 8, rows, dtype=F32),
        ],
        scratch_shapes=[pltpu.VMEM((2, 3, depth, BLOCK), BF), pltpu.SemaphoreType.DMA((2, 2))],
        compiler_params=params(),
        cost_estimate=cost("space_rest"),
        name="space_rest",
    )(normed, *qkv_slots)


def out_kernel(bits_ref, stream_ref, own_ref, other_ref, w_ref, o0, o1, o2, o3, mid_ref, assembled):
    clip_bit, core_bit = bits_ref[0], bits_ref[1]
    for i, piece in enumerate((o0, o1, o2, o3)):
        place = 2 * (clip_bit if i < 2 else 1 - clip_bit) + (core_bit if i % 2 == 0 else 1 - core_bit)
        assembled[pl.ds(pl.multiple_of(place * PAIR, PAIR), PAIR), :] = piece[...]
    total = stream_ref[...]
    for b in range(own_ref.shape[0]):
        cols = slice(b * BLOCK, (b + 1) * BLOCK)
        total = total + dot_n(own_ref[b], w_ref[cols, :]) + dot_n(other_ref[b], assembled[cols, :])
    mid_ref[...] = total.astype(BF)


def space_mix(bits, started, own, other, weight, out_slots):
    rows, depth = started.shape
    half = weight.shape[0]
    return pl.pallas_call(
        out_kernel,
        grid_spec=pltpu.PrefetchScalarGridSpec(
            num_scalar_prefetch=1,
            grid=(1,),
            in_specs=[whole(rows, depth), whole(*own.shape), whole(*other.shape), whole(half, depth)]
            + [whole(half // 4, depth)] * 4,
            out_specs=whole(rows, depth),
            scratch_shapes=[pltpu.VMEM((half, depth), BF)],
        ),
        out_shape=shape_of(rows, depth),
        compiler_params=params(),
        cost_estimate=cost("space_mix"),
        name="space_mix",
    )(bits, started, own, other, weight, *out_slots)


def time_kernel(groups, mid_ref, gain_ref, wq_any, wo_any, q0, q1, q2, q3,
                late_ref, normed_ref, heads_ref, proj_ref, logs_ref, acc, wq, wo, sems):
    step = pl.program_id(0)
    rows = mid_ref.shape[0]

    @pl.when(step == 0)
    def _():
        gain = gain_ref[...]
        for chunk in row_chunks(rows):
            values = mid_ref[chunk, :].astype(F32)
            acc[chunk, :] = values
            normed_ref[chunk, :] = (norm_parts(values)[0] * gain).astype(BF)

    slot = stream_weights(wq_any, wo_any, (q0, q1, q2, q3), None, wq, wo, sems, step, 4)
    project_block(normed_ref, lambda i: wq[slot, i], proj_ref.at[0])
    attend_block(groups, proj_ref.at[0], heads_ref.at[0], logs_ref.at[0])
    acc[...] += dot_n(heads_ref[0], wo[slot])

    @pl.when(step == 3)
    def _():
        late_ref[...] = acc[...].astype(BF)


def time_forward(middle, gain, qkv, out, slots, groups):
    rows, depth = middle.shape
    return pl.pallas_call(
        partial(time_kernel, groups),
        grid=(4,),
        in_specs=[whole(rows, depth), whole(1, depth)] + [any_spec()] * 6,
        out_specs=[
            whole(rows, depth),
            whole(rows, depth),
            pl.BlockSpec((1, rows, BLOCK), lambda s: (s, 0, 0)),
            pl.BlockSpec((1, 3, rows, BLOCK), lambda s: (s, 0, 0, 0)),
            pl.BlockSpec((1, 8, rows), lambda s: (s, 0, 0)),
        ],
        out_shape=[
            shape_of(rows, depth),
            shape_of(rows, depth),
            shape_of(4, rows, BLOCK),
            shape_of(4, 3, rows, BLOCK),
            shape_of(4, 8, rows, dtype=F32),
        ],
        scratch_shapes=[
            pltpu.VMEM((rows, depth), F32),
            pltpu.VMEM((2, 3, depth, BLOCK), BF),
            pltpu.VMEM((2, BLOCK, depth), BF),
            pltpu.SemaphoreType.DMA((2, 2)),
        ],
        compiler_params=params(),
        cost_estimate=cost("time_forward"),
        name="time_forward",
    )(middle, gain, qkv, out, *slots)


def gelu_parts(hidden):
    root = 0.7978845608028654
    square = hidden * hidden
    curve = jnp.tanh(hidden * (root + (root * 0.044715) * square))
    half = 0.5 + 0.5 * curve
    slope = half + hidden * (half * (1.0 - curve)) * (root + (3 * 0.044715 * root) * square)
    return hidden * half, slope


def norm_back_rows(values, gain, d_normed):
    normal, inverse = norm_parts(values)
    scaled = d_normed * gain
    mean_first = jnp.mean(scaled, -1, keepdims=True)
    mean_second = jnp.mean(scaled * normal, -1, keepdims=True)
    return (scaled - mean_first - normal * mean_second) * inverse, d_normed * normal


def ffn_kernel(late_ref, cot_ref, gain_ref, up_any, down_any, u0, u1, u2, u3, d0, d1, d2, d3,
               out_ref, d_late_ref, normed_ref, hidden_ref, d_gain_ref, total, d_normed, wu, wd, sems):
    step = pl.program_id(0)
    rows, depth = late_ref.shape
    width = wu.shape[2]
    steps = 8

    @pl.when(step == 0)
    def _():
        gain = gain_ref[...]
        for chunk in row_chunks(rows):
            values = late_ref[chunk, :].astype(F32)
            total[chunk, :] = values
            d_normed[chunk, :] = jnp.zeros_like(values)
            normed_ref[chunk, :] = (norm_parts(values)[0] * gain).astype(BF)

    def start(index, slot):
        for s in range(steps):

            @pl.when(index == s)
            def _(s=s):
                cols = pl.ds(s * width, width)
                up = up_any.at[:, cols] if s < 4 else (u0, u1, u2, u3)[s - 4]
                down = down_any.at[cols, :] if s < 4 else (d0, d1, d2, d3)[s - 4]
                pltpu.make_async_copy(up, wu.at[slot], sems.at[slot, 0]).start()
                pltpu.make_async_copy(down, wd.at[slot], sems.at[slot, 1]).start()

    slot = step % 2

    @pl.when(step == 0)
    def _():
        start(step, slot)

    @pl.when(step + 1 < steps)
    def _():
        start(step + 1, 1 - slot)

    pltpu.make_async_copy(wu.at[slot], wu.at[slot], sems.at[slot, 0]).wait()
    pltpu.make_async_copy(wd.at[slot], wd.at[slot], sems.at[slot, 1]).wait()
    for chunk in row_chunks(rows, rows // 2):
        gelu, slope = gelu_parts(dot_n(normed_ref[chunk, :], wu[slot]))
        gelu = gelu.astype(BF)
        hidden_ref[0, 0, chunk, :] = gelu
        d_hidden = (dot_t(cot_ref[chunk, :], wd[slot]) * slope).astype(BF)
        hidden_ref[0, 1, chunk, :] = d_hidden
        total[chunk, :] += dot_n(gelu, wd[slot])
        d_normed[chunk, :] += dot_t(d_hidden, wu[slot])

    @pl.when(step == steps - 1)
    def _():
        gain = gain_ref[...]
        d_gain = jnp.zeros_like(gain)
        for chunk in row_chunks(rows):
            out_ref[chunk, :] = total[chunk, :].astype(BF)
            back, d_gain_rows = norm_back_rows(late_ref[chunk, :].astype(F32), gain, d_normed[chunk, :])
            d_late_ref[chunk, :] = (cot_ref[chunk, :].astype(F32) + back).astype(BF)
            d_gain = d_gain + jnp.sum(d_gain_rows, 0, keepdims=True)
        d_gain_ref[...] = d_gain


def feed_forward(latest, cot, gain, up, down, up_slots, down_slots):
    rows, depth = latest.shape
    width = up.shape[1] // 4
    stream = pl.BlockSpec((1, 2, rows, width), lambda s: (s, 0, 0, 0))
    return pl.pallas_call(
        ffn_kernel,
        grid=(8,),
        in_specs=[whole(rows, depth), whole(rows, depth), whole(1, depth)] + [any_spec()] * 10,
        out_specs=[whole(rows, depth), whole(rows, depth), whole(rows, depth), stream, whole(1, depth)],
        out_shape=[
            shape_of(rows, depth),
            shape_of(rows, depth),
            shape_of(rows, depth),
            shape_of(8, 2, rows, width),
            shape_of(1, depth, dtype=F32),
        ],
        scratch_shapes=[
            pltpu.VMEM((rows, depth), F32),
            pltpu.VMEM((rows, depth), F32),
            pltpu.VMEM((2, depth, width), BF),
            pltpu.VMEM((2, width, depth), BF),
            pltpu.SemaphoreType.DMA((2, 2)),
        ],
        compiler_params=params(),
        cost_estimate=cost("feed_forward"),
        name="feed_forward",
    )(latest, cot, gain, up, down, *up_slots, *down_slots)


def back_kernel(groups, segments, sums, final, packed, offset, dy_ref, proj_any, logs_any, *refs):
    if final:
        stream_ref, gain_ref, partial_ref, q0, q1, q2, q3 = refs[:7]
        refs = refs[7:]
        out_slots = None
        if not packed:
            out_slots, refs = refs[:4], refs[4:]
        own, slots = (None, None), ((q0, q1, q2, q3), out_slots)
        d_stream_ref, d_proj_ref, d_gain_ref, sums_ref, d_normed = refs[:5]
        first = 2
    else:
        own, slots = refs[:2], (None, None)
        d_normed, d_proj_ref = refs[2:4]
        first = 0
    d_heads, proj, logs, wq, wo, sems, more = refs[-7:]
    step = pl.program_id(0)

    def start(index, slot):
        pltpu.make_async_copy(proj_any.at[index + offset], proj.at[slot], more.at[slot, 0]).start()
        pltpu.make_async_copy(logs_any.at[index + offset], logs.at[slot], more.at[slot, 1]).start()

    slot = step % 2

    @pl.when(step == 0)
    def _():
        start(step, slot)
        start(step + 1, 1 - slot)

    slot = stream_weights(*own, *slots, wq, wo, sems, step, 2, first)
    d_heads[...] = dot_t(dy_ref[...], wo[slot]).astype(BF)
    pltpu.make_async_copy(proj.at[slot], proj.at[slot], more.at[slot, 0]).wait()
    pltpu.make_async_copy(logs.at[slot], logs.at[slot], more.at[slot, 1]).wait()
    attend_back_block(groups, proj.at[slot], d_heads, logs.at[slot], d_proj_ref.at[0])
    term = (
        dot_t(d_proj_ref[0, 0], wq[slot, 0])
        + dot_t(d_proj_ref[0, 1], wq[slot, 1])
        + dot_t(d_proj_ref[0, 2], wq[slot, 2])
    )

    @pl.when(step == 0)
    def _():
        d_normed[...] = term + partial_ref[...] if final else term

    @pl.when(step > 0)
    def _():
        d_normed[...] += term

    if not final:
        return

    @pl.when(step == 1)
    def _():
        gain = gain_ref[...]
        d_gain = jnp.zeros_like(gain)
        for index, (begin, count) in enumerate(segments):
            summed = jnp.zeros_like(gain)
            for piece in row_chunks(count):
                chunk = slice(begin + piece.start, begin + piece.stop)
                back, d_gain_rows = norm_back_rows(stream_ref[chunk, :].astype(F32), gain, d_normed[chunk, :])
                d_values = dy_ref[chunk, :].astype(F32) + back
                d_stream_ref[chunk, :] = d_values.astype(BF)
                d_gain = d_gain + jnp.sum(d_gain_rows, 0, keepdims=True)
                if sums:
                    summed = summed + jnp.sum(d_values, 0, keepdims=True)
            if sums:
                sums_ref[index : index + 1, :] = summed
        d_gain_ref[...] = d_gain
        if not sums:
            sums_ref[...] = jnp.zeros_like(sums_ref)


def branch_back(name, dy, proj, logs, offset, weights, groups, tail=None, segments=(), sums=False):
    rows, depth = dy.shape
    final = tail is not None
    if final:
        slots = [piece for group in weights for piece in group]
        others = [*tail, *slots]
        specs = [whole(rows, depth), whole(1, depth), whole(rows, depth)] + [any_spec()] * len(slots)
        outs = [
            (whole(rows, depth), shape_of(rows, depth)),
            (pl.BlockSpec((1, 3, rows, BLOCK), lambda s: (s, 0, 0, 0)), shape_of(2, 3, rows, BLOCK)),
            (whole(1, depth), shape_of(1, depth, dtype=F32)),
            (whole(8, depth), shape_of(8, depth, dtype=F32)),
        ]
        scratch = [pltpu.VMEM((rows, depth), F32)]
    else:
        others = list(weights)
        specs = [any_spec()] * 2
        outs = [
            (whole(rows, depth), shape_of(rows, depth, dtype=F32)),
            (pl.BlockSpec((1, 3, rows, BLOCK), lambda s: (s, 0, 0, 0)), shape_of(2, 3, rows, BLOCK)),
        ]
        scratch = []
    return pl.pallas_call(
        partial(back_kernel, groups, segments, sums, final, len(weights) == 1, offset),
        grid=(2,),
        in_specs=[whole(rows, depth), any_spec(), any_spec()] + specs,
        out_specs=[o[0] for o in outs],
        out_shape=[o[1] for o in outs],
        scratch_shapes=scratch
        + [
            pltpu.VMEM((rows, BLOCK), BF),
            pltpu.VMEM((2, 3, rows, BLOCK), BF),
            pltpu.VMEM((2, 8, rows), F32),
            pltpu.VMEM((2, 3, depth, BLOCK), BF),
            pltpu.VMEM((2, BLOCK, depth), BF),
            pltpu.SemaphoreType.DMA((2, 2)),
            pltpu.SemaphoreType.DMA((2, 2)),
        ],
        compiler_params=params(),
        cost_estimate=cost(name),
        name=name,
    )(dy, proj, logs, *others)


def grad_kernel(chunk, y_first, lefts, bits_ref, *refs):
    count = len(lefts)
    n_left = max(lefts) + 1
    left_refs, refs = refs[: 2 * n_left], refs[2 * n_left :]
    own_refs, other_refs = refs[: 2 * count], refs[2 * count : 4 * count]
    keep_ref, leave_ref, turned = refs[4 * count :]
    step = pl.program_id(0)
    core_bit, z_index = bits_ref[1], bits_ref[2]
    _, stacks, cut, _ = keep_ref.shape
    rows = left_refs[0].shape[0]

    @pl.when(step == 0)
    def _():
        for n, left_ref in enumerate(left_refs):
            columns = slice(n % 2 * rows, (n % 2 + 1) * rows)
            for j in range(stacks):
                place = slice(j * cut, (j + 1) * cut)
                start = pl.multiple_of((z_index ^ j) * 2 * cut, 2 * cut)
                if cut % 128 == 0:
                    start = pl.multiple_of(start + core_bit * cut, cut)
                    turned[n // 2, place, columns] = left_ref[:, pl.ds(start, cut)].T
                    continue
                both = left_ref[:, pl.ds(start, 2 * cut)].T
                for core in range(2):

                    @pl.when(core_bit == core)
                    def _(core=core, both=both, place=place, n=n, columns=columns):
                        turned[n // 2, place, columns] = both[core * cut : (core + 1) * cut]

    def fill(half, out_ref):
        matrix = 0
        for term, n in enumerate(lefts):
            mine_ref, partner_ref = (own_refs if half == 0 else other_refs)[2 * term : 2 * term + 2]
            blocks, parts, _, span = mine_ref.shape
            for t in range(parts):
                for b in range(blocks):
                    mine = mine_ref[b, t]
                    if half == 0:
                        partner = partner_ref[b, t]
                    elif span == chunk:
                        partner = partner_ref[1 - b, t]
                    else:
                        partner = partner_ref[b, t]
                        partner = jnp.concatenate([partner[:, chunk:], partner[:, :chunk]], 1)
                    block = dot_n(turned[n], jnp.concatenate([mine, partner], 0)).astype(BF)
                    for i in range(span // chunk):
                        index = b * (span // chunk) + i
                        if half == 1:
                            index = index ^ core_bit
                        lanes = pl.ds(pl.multiple_of((2 * matrix + index) * chunk, chunk), chunk)
                        for j in range(stacks):
                            out_ref[0, j, :, lanes] = block[
                                j * cut : (j + 1) * cut, i * chunk : (i + 1) * chunk
                            ]
                matrix += 1

    for g in range(4):

        @pl.when(step == g)
        def _(g=g):
            first, second = 1 - g // 2, g % 2
            fill(second if y_first else first, leave_ref if first == 1 else keep_ref)


def grad_product(bits, left_arrays, terms, chunk, y_first, sizes, name):
    rows, depth = left_arrays[0][0].shape
    stacks = sizes["wide"] // 2
    cut = depth // sizes["wide"]
    columns = 2 * sum(term[4] for term in terms) * chunk

    def flip(g, half):
        if y_first:
            return 1 - g // 2
        return jnp.where(1 - g // 2 == half, g % 2, 1 - half)

    def half_spec(value, half, first_part, parts):
        arrays, at = value
        shape = arrays[0].shape
        lead = 2 * chunk // shape[3]

        def index(g, b):
            y = flip(g, half)
            return (2 * at + ((b[0] ^ y) if half == 0 else y), first_part // parts, 0, 0)

        return [pl.BlockSpec((lead, parts, *shape[2:]), index)] * 2

    block = (1, stacks, cut, columns)
    return pl.pallas_call(
        partial(grad_kernel, chunk, y_first, [term[0] for term in terms]),
        grid_spec=pltpu.PrefetchScalarGridSpec(
            num_scalar_prefetch=1,
            grid=(4,),
            in_specs=[whole(rows, depth)] * (2 * len(left_arrays))
            + [spec for term in terms for spec in half_spec(term[1], 0, *term[3:])]
            + [spec for term in terms for spec in half_spec(term[2], 1, *term[3:])],
            out_specs=[
                pl.BlockSpec(block, lambda g, b: (jnp.maximum(g - 2, 0), 0, 0, 0)),
                pl.BlockSpec(block, lambda g, b: (jnp.minimum(g, 1), 0, 0, 0)),
            ],
            scratch_shapes=[pltpu.VMEM((len(left_arrays), stacks * cut, 2 * rows), BF)],
        ),
        out_shape=[shape_of(2, stacks, cut, columns)] * 2,
        compiler_params=params(),
        cost_estimate=cost(name),
        name="grad_product",
    )(
        bits,
        *[array for pair in left_arrays for array in pair],
        *[array for term in terms for array in term[1][0]],
        *[array for term in terms for array in term[2][0]],
    )


def swap(value, axis, sizes, step=1):
    return lax.ppermute(value, axis, [(i, i ^ step) for i in range(sizes[axis])])


def after(value, *others):
    return lax.optimization_barrier((value, *others))[0]


def pause_kernel(x_ref, o_ref):
    o_ref[...] = x_ref[...]


def pause(tokens, *deps):
    token = after(jnp.zeros((8, 128), F32), *deps)
    tokens.append(pl.pallas_call(
        pause_kernel,
        out_shape=shape_of(8, 128, dtype=F32),
        cost_estimate=cost("pause%d" % len(tokens)),
        name="pause",
    )(token))
    return tokens[-1]


def wide(value):
    return value.astype(F32)


class Moves:
    def __init__(self, sizes):
        self.sizes = sizes
        self.tp = lax.axis_index("tp")
        self.clip = lax.axis_index("clip")
        self.clip_bit = self.clip % 2
        place = lax.axis_index("wide")
        self.core_bit = place % 2
        self.z = place // 2
        self.bits = jnp.stack([self.clip_bit, self.core_bit, self.z]).astype(jnp.int32)

    def quarter(self, weight, axis):
        size = weight.shape[axis] // 4
        return lax.dynamic_slice_in_dim(weight, (2 * self.clip_bit + self.core_bit) * size, size, axis)

    def spread(self, from_x):
        from_y = swap(from_x, "clip", self.sizes)
        return (from_x, swap(from_x, "wide", self.sizes), from_y, swap(from_y, "wide", self.sizes))

    def spread_core(self, from_x, from_y):
        return (from_x, swap(from_x, "wide", self.sizes), from_y, swap(from_y, "wide", self.sizes))

    def reduction(self, product, y_first):
        return Reduction(self, *product, y_first)

    def take(self, value, index, axis):
        return lax.dynamic_index_in_dim(value, index, axis, keepdims=False)

    def small_first(self, rows):
        count, depth = rows.shape
        wide_size = self.sizes["wide"]
        blocks = rows.reshape(count, wide_size // 2, 2, depth // wide_size).transpose(1, 2, 0, 3)
        other = swap(self.take(blocks, 1 - self.core_bit, 1), "wide", self.sizes)
        return self.take(blocks, self.core_bit, 1), other

    def small_last(self, total):
        result = self.take(total, self.z, 0)
        for j in range(1, self.sizes["wide"] // 2):
            result = result + swap(self.take(total, self.z ^ j, 0), "wide", self.sizes, 2 * j)
        return result


class Reduction:
    def __init__(self, moves, keep, leaving, y_first):
        self.moves, self.sizes, self.keep = moves, moves.sizes, keep
        self.axes = ("clip", "tp") if y_first else ("tp", "clip")
        self.leaving = leaving
        self.arrived = swap(leaving, self.axes[0], self.sizes)

    def third(self, *deps):
        keep = after(self.keep, *deps) if deps else self.keep
        total = wide(keep) + wide(self.arrived)
        self.leaving = total[1].astype(BF)
        self.mine = total[0].astype(BF)
        self.arrived = swap(self.leaving, self.axes[1], self.sizes)
        return self.leaving

    def sum(self, *deps):
        if deps:
            self.mine = after(self.mine, *deps)
        total = wide(self.mine) + wide(self.arrived)
        step = 2
        while step < self.sizes["clip"]:
            total = total + wide(swap(total.astype(BF), "clip", self.sizes, step))
            step *= 2
        self.total = total.astype(BF)
        return self.total


class Pair:
    def __init__(self, moves, one, two):
        self.moves, self.sizes, self.one, self.two = moves, moves.sizes, one, two

    def fourth(self, *deps):
        one, two = self.one.total, self.two.total
        if deps:
            one = after(one, *deps)
        low = jnp.stack([one, two], 1)
        self.mine = low[0]
        self.pieces = [swap(low[j], "wide", self.sizes, 2 * j) for j in range(1, low.shape[0])]
        return low

    def fifth(self, *deps):
        result = wide(after(self.mine, *deps) if deps else self.mine)
        for piece in self.pieces:
            result = result + wide(piece)
        self.mine = result.astype(BF)
        self.arrived = swap(self.mine, "clip", self.sizes)
        return self.mine

    def halves(self, which, matrix, count):
        first = self.moves.clip_bit == 0
        columns = self.mine.shape[2] // count
        part = slice(matrix * columns, (matrix + 1) * columns)
        mine, arrived = self.mine[which, :, part], self.arrived[which, :, part]
        return jnp.concatenate(
            [wide(jnp.where(first, mine, arrived)), wide(jnp.where(first, arrived, mine))], -1
        )


def frame_groups(frames, grid_a, grid_b):
    groups = [(i * grid_a, grid_a, None) for i in range(frames)]
    base = frames * grid_a
    if frames % 2 == 0:
        groups += [(base + i * grid_b, 2 * grid_b, ("block", grid_b, 1)) for i in range(0, frames, 2)]
    else:
        groups += [(base + i * grid_b, grid_b, None) for i in range(frames)]
    return tuple(groups)


def per_device(
    sizes,
    frames_a,
    frames_b,
    actions_a,
    actions_b,
    action_table,
    gain_space,
    space_qkv,
    space_out,
    gain_time,
    time_qkv,
    time_out,
    gain_ffn,
    ffn_up,
    ffn_down,
    cot_a,
    cot_b,
):
    moves = Moves(sizes)
    n_wide = sizes["wide"]
    _, n_frames, grid_a, depth = frames_a.shape
    grid_b = frames_b.shape[2]
    rows_a, rows_b = n_frames * grid_a, n_frames * grid_b
    rows = rows_a + rows_b
    spots_a, spots_b = grid_a // n_wide, grid_b // n_wide
    spots = spots_a + spots_b
    all_frames = n_frames * n_wide
    inner = 8 if spots % 8 == 0 else 4
    gain_space, gain_time, gain_ffn = (g[None] for g in (gain_space, gain_time, gain_ffn))

    def exchange(packed):
        return lax.all_to_all(packed, "wide", split_axis=0, concat_axis=0, tiled=True)

    def pack_grid(first, second):
        first = first.reshape(n_frames, n_wide, spots_a, depth)
        second = second.reshape(n_frames, n_wide, spots_b, depth)
        return jnp.concatenate([first, second], 2).transpose(1, 0, 2, 3)

    def unpack_grid(moved):
        moved = moved.reshape(all_frames, spots // inner, inner, depth)
        return moved.transpose(1, 0, 2, 3).reshape(rows, depth)

    def pack_frames(rows_in):
        packed = rows_in.reshape(spots // inner, n_wide, n_frames, inner, depth)
        return packed.transpose(1, 2, 0, 3, 4).reshape(n_wide, n_frames, spots, depth)

    def unpack_frames(moved):
        first = moved[:, :, :spots_a].transpose(1, 0, 2, 3).reshape(rows_a, depth)
        second = moved[:, :, spots_a:].transpose(1, 0, 2, 3).reshape(rows_b, depth)
        return jnp.concatenate([first, second])

    def both_clips(mine, partner):
        low = moves.tp == 0
        pair = jnp.stack([jnp.where(low, mine, partner), jnp.where(low, partner, mine)])
        return (
            pair[:, :rows_a].reshape(2, n_frames, grid_a, depth),
            pair[:, rows_a:].reshape(2, n_frames, grid_b, depth),
        )

    def pick(value):
        return lax.dynamic_index_in_dim(value, moves.tp, 0, keepdims=False)

    space_groups = frame_groups(n_frames, grid_a, grid_b)
    group = inner * all_frames
    time_groups = tuple((i, group, ("causal", all_frames, inner)) for i in range(0, rows, group))
    codes = jnp.arange(action_table.shape[0])
    acts = jnp.concatenate([actions_a, actions_b], 1)
    one_hot = (acts[:, :, None] == codes).astype(F32)
    shifts = jnp.einsum("cfa,ad->cfd", one_hot, action_table.astype(F32), precision=lax.Precision.HIGHEST)

    clip = moves.tp[None].astype(jnp.int32)
    n_codes = action_table.shape[0]

    def from_x(weight, axis, *deps):
        piece = moves.quarter(weight, axis)
        return swap(after(piece, *deps) if deps else piece, "tp", sizes)

    def from_y(value, *deps):
        return swap(after(value, *deps) if deps else value, "clip", sizes)

    def cores(value, *deps):
        return swap(after(value, *deps) if deps else value, "wide", sizes)

    tokens = []

    def product(left_arrays, terms, chunk, y_first, name):
        return grad_product(moves.bits, left_arrays, terms, chunk, y_first, sizes, name)

    def both(value, *deps):
        return (value, cores(value, *deps))

    so_piece = moves.quarter(space_out, 0)
    out_piece = moves.quarter(time_out, 0)
    out_piece = out_piece.reshape(PAIR, -1, PAIR).transpose(1, 0, 2).reshape(1, -1, PAIR)
    time_piece = jnp.concatenate([moves.quarter(time_qkv, 2), out_piece])
    cot_packed = pack_grid(pick(cot_a), pick(cot_b))
    so_x = swap(so_piece, "tp", sizes)
    time_x = swap(time_piece, "tp", sizes)
    cot_moved = exchange(cot_packed)
    token = pause(tokens, so_piece, time_piece, cot_packed)
    cot_moved = after(cot_moved, token)
    (partner_heads,) = space_heads(
        after(1 - clip, token),
        frames_a, frames_b, shifts, gain_space, space_qkv, space_groups, False,
    )
    heads_other = swap(partner_heads, "tp", sizes)
    so_y = from_y(so_x, partner_heads)
    heads_own, proj_own, logs_own, started, normed_space = space_heads(
        after(clip, partner_heads), frames_a, frames_b, shifts, gain_space, space_qkv, space_groups, True
    )
    so_x, so_y = after(so_x, heads_own), after(so_y, heads_own)
    so_slots = (so_x, cores(so_x), so_y, cores(so_y))
    up_piece = moves.quarter(ffn_up, 1)
    down_piece = moves.quarter(ffn_down, 0)
    up_x = swap(after(up_piece, heads_other), "tp", sizes)
    middle = space_mix(moves.bits, started, heads_own, heads_other, space_out, so_slots)
    packed = pack_grid(middle[:rows_a], middle[rows_a:])
    middle_moved = exchange(after(packed, cot_moved))
    time_x = after(time_x, packed)
    time_y = swap(time_x, "clip", sizes)
    time_x_core = cores(time_x)
    token = pause(tokens, packed)

    up_x = after(up_x, token)
    up_y = swap(up_x, "clip", sizes)
    up_x_core = cores(up_x)
    down_x = swap(after(down_piece, up_x), "tp", sizes)
    token = pause(tokens, up_x)
    time_y = after(time_y, token)
    time_slots = (time_x, time_x_core, time_y, cores(time_y))
    down_x = after(down_x, token)
    down_y = swap(down_x, "clip", sizes)
    down_x_core = cores(down_x)
    sq_x = swap(after(moves.quarter(space_qkv, 2), down_x), "tp", sizes)
    token = pause(tokens, time_y, down_x)
    middle = unpack_grid(after(middle_moved, token))
    up_y = after(up_y, token)
    up_y_core = cores(up_y)
    latest, normed_time, heads_time, proj_time, logs_time = time_forward(
        after(middle, up_y), gain_time, time_qkv, time_out, time_slots, time_groups
    )
    down_y = after(down_y, latest)
    up_slots = (up_x, up_x_core, up_y, up_y_core)
    down_slots = (down_x, down_x_core, down_y, cores(down_y))
    cot = unpack_grid(after(cot_moved, latest))
    out, d_latest, normed_ffn, hidden, d_gain_ffn = feed_forward(
        latest, cot, gain_ffn, ffn_up, ffn_down, up_slots, down_slots
    )

    out_packed = pack_frames(out)
    out_moved = exchange(out_packed)
    normed_time2, heads_time2 = both(normed_time, latest), both(heads_time[:, None], latest)
    cot2, normed_ffn2, hidden2 = both(cot, latest), both(normed_ffn), both(hidden)
    partial_time, d_proj_own = branch_back(
        "time_back", after(d_latest, out_packed), proj_time, logs_time, 0,
        (time_qkv, time_out), time_groups,
    )
    own = (both(d_proj_own), 0)
    d_latest2 = both(d_latest, partial_time)
    sq_x = after(sq_x, partial_time)
    sq_y = swap(sq_x, "clip", sizes)
    chunk = ffn_up.shape[1] // 4
    up = product(
        [(after(normed_ffn2[0], partial_time), normed_ffn2[1])],
        [(0, (hidden2, 0), (hidden2, 1), 1, 1)], chunk, False, "grad_up",
    )
    up = moves.reduction(up, False)
    sq_x, sq_y = after(sq_x, up.keep), after(sq_y, up.keep, d_latest2[1])
    sq_slots = (sq_x, cores(sq_x), sq_y, cores(sq_y))
    down = product(
        [(after(cot2[0], up.keep), cot2[1])], [(0, (hidden2, 0), (hidden2, 1), 0, 1)], chunk, True, "grad_down"
    )
    down = moves.reduction(down, True)
    out_rows = unpack_frames(after(out_moved, down.keep))
    out_partner = swap(out_rows, "tp", sizes)
    d_middle, d_proj_rest, d_gain_time, _ = branch_back(
        "time_back_end", d_latest, proj_time, logs_time, 2, (time_slots,), time_groups,
        (middle, gain_time, after(partial_time, out_rows)), ((0, rows),),
    )
    rest = (both(d_proj_rest), 0)
    packed = pack_frames(d_middle)
    d_middle = exchange(packed)
    gate = up.third(packed)
    time_one = product(
        [(after(normed_time, gate), normed_time2[1])], [(0, own, rest, 0, 2)], PAIR, False, "time_one"
    )
    time_one = moves.reduction(time_one, False)
    time_two = product(
        [(normed_time, normed_time2[1]), (after(d_latest, time_one.keep), d_latest2[1])],
        [(0, own, rest, 2, 1), (1, (heads_time2, 0), (heads_time2, 1), 0, 1)],
        PAIR, True, "time_two",
    )
    time_two = moves.reduction(time_two, True)
    gate = down.third(time_two.keep)
    out_a, out_b = both_clips(out_rows, after(out_partner, gate))
    heads_rest, proj_rest, logs_rest = space_rest(
        after(normed_space, gate, out_a, out_b), sq_slots, space_groups
    )
    heads_rest2 = both(heads_rest[:, None])
    heads_own2, normed_space2 = both(heads_own[:, None], heads_rest), both(normed_space, heads_rest)
    gate = time_one.third(heads_rest)
    d_middle = unpack_frames(after(d_middle, gate))
    d_middle2 = both(d_middle)
    partial_space, d_proj_own = branch_back(
        "space_back", d_middle, proj_own, logs_own, 0, (space_qkv, space_out), space_groups
    )
    own = (both(d_proj_own), 0)
    ffn, time = Pair(moves, up, down), Pair(moves, time_one, time_two)
    gates = [up.sum(partial_space), down.sum(partial_space)]
    ffn.fourth()
    gates += [time_two.third(gates[1])]
    token = pause(tokens, *gates)
    segments = tuple((i * grid_a, grid_a) for i in range(n_frames)) + tuple(
        (rows_a + i * grid_b, grid_b) for i in range(n_frames)
    )
    d_started, d_proj_rest, d_gain_space, frame_sums = branch_back(
        "space_back_end", d_middle, proj_rest, logs_rest, 0, (sq_slots, so_slots), space_groups,
        (started, gain_space, after(partial_space, token)), segments, True,
    )
    rest = (both(d_proj_rest), 0)
    started_partner = swap(d_started, "tp", sizes)
    d_table = jnp.einsum(
        "fa,fd->ad", pick(one_hot), frame_sums[: 2 * n_frames], precision=lax.Precision.HIGHEST
    )
    small, small_other = moves.small_first(jnp.concatenate([d_table, d_gain_space, d_gain_time, d_gain_ffn]))
    gates = [time_one.sum(d_started), time_two.sum(d_started)]
    time.fourth()
    space_two = product(
        [(after(normed_space, small, *gates), normed_space2[1]), d_middle2],
        [(0, own, rest, 2, 1), (1, (heads_own2, 0), (heads_rest2, 0), 0, 1)],
        PAIR, True, "space_two",
    )
    space_two = moves.reduction(space_two, True)
    small = small + after(small_other, space_two.keep)
    small_other = swap(small, "tp", sizes)
    space_one = product(
        [(after(normed_space, space_two.keep, small), normed_space2[1])], [(0, own, rest, 0, 2)], PAIR, False, "space_one"
    )
    space_one = moves.reduction(space_one, False)
    token = pause(tokens, space_one.keep)
    small = small + after(small_other, token)
    small_other = small
    step = 1
    while step < sizes["clip"]:
        small_other = swap(small, "clip", sizes, step)
        if 2 * step < sizes["clip"]:
            small = small + small_other
        step *= 2
    d_frames_a, d_frames_b = both_clips(d_started, after(started_partner, small))
    gate = space_two.third(d_frames_a, d_frames_b)
    gate2 = space_one.third(gate)
    gate3 = ffn.fifth(gate2)
    token = pause(tokens, gate, gate2, gate3)
    small = small + after(small_other, token)
    gates = [space_two.sum(token), space_one.sum(token)]
    space = Pair(moves, space_one, space_two)
    space.fourth()
    small = moves.small_last(after(small, *gates))
    gates += [time.fifth(gates[1])]
    token = pause(tokens, *gates)
    gate = space.fifth(token)
    token = pause(tokens, gate)
    ffn.arrived, time.arrived = after(ffn.arrived, gates[0]), after(time.arrived, token)
    space.arrived = after(space.arrived, token)

    small = small + sum(tokens)[:1, :1]

    def qkv(pair):
        return jnp.stack([pair.halves(0, 0, 2), pair.halves(0, 1, 2), pair.halves(1, 0, 2)])

    return (
        out_a,
        out_b,
        d_frames_a,
        d_frames_b,
        small[:n_codes],
        small[n_codes],
        qkv(space),
        space.halves(1, 1, 2).T,
        small[n_codes + 1],
        qkv(time),
        time.halves(1, 1, 2).T,
        small[n_codes + 2],
        ffn.halves(0, 0, 1),
        ffn.halves(1, 0, 1).T,
    )


def solution(mesh):
    sizes = dict(mesh.shape)
    return jax.shard_map(
        partial(per_device, sizes),
        mesh=mesh,
        in_specs=(
            P("clip", "wide", None, None),
            P("clip", "wide", None, None),
            P("clip", "wide"),
            P("clip", "wide"),
            P(),
            P(),
            P(None, None, "tp"),
            P("tp", None),
            P(),
            P(None, None, "tp"),
            P("tp", None),
            P(),
            P(None, "tp"),
            P("tp", None),
            P("clip", "wide", None, None),
            P("clip", "wide", None, None),
        ),
        out_specs=(
            P("clip", "wide", None, None),
            P("clip", "wide", None, None),
            P("clip", "wide", None, None),
            P("clip", "wide", None, None),
            P(None, "wide"),
            P("wide"),
            P(None, "wide", "tp"),
            P("tp", "wide"),
            P("wide"),
            P(None, "wide", "tp"),
            P("tp", "wide"),
            P("wide"),
            P("wide", "tp"),
            P("tp", "wide"),
        ),
        check_vma=False,
    )
```

```python
from functools import partial

import jax
import jax.numpy as jnp
from jax import lax
from jax.experimental import pallas as pl
from jax.experimental.pallas import tpu as pltpu
from jax.sharding import PartitionSpec as P

HEAD = 64
PAIR = 2 * HEAD
BLOCK = 2 * PAIR
BATCH = 2**30
BF = jnp.bfloat16
F32 = jnp.float32
LIMIT = 60 * 2**20


def dot_n(a, b):
    return lax.dot_general(a, b, (((1,), (0,)), ((), ())), preferred_element_type=F32)


def dot_t(a, b):
    return lax.dot_general(a, b, (((1,), (1,)), ((), ())), preferred_element_type=F32)


def shape_of(*dims, dtype=BF):
    return jax.ShapeDtypeStruct(dims, dtype)


def whole(*dims):
    return pl.BlockSpec(dims, lambda *_: (0,) * len(dims))


def any_spec():
    return pl.BlockSpec(memory_space=pl.ANY)


def params():
    return pltpu.CompilerParams(vmem_limit_bytes=LIMIT)


MICROS = {'space_partner': 8, 'space_own': 8, 'space_mix': 8, 'space_rest': 1.031, 'time_forward': 44.8106, 'feed_forward': 15.1219, 'time_back': 11.3339, 'time_back_end': 0.852, 'space_back': 6.0811, 'space_back_end': 30.4331, 'grad_up': 12.841, 'grad_down': 0.5749, 'time_one': 0.1151, 'time_two': 0.6269, 'space_two': 0.3517, 'space_one': 1.624, 'pause0': 1, 'pause1': 0.02, 'pause2': 12, 'pause3': 5.3533, 'pause4': 12, 'pause5': 5.9164, 'pause6': 3.5109, 'pause7': 2.6464, 'pause8': 12.3069, 'pause9': 160.0718, 'pause10': 0.8432, 'feed_forward_end': 15.1219}


def cost(name):
    return pl.CostEstimate(flops=int(MICROS[name] * 1e9), bytes_accessed=2**20, transcendentals=0)


def group_mask(kind, length):
    if kind is None:
        return None
    name, size, inner = kind
    key = lax.broadcasted_iota(jnp.int32, (length, length), 0)
    query = lax.broadcasted_iota(jnp.int32, (length, length), 1)
    if name == "block":
        shift = size.bit_length() - 1
        return (query >> shift) == (key >> shift)
    shift = inner.bit_length() - 1
    return ((query & (inner - 1)) == (key & (inner - 1))) & ((key >> shift) <= (query >> shift))


def head_masks(value):
    lane = lax.broadcasted_iota(jnp.int32, (1, PAIR), 1)
    return (
        jnp.where(lane < HEAD, value, 0.0).astype(BF),
        jnp.where(lane < HEAD, 0.0, value).astype(BF),
    )


def batches(groups):
    result, area = [], 0
    for group in groups:
        size = group[1] * group[1]
        if result and area + size <= BATCH:
            result[-1].append(group)
            area += size
        else:
            result.append([group])
            area = size
    return result


def attend_block(groups, proj_ref, heads_ref, logs_ref):
    scaled = head_masks(HEAD**-0.5)
    masks = {kind: group_mask(kind, length) for _, length, kind in groups}
    for batch in batches([(*group, pair) for pair in range(2) for group in groups]):
        if True:
            places = [slice(start, start + length) for start, length, _, _ in batch]
            spots = [slice(group[3] * PAIR, (group[3] + 1) * PAIR) for group in batch]
            items = [(g, h) for g in range(len(batch)) for h in range(2)]
            scores = [
                dot_t(proj_ref[1, places[g], spots[g]] * scaled[h], proj_ref[0, places[g], spots[g]]) for g, h in items
            ]
            scores = [
                scores[n] if batch[g][2] is None else jnp.where(masks[batch[g][2]], scores[n], -1e30)
                for n, (g, h) in enumerate(items)
            ]
            largest = [jnp.max(v, 0, keepdims=True) for v in scores]
            shifted = [jnp.exp(v - m) for v, m in zip(scores, largest)]
            totals = [jnp.sum(v, 0, keepdims=True) for v in shifted]
            values_t = [proj_ref[2, rows, cols].T for rows, cols in zip(places, spots)]
            outs = [
                dot_n(values_t[g][h * HEAD : (h + 1) * HEAD], shifted[n].astype(BF)) * (1.0 / totals[n])
                for n, (g, h) in enumerate(items)
            ]
            for n, (g, h) in enumerate(items):
                if logs_ref is not None:
                    logs_ref[2 * batch[g][3] + h : 2 * batch[g][3] + h + 1, places[g]] = largest[n] + jnp.log(totals[n])
            for g, (rows, cols) in enumerate(zip(places, spots)):
                heads_ref[rows, cols] = jnp.concatenate(outs[2 * g : 2 * g + 2], 0).T.astype(BF)


def attend_back_block(groups, proj_ref, d_ref, logs_ref, o_ref):
    scale = HEAD**-0.5
    scaled = head_masks(scale)
    parts = head_masks(1.0)
    masks = {kind: group_mask(kind, length) for _, length, kind in groups}
    for batch in batches([(*group, pair) for pair in range(2) for group in groups]):
        if True:
            places = [slice(start, start + length) for start, length, _, _ in batch]
            spots = [slice(group[3] * PAIR, (group[3] + 1) * PAIR) for group in batch]
            items = [(g, h) for g in range(len(batch)) for h in range(2)]
            scores = [
                dot_t(proj_ref[1, places[g], spots[g]] * scaled[h], proj_ref[0, places[g], spots[g]]) for g, h in items
            ]
            d_soft = [dot_t(proj_ref[2, places[g], spots[g]] * parts[h], d_ref[places[g], spots[g]]) for g, h in items]
            soft = [
                jnp.exp(scores[n] - logs_ref[2 * batch[g][3] + h : 2 * batch[g][3] + h + 1, places[g]])
                for n, (g, h) in enumerate(items)
            ]
            soft = [
                soft[n] if batch[g][2] is None else jnp.where(masks[batch[g][2]], soft[n], 0.0)
                for n, (g, h) in enumerate(items)
            ]
            row_dots = [jnp.sum(p * d, 0, keepdims=True) for p, d in zip(soft, d_soft)]
            d_scores = [(p * (d - r)).astype(BF) for p, d, r in zip(soft, d_soft, row_dots)]
            soft = [p.astype(BF) for p in soft]
            keys_t = [proj_ref[1, rows, cols].T for rows, cols in zip(places, spots)]
            d_query = [
                dot_n(keys_t[g][h * HEAD : (h + 1) * HEAD], d_scores[n]) for n, (g, h) in enumerate(items)
            ]
            d_key = [dot_n(d_scores[n], proj_ref[0, places[g], spots[g]] * parts[h]) for n, (g, h) in enumerate(items)]
            d_value = [dot_n(soft[n], d_ref[places[g], spots[g]] * parts[h]) for n, (g, h) in enumerate(items)]
            for g, (rows, cols) in enumerate(zip(places, spots)):
                o_ref[0, rows, cols] = (jnp.concatenate(d_query[2 * g : 2 * g + 2], 0).T * scale).astype(BF)
                o_ref[1, rows, cols] = ((d_key[2 * g] + d_key[2 * g + 1]) * scale).astype(BF)
                o_ref[2, rows, cols] = (d_value[2 * g] + d_value[2 * g + 1]).astype(BF)


def row_chunks(rows, size=64):
    return [slice(i, i + size) for i in range(0, rows, size)]


def norm_parts(values):
    centered = values - jnp.mean(values, -1, keepdims=True)
    inverse = lax.rsqrt(jnp.mean(centered * centered, -1, keepdims=True) + 1e-05)
    return centered * inverse, inverse


def project_block(normed_ref, weight, proj_ref):
    for i in range(3):
        proj_ref[i] = dot_n(normed_ref[...], weight(i)).astype(BF)


def space_kernel(groups, full, _, fa_ref, fb_ref, shift_ref, gain_ref, w_ref, *refs):
    if full:
        heads_ref, proj_ref, logs_ref, started_ref, normed_ref = refs
        proj, logs = proj_ref.at[0], logs_ref.at[0]
    else:
        heads_ref, proj, normed_ref = refs
        logs = None
    _, frames, grid_a, _ = fa_ref.shape
    grid_b = fb_ref.shape[2]

    @pl.when(pl.program_id(0) == 0)
    def _():
        gain = gain_ref[...]
        base = 0
        for frame_ref, grid, first in ((fa_ref, grid_a, 0), (fb_ref, grid_b, frames)):
            for f in range(frames):
                move = shift_ref[0, first + f : first + f + 1, :]
                for rows in row_chunks(grid):
                    values = frame_ref[0, f, rows, :].astype(F32) + move
                    out = slice(base + rows.start, base + rows.stop)
                    if full:
                        started_ref[out, :] = values
                    normed_ref[out, :] = (norm_parts(values)[0] * gain).astype(BF)
                base += grid

    project_block(normed_ref, lambda i: w_ref[i], proj)
    attend_block(groups, proj, heads_ref.at[0], logs)


def space_heads(clip, frames_a, frames_b, shifts, gain, qkv, groups, full):
    _, frames, grid_a, depth = frames_a.shape
    grid_b = frames_b.shape[2]
    rows = frames * (grid_a + grid_b)
    blocks = qkv.shape[2] // BLOCK

    def chosen(*dims):
        return pl.BlockSpec((1, *dims), lambda s, c: (c[0],) + (0,) * len(dims))

    heads = (pl.BlockSpec((1, rows, BLOCK), lambda s, c: (s, 0, 0)), shape_of(blocks, rows, BLOCK))
    if full:
        outs = [
            heads,
            (pl.BlockSpec((1, 3, rows, BLOCK), lambda s, c: (s, 0, 0, 0)), shape_of(blocks, 3, rows, BLOCK)),
            (pl.BlockSpec((1, 8, rows), lambda s, c: (s, 0, 0)), shape_of(blocks, 8, rows, dtype=F32)),
            (whole(rows, depth), shape_of(rows, depth, dtype=F32)),
            (whole(rows, depth), shape_of(rows, depth)),
        ]
        scratch = []
    else:
        outs = [heads]
        scratch = [pltpu.VMEM((3, rows, BLOCK), BF), pltpu.VMEM((rows, depth), BF)]
    return pl.pallas_call(
        partial(space_kernel, groups, full),
        grid_spec=pltpu.PrefetchScalarGridSpec(
            num_scalar_prefetch=1,
            grid=(blocks,),
            in_specs=[
                chosen(frames, grid_a, depth),
                chosen(frames, grid_b, depth),
                chosen(2 * frames, depth),
                whole(1, depth),
                pl.BlockSpec((3, depth, BLOCK), lambda s, c: (0, 0, s)),
            ],
            out_specs=[o[0] for o in outs],
            scratch_shapes=scratch,
        ),
        out_shape=[o[1] for o in outs],
        compiler_params=params(),
        cost_estimate=cost("space_own" if full else "space_partner"),
        name="space_own" if full else "space_partner",
    )(clip, frames_a, frames_b, shifts, gain, qkv)


def stream_weights(own_qkv, own_out, qkv_slots, out_slots, wq, wo, sems, step, steps, first=0):
    def start(index, slot):
        for s in range(steps):

            @pl.when(index == s)
            def _(s=s):
                if s + first < 2:
                    cols = pl.ds((s + first) * BLOCK, BLOCK)
                    pltpu.make_async_copy(own_qkv.at[:, :, cols], wq.at[slot], sems.at[slot, 0]).start()
                    if wo is not None:
                        pltpu.make_async_copy(own_out.at[cols, :], wo.at[slot], sems.at[slot, 1]).start()
                else:
                    for i in range(2):
                        part = 2 * (s + first - 2) + i
                        cols = pl.ds(i * PAIR, PAIR)
                        pltpu.make_async_copy(
                            qkv_slots[part].at[0:3], wq.at[slot, :, :, cols], sems.at[slot, 0]
                        ).start()
                        if wo is None:
                            continue
                        if out_slots is not None:
                            pltpu.make_async_copy(
                                out_slots[part], wo.at[slot, cols, :], sems.at[slot, 1]
                            ).start()
                            continue
                        for j in range(wo.shape[2] // PAIR):
                            place = pl.ds(j * PAIR, PAIR)
                            pltpu.make_async_copy(
                                qkv_slots[part].at[3, place, :], wo.at[slot, cols, place], sems.at[slot, 1]
                            ).start()

    slot = step % 2

    @pl.when(step == 0)
    def _():
        start(step, slot)

    @pl.when(step + 1 < steps)
    def _():
        start(step + 1, 1 - slot)

    pltpu.make_async_copy(wq.at[slot], wq.at[slot], sems.at[slot, 0]).wait()
    if wo is not None:
        pltpu.make_async_copy(wo.at[slot], wo.at[slot], sems.at[slot, 1]).wait()
    return slot


def rest_kernel(groups, normed_ref, q0, q1, q2, q3, heads_ref, proj_ref, logs_ref, wq, sems):
    slot = stream_weights(None, None, (q0, q1, q2, q3), None, wq, None, sems, pl.program_id(0), 2, 2)
    project_block(normed_ref, lambda i: wq[slot, i], proj_ref.at[0])
    attend_block(groups, proj_ref.at[0], heads_ref.at[0], logs_ref.at[0])


def space_rest(normed, qkv_slots, groups):
    rows, depth = normed.shape
    return pl.pallas_call(
        partial(rest_kernel, groups),
        grid=(2,),
        in_specs=[whole(rows, depth)] + [any_spec()] * 4,
        out_specs=[
            pl.BlockSpec((1, rows, BLOCK), lambda s: (s, 0, 0)),
            pl.BlockSpec((1, 3, rows, BLOCK), lambda s: (s, 0, 0, 0)),
            pl.BlockSpec((1, 8, rows), lambda s: (s, 0, 0)),
        ],
        out_shape=[
            shape_of(2, rows, BLOCK),
            shape_of(2, 3, rows, BLOCK),
            shape_of(2, 8, rows, dtype=F32),
        ],
        scratch_shapes=[pltpu.VMEM((2, 3, depth, BLOCK), BF), pltpu.SemaphoreType.DMA((2, 2))],
        compiler_params=params(),
        cost_estimate=cost("space_rest"),
        name="space_rest",
    )(normed, *qkv_slots)


def out_kernel(bits_ref, stream_ref, own_ref, other_ref, w_ref, o0, o1, o2, o3, mid_ref, assembled):
    clip_bit, core_bit = bits_ref[0], bits_ref[1]
    for i, piece in enumerate((o0, o1, o2, o3)):
        place = 2 * (clip_bit if i < 2 else 1 - clip_bit) + (core_bit if i % 2 == 0 else 1 - core_bit)
        assembled[pl.ds(pl.multiple_of(place * PAIR, PAIR), PAIR), :] = piece[...]
    total = stream_ref[...]
    for b in range(own_ref.shape[0]):
        cols = slice(b * BLOCK, (b + 1) * BLOCK)
        total = total + dot_n(own_ref[b], w_ref[cols, :]) + dot_n(other_ref[b], assembled[cols, :])
    mid_ref[...] = total.astype(BF)


def space_mix(bits, started, own, other, weight, out_slots):
    rows, depth = started.shape
    half = weight.shape[0]
    return pl.pallas_call(
        out_kernel,
        grid_spec=pltpu.PrefetchScalarGridSpec(
            num_scalar_prefetch=1,
            grid=(1,),
            in_specs=[whole(rows, depth), whole(*own.shape), whole(*other.shape), whole(half, depth)]
            + [whole(half // 4, depth)] * 4,
            out_specs=whole(rows, depth),
            scratch_shapes=[pltpu.VMEM((half, depth), BF)],
        ),
        out_shape=shape_of(rows, depth),
        compiler_params=params(),
        cost_estimate=cost("space_mix"),
        name="space_mix",
    )(bits, started, own, other, weight, *out_slots)


def time_kernel(groups, mid_ref, gain_ref, wq_any, wo_any, q0, q1, q2, q3,
                late_ref, normed_ref, heads_ref, proj_ref, logs_ref, acc, wq, wo, sems):
    step = pl.program_id(0)
    rows = mid_ref.shape[0]

    @pl.when(step == 0)
    def _():
        gain = gain_ref[...]
        for chunk in row_chunks(rows):
            values = mid_ref[chunk, :].astype(F32)
            acc[chunk, :] = values
            normed_ref[chunk, :] = (norm_parts(values)[0] * gain).astype(BF)

    slot = stream_weights(wq_any, wo_any, (q0, q1, q2, q3), None, wq, wo, sems, step, 4)
    project_block(normed_ref, lambda i: wq[slot, i], proj_ref.at[0])
    attend_block(groups, proj_ref.at[0], heads_ref.at[0], logs_ref.at[0])
    acc[...] += dot_n(heads_ref[0], wo[slot])

    @pl.when(step == 3)
    def _():
        late_ref[...] = acc[...].astype(BF)


def time_forward(middle, gain, qkv, out, slots, groups):
    rows, depth = middle.shape
    return pl.pallas_call(
        partial(time_kernel, groups),
        grid=(4,),
        in_specs=[whole(rows, depth), whole(1, depth)] + [any_spec()] * 6,
        out_specs=[
            whole(rows, depth),
            whole(rows, depth),
            pl.BlockSpec((1, rows, BLOCK), lambda s: (s, 0, 0)),
            pl.BlockSpec((1, 3, rows, BLOCK), lambda s: (s, 0, 0, 0)),
            pl.BlockSpec((1, 8, rows), lambda s: (s, 0, 0)),
        ],
        out_shape=[
            shape_of(rows, depth),
            shape_of(rows, depth),
            shape_of(4, rows, BLOCK),
            shape_of(4, 3, rows, BLOCK),
            shape_of(4, 8, rows, dtype=F32),
        ],
        scratch_shapes=[
            pltpu.VMEM((rows, depth), F32),
            pltpu.VMEM((2, 3, depth, BLOCK), BF),
            pltpu.VMEM((2, BLOCK, depth), BF),
            pltpu.SemaphoreType.DMA((2, 2)),
        ],
        compiler_params=params(),
        cost_estimate=cost("time_forward"),
        name="time_forward",
    )(middle, gain, qkv, out, *slots)


def gelu_parts(hidden):
    root = 0.7978845608028654
    square = hidden * hidden
    curve = jnp.tanh(hidden * (root + (root * 0.044715) * square))
    half = 0.5 + 0.5 * curve
    slope = half + hidden * (half * (1.0 - curve)) * (root + (3 * 0.044715 * root) * square)
    return hidden * half, slope


def norm_back_rows(values, gain, d_normed):
    normal, inverse = norm_parts(values)
    scaled = d_normed * gain
    mean_first = jnp.mean(scaled, -1, keepdims=True)
    mean_second = jnp.mean(scaled * normal, -1, keepdims=True)
    return (scaled - mean_first - normal * mean_second) * inverse, d_normed * normal


def ffn_kernel(final, late_ref, cot_ref, gain_ref, *refs):
    if final:
        normed_ref, total_in, d_normed_in, u0, u1, u2, u3, d0, d1, d2, d3 = refs[:11]
        out_ref, d_late_ref, hidden_ref, d_gain_ref, total, d_normed, wu, wd, sems = refs[11:]
    else:
        up_any, down_any, normed_ref, hidden_ref, total, d_normed, wu, wd, sems = refs
    step = pl.program_id(0)
    rows = late_ref.shape[0]
    width = wu.shape[2]
    steps = 4

    @pl.when(step == 0)
    def _():
        if final:
            total[...] = total_in[...]
            d_normed[...] = d_normed_in[...]
            return
        gain = gain_ref[...]
        for chunk in row_chunks(rows):
            values = late_ref[chunk, :].astype(F32)
            total[chunk, :] = values
            d_normed[chunk, :] = jnp.zeros_like(values)
            normed_ref[chunk, :] = (norm_parts(values)[0] * gain).astype(BF)

    def start(index, slot):
        for s in range(steps):

            @pl.when(index == s)
            def _(s=s):
                cols = pl.ds(s * width, width)
                up = (u0, u1, u2, u3)[s] if final else up_any.at[:, cols]
                down = (d0, d1, d2, d3)[s] if final else down_any.at[cols, :]
                pltpu.make_async_copy(up, wu.at[slot], sems.at[slot, 0]).start()
                pltpu.make_async_copy(down, wd.at[slot], sems.at[slot, 1]).start()

    slot = step % 2

    @pl.when(step == 0)
    def _():
        start(step, slot)

    @pl.when(step + 1 < steps)
    def _():
        start(step + 1, 1 - slot)

    pltpu.make_async_copy(wu.at[slot], wu.at[slot], sems.at[slot, 0]).wait()
    pltpu.make_async_copy(wd.at[slot], wd.at[slot], sems.at[slot, 1]).wait()
    for chunk in row_chunks(rows, rows // 2):
        gelu, slope = gelu_parts(dot_n(normed_ref[chunk, :], wu[slot]))
        gelu = gelu.astype(BF)
        hidden_ref[0, 0, chunk, :] = gelu
        d_hidden = (dot_t(cot_ref[chunk, :], wd[slot]) * slope).astype(BF)
        hidden_ref[0, 1, chunk, :] = d_hidden
        total[chunk, :] += dot_n(gelu, wd[slot])
        d_normed[chunk, :] += dot_t(d_hidden, wu[slot])

    if not final:
        return

    @pl.when(step == steps - 1)
    def _():
        gain = gain_ref[...]
        d_gain = jnp.zeros_like(gain)
        for chunk in row_chunks(rows):
            out_ref[chunk, :] = total[chunk, :].astype(BF)
            back, d_gain_rows = norm_back_rows(late_ref[chunk, :].astype(F32), gain, d_normed[chunk, :])
            d_late_ref[chunk, :] = (cot_ref[chunk, :].astype(F32) + back).astype(BF)
            d_gain = d_gain + jnp.sum(d_gain_rows, 0, keepdims=True)
        d_gain_ref[...] = d_gain


def feed_forward(latest, cot, gain, weights, width, tail=None):
    rows, depth = latest.shape
    stream = (pl.BlockSpec((1, 2, rows, width), lambda s: (s, 0, 0, 0)), shape_of(4, 2, rows, width))
    plain = (whole(rows, depth), shape_of(rows, depth))
    sums = (whole(rows, depth), shape_of(rows, depth, dtype=F32))
    final = tail is not None
    if final:
        outs = [plain, plain, stream, (whole(1, depth), shape_of(1, depth, dtype=F32))]
        scratch = [pltpu.VMEM((rows, depth), F32)] * 2
    else:
        outs = [plain, stream, sums, sums]
        scratch = []
    return pl.pallas_call(
        partial(ffn_kernel, final),
        grid=(4,),
        in_specs=[whole(rows, depth), whole(rows, depth), whole(1, depth)]
        + [whole(rows, depth)] * (3 if final else 0)
        + [any_spec()] * len(weights),
        out_specs=[o[0] for o in outs],
        out_shape=[o[1] for o in outs],
        scratch_shapes=scratch
        + [
            pltpu.VMEM((2, depth, width), BF),
            pltpu.VMEM((2, width, depth), BF),
            pltpu.SemaphoreType.DMA((2, 2)),
        ],
        compiler_params=params(),
        cost_estimate=cost("feed_forward_end" if final else "feed_forward"),
        name="feed_forward_end" if final else "feed_forward",
    )(latest, cot, gain, *(tail or ()), *weights)


def back_kernel(groups, segments, sums, final, packed, offset, dy_ref, proj_any, logs_any, *refs):
    if final:
        stream_ref, gain_ref, partial_ref, q0, q1, q2, q3 = refs[:7]
        refs = refs[7:]
        out_slots = None
        if not packed:
            out_slots, refs = refs[:4], refs[4:]
        own, slots = (None, None), ((q0, q1, q2, q3), out_slots)
        d_stream_ref, d_proj_ref, d_gain_ref, sums_ref, d_normed = refs[:5]
        first = 2
    else:
        own, slots = refs[:2], (None, None)
        d_normed, d_proj_ref = refs[2:4]
        first = 0
    d_heads, proj, logs, wq, wo, sems, more = refs[-7:]
    step = pl.program_id(0)

    def start(index, slot):
        pltpu.make_async_copy(proj_any.at[index + offset], proj.at[slot], more.at[slot, 0]).start()
        pltpu.make_async_copy(logs_any.at[index + offset], logs.at[slot], more.at[slot, 1]).start()

    slot = step % 2

    @pl.when(step == 0)
    def _():
        start(step, slot)
        start(step + 1, 1 - slot)

    slot = stream_weights(*own, *slots, wq, wo, sems, step, 2, first)
    d_heads[...] = dot_t(dy_ref[...], wo[slot]).astype(BF)
    pltpu.make_async_copy(proj.at[slot], proj.at[slot], more.at[slot, 0]).wait()
    pltpu.make_async_copy(logs.at[slot], logs.at[slot], more.at[slot, 1]).wait()
    attend_back_block(groups, proj.at[slot], d_heads, logs.at[slot], d_proj_ref.at[0])
    term = (
        dot_t(d_proj_ref[0, 0], wq[slot, 0])
        + dot_t(d_proj_ref[0, 1], wq[slot, 1])
        + dot_t(d_proj_ref[0, 2], wq[slot, 2])
    )

    @pl.when(step == 0)
    def _():
        d_normed[...] = term + partial_ref[...] if final else term

    @pl.when(step > 0)
    def _():
        d_normed[...] += term

    if not final:
        return

    @pl.when(step == 1)
    def _():
        gain = gain_ref[...]
        d_gain = jnp.zeros_like(gain)
        for index, (begin, count) in enumerate(segments):
            summed = jnp.zeros_like(gain)
            for piece in row_chunks(count):
                chunk = slice(begin + piece.start, begin + piece.stop)
                back, d_gain_rows = norm_back_rows(stream_ref[chunk, :].astype(F32), gain, d_normed[chunk, :])
                d_values = dy_ref[chunk, :].astype(F32) + back
                d_stream_ref[chunk, :] = d_values.astype(BF)
                d_gain = d_gain + jnp.sum(d_gain_rows, 0, keepdims=True)
                if sums:
                    summed = summed + jnp.sum(d_values, 0, keepdims=True)
            if sums:
                sums_ref[index : index + 1, :] = summed
        d_gain_ref[...] = d_gain
        if not sums:
            sums_ref[...] = jnp.zeros_like(sums_ref)


def branch_back(name, dy, proj, logs, offset, weights, groups, tail=None, segments=(), sums=False):
    rows, depth = dy.shape
    final = tail is not None
    if final:
        slots = [piece for group in weights for piece in group]
        others = [*tail, *slots]
        specs = [whole(rows, depth), whole(1, depth), whole(rows, depth)] + [any_spec()] * len(slots)
        outs = [
            (whole(rows, depth), shape_of(rows, depth)),
            (pl.BlockSpec((1, 3, rows, BLOCK), lambda s: (s, 0, 0, 0)), shape_of(2, 3, rows, BLOCK)),
            (whole(1, depth), shape_of(1, depth, dtype=F32)),
            (whole(8, depth), shape_of(8, depth, dtype=F32)),
        ]
        scratch = [pltpu.VMEM((rows, depth), F32)]
    else:
        others = list(weights)
        specs = [any_spec()] * 2
        outs = [
            (whole(rows, depth), shape_of(rows, depth, dtype=F32)),
            (pl.BlockSpec((1, 3, rows, BLOCK), lambda s: (s, 0, 0, 0)), shape_of(2, 3, rows, BLOCK)),
        ]
        scratch = []
    return pl.pallas_call(
        partial(back_kernel, groups, segments, sums, final, len(weights) == 1, offset),
        grid=(2,),
        in_specs=[whole(rows, depth), any_spec(), any_spec()] + specs,
        out_specs=[o[0] for o in outs],
        out_shape=[o[1] for o in outs],
        scratch_shapes=scratch
        + [
            pltpu.VMEM((rows, BLOCK), BF),
            pltpu.VMEM((2, 3, rows, BLOCK), BF),
            pltpu.VMEM((2, 8, rows), F32),
            pltpu.VMEM((2, 3, depth, BLOCK), BF),
            pltpu.VMEM((2, BLOCK, depth), BF),
            pltpu.SemaphoreType.DMA((2, 2)),
            pltpu.SemaphoreType.DMA((2, 2)),
        ],
        compiler_params=params(),
        cost_estimate=cost(name),
        name=name,
    )(dy, proj, logs, *others)


def grad_kernel(chunk, y_first, lefts, bits_ref, *refs):
    count = len(lefts)
    n_left = max(lefts) + 1
    left_refs, refs = refs[: 2 * n_left], refs[2 * n_left :]
    own_refs, other_refs = refs[: 2 * count], refs[2 * count : 4 * count]
    keep_ref, leave_ref, turned = refs[4 * count :]
    step = pl.program_id(0)
    core_bit, z_index = bits_ref[1], bits_ref[2]
    _, stacks, cut, _ = keep_ref.shape
    rows = left_refs[0].shape[0]

    @pl.when(step == 0)
    def _():
        for n, left_ref in enumerate(left_refs):
            columns = slice(n % 2 * rows, (n % 2 + 1) * rows)
            for j in range(stacks):
                place = slice(j * cut, (j + 1) * cut)
                start = pl.multiple_of((z_index ^ j) * 2 * cut, 2 * cut)
                if cut % 128 == 0:
                    start = pl.multiple_of(start + core_bit * cut, cut)
                    turned[n // 2, place, columns] = left_ref[:, pl.ds(start, cut)].T
                    continue
                both = left_ref[:, pl.ds(start, 2 * cut)].T
                for core in range(2):

                    @pl.when(core_bit == core)
                    def _(core=core, both=both, place=place, n=n, columns=columns):
                        turned[n // 2, place, columns] = both[core * cut : (core + 1) * cut]

    def fill(half, out_ref):
        matrix = 0
        for term, n in enumerate(lefts):
            mine_ref, partner_ref = (own_refs if half == 0 else other_refs)[2 * term : 2 * term + 2]
            blocks, parts, _, span = mine_ref.shape
            for t in range(parts):
                for b in range(blocks):
                    mine = mine_ref[b, t]
                    if half == 0:
                        partner = partner_ref[b, t]
                    elif span == chunk:
                        partner = partner_ref[1 - b, t]
                    else:
                        partner = partner_ref[b, t]
                        partner = jnp.concatenate([partner[:, chunk:], partner[:, :chunk]], 1)
                    block = dot_n(turned[n], jnp.concatenate([mine, partner], 0)).astype(BF)
                    for i in range(span // chunk):
                        index = b * (span // chunk) + i
                        if half == 1:
                            index = index ^ core_bit
                        lanes = pl.ds(pl.multiple_of((2 * matrix + index) * chunk, chunk), chunk)
                        for j in range(stacks):
                            out_ref[0, j, :, lanes] = block[
                                j * cut : (j + 1) * cut, i * chunk : (i + 1) * chunk
                            ]
                matrix += 1

    for g in range(4):

        @pl.when(step == g)
        def _(g=g):
            first, second = 1 - g // 2, g % 2
            fill(second if y_first else first, leave_ref if first == 1 else keep_ref)


def grad_product(bits, left_arrays, terms, chunk, y_first, sizes, name):
    rows, depth = left_arrays[0][0].shape
    stacks = sizes["wide"] // 2
    cut = depth // sizes["wide"]
    columns = 2 * sum(term[4] for term in terms) * chunk

    def flip(g, half):
        if y_first:
            return 1 - g // 2
        return jnp.where(1 - g // 2 == half, g % 2, 1 - half)

    def half_spec(value, half, first_part, parts):
        arrays, at = value
        shape = arrays[0].shape
        lead = 2 * chunk // shape[3]

        def index(g, b):
            y = flip(g, half)
            return (2 * at + ((b[0] ^ y) if half == 0 else y), first_part // parts, 0, 0)

        return [pl.BlockSpec((lead, parts, *shape[2:]), index)] * 2

    block = (1, stacks, cut, columns)
    return pl.pallas_call(
        partial(grad_kernel, chunk, y_first, [term[0] for term in terms]),
        grid_spec=pltpu.PrefetchScalarGridSpec(
            num_scalar_prefetch=1,
            grid=(4,),
            in_specs=[whole(rows, depth)] * (2 * len(left_arrays))
            + [spec for term in terms for spec in half_spec(term[1], 0, *term[3:])]
            + [spec for term in terms for spec in half_spec(term[2], 1, *term[3:])],
            out_specs=[
                pl.BlockSpec(block, lambda g, b: (jnp.maximum(g - 2, 0), 0, 0, 0)),
                pl.BlockSpec(block, lambda g, b: (jnp.minimum(g, 1), 0, 0, 0)),
            ],
            scratch_shapes=[pltpu.VMEM((len(left_arrays), stacks * cut, 2 * rows), BF)],
        ),
        out_shape=[shape_of(2, stacks, cut, columns)] * 2,
        compiler_params=params(),
        cost_estimate=cost(name),
        name="grad_product",
    )(
        bits,
        *[array for pair in left_arrays for array in pair],
        *[array for term in terms for array in term[1][0]],
        *[array for term in terms for array in term[2][0]],
    )


def swap(value, axis, sizes, step=1):
    return lax.ppermute(value, axis, [(i, i ^ step) for i in range(sizes[axis])])


def after(value, *others):
    return lax.optimization_barrier((value, *others))[0]


def pause_kernel(x_ref, o_ref):
    o_ref[...] = x_ref[...]


def pause(tokens, *deps):
    token = after(jnp.zeros((8, 128), F32), *deps)
    tokens.append(pl.pallas_call(
        pause_kernel,
        out_shape=shape_of(8, 128, dtype=F32),
        cost_estimate=cost("pause%d" % len(tokens)),
        name="pause",
    )(token))
    return tokens[-1]


def wide(value):
    return value.astype(F32)


class Moves:
    def __init__(self, sizes):
        self.sizes = sizes
        self.tp = lax.axis_index("tp")
        self.clip = lax.axis_index("clip")
        self.clip_bit = self.clip % 2
        place = lax.axis_index("wide")
        self.core_bit = place % 2
        self.z = place // 2
        self.bits = jnp.stack([self.clip_bit, self.core_bit, self.z]).astype(jnp.int32)

    def quarter(self, weight, axis):
        size = weight.shape[axis] // 4
        return lax.dynamic_slice_in_dim(weight, (2 * self.clip_bit + self.core_bit) * size, size, axis)

    def spread(self, from_x):
        from_y = swap(from_x, "clip", self.sizes)
        return (from_x, swap(from_x, "wide", self.sizes), from_y, swap(from_y, "wide", self.sizes))

    def spread_core(self, from_x, from_y):
        return (from_x, swap(from_x, "wide", self.sizes), from_y, swap(from_y, "wide", self.sizes))

    def reduction(self, product, y_first):
        return Reduction(self, *product, y_first)

    def take(self, value, index, axis):
        return lax.dynamic_index_in_dim(value, index, axis, keepdims=False)

    def small_first(self, rows):
        count, depth = rows.shape
        wide_size = self.sizes["wide"]
        blocks = rows.reshape(count, wide_size // 2, 2, depth // wide_size).transpose(1, 2, 0, 3)
        other = swap(self.take(blocks, 1 - self.core_bit, 1), "wide", self.sizes)
        return self.take(blocks, self.core_bit, 1), other

    def small_last(self, total):
        result = self.take(total, self.z, 0)
        for j in range(1, self.sizes["wide"] // 2):
            result = result + swap(self.take(total, self.z ^ j, 0), "wide", self.sizes, 2 * j)
        return result


class Reduction:
    def __init__(self, moves, keep, leaving, y_first):
        self.moves, self.sizes, self.keep = moves, moves.sizes, keep
        self.axes = ("clip", "tp") if y_first else ("tp", "clip")
        self.leaving = leaving
        self.arrived = swap(leaving, self.axes[0], self.sizes)

    def third(self, *deps):
        keep = after(self.keep, *deps) if deps else self.keep
        total = wide(keep) + wide(self.arrived)
        self.leaving = total[1].astype(BF)
        self.mine = total[0].astype(BF)
        self.arrived = swap(self.leaving, self.axes[1], self.sizes)
        return self.leaving

    def sum(self, *deps):
        if deps:
            self.mine = after(self.mine, *deps)
        total = wide(self.mine) + wide(self.arrived)
        step = 2
        while step < self.sizes["clip"]:
            total = total + wide(swap(total.astype(BF), "clip", self.sizes, step))
            step *= 2
        self.total = total.astype(BF)
        return self.total


class Pair:
    def __init__(self, moves, one, two):
        self.moves, self.sizes, self.one, self.two = moves, moves.sizes, one, two

    def fourth(self, *deps):
        one, two = self.one.total, self.two.total
        if deps:
            one = after(one, *deps)
        low = jnp.stack([one, two], 1)
        self.mine = low[0]
        self.pieces = [swap(low[j], "wide", self.sizes, 2 * j) for j in range(1, low.shape[0])]
        return low

    def fifth(self, *deps):
        result = wide(after(self.mine, *deps) if deps else self.mine)
        for piece in self.pieces:
            result = result + wide(piece)
        self.mine = result.astype(BF)
        self.arrived = swap(self.mine, "clip", self.sizes)
        return self.mine

    def halves(self, which, matrix, count):
        first = self.moves.clip_bit == 0
        columns = self.mine.shape[2] // count
        part = slice(matrix * columns, (matrix + 1) * columns)
        mine, arrived = self.mine[which, :, part], self.arrived[which, :, part]
        return jnp.concatenate(
            [wide(jnp.where(first, mine, arrived)), wide(jnp.where(first, arrived, mine))], -1
        )


def frame_groups(frames, grid_a, grid_b):
    groups = [(i * grid_a, grid_a, None) for i in range(frames)]
    base = frames * grid_a
    if frames % 2 == 0:
        groups += [(base + i * grid_b, 2 * grid_b, ("block", grid_b, 1)) for i in range(0, frames, 2)]
    else:
        groups += [(base + i * grid_b, grid_b, None) for i in range(frames)]
    return tuple(groups)


def per_device(
    sizes,
    frames_a,
    frames_b,
    actions_a,
    actions_b,
    action_table,
    gain_space,
    space_qkv,
    space_out,
    gain_time,
    time_qkv,
    time_out,
    gain_ffn,
    ffn_up,
    ffn_down,
    cot_a,
    cot_b,
):
    moves = Moves(sizes)
    n_wide = sizes["wide"]
    _, n_frames, grid_a, depth = frames_a.shape
    grid_b = frames_b.shape[2]
    rows_a, rows_b = n_frames * grid_a, n_frames * grid_b
    rows = rows_a + rows_b
    spots_a, spots_b = grid_a // n_wide, grid_b // n_wide
    spots = spots_a + spots_b
    all_frames = n_frames * n_wide
    inner = 8 if spots % 8 == 0 else 4
    gain_space, gain_time, gain_ffn = (g[None] for g in (gain_space, gain_time, gain_ffn))

    def exchange(packed):
        return lax.all_to_all(packed, "wide", split_axis=0, concat_axis=0, tiled=True)

    def pack_grid(first, second):
        first = first.reshape(n_frames, n_wide, spots_a, depth)
        second = second.reshape(n_frames, n_wide, spots_b, depth)
        return jnp.concatenate([first, second], 2).transpose(1, 0, 2, 3)

    def unpack_grid(moved):
        moved = moved.reshape(all_frames, spots // inner, inner, depth)
        return moved.transpose(1, 0, 2, 3).reshape(rows, depth)

    def pack_frames(rows_in):
        packed = rows_in.reshape(spots // inner, n_wide, n_frames, inner, depth)
        return packed.transpose(1, 2, 0, 3, 4).reshape(n_wide, n_frames, spots, depth)

    def unpack_frames(moved):
        first = moved[:, :, :spots_a].transpose(1, 0, 2, 3).reshape(rows_a, depth)
        second = moved[:, :, spots_a:].transpose(1, 0, 2, 3).reshape(rows_b, depth)
        return jnp.concatenate([first, second])

    def both_clips(mine, partner):
        low = moves.tp == 0
        pair = jnp.stack([jnp.where(low, mine, partner), jnp.where(low, partner, mine)])
        return (
            pair[:, :rows_a].reshape(2, n_frames, grid_a, depth),
            pair[:, rows_a:].reshape(2, n_frames, grid_b, depth),
        )

    def pick(value):
        return lax.dynamic_index_in_dim(value, moves.tp, 0, keepdims=False)

    space_groups = frame_groups(n_frames, grid_a, grid_b)
    group = inner * all_frames
    time_groups = tuple((i, group, ("causal", all_frames, inner)) for i in range(0, rows, group))
    codes = jnp.arange(action_table.shape[0])
    acts = jnp.concatenate([actions_a, actions_b], 1)
    one_hot = (acts[:, :, None] == codes).astype(F32)
    shifts = jnp.einsum("cfa,ad->cfd", one_hot, action_table.astype(F32), precision=lax.Precision.HIGHEST)

    clip = moves.tp[None].astype(jnp.int32)
    n_codes = action_table.shape[0]

    def from_x(weight, axis, *deps):
        piece = moves.quarter(weight, axis)
        return swap(after(piece, *deps) if deps else piece, "tp", sizes)

    def from_y(value, *deps):
        return swap(after(value, *deps) if deps else value, "clip", sizes)

    def cores(value, *deps):
        return swap(after(value, *deps) if deps else value, "wide", sizes)

    tokens = []

    def product(left_arrays, terms, chunk, y_first, name):
        return grad_product(moves.bits, left_arrays, terms, chunk, y_first, sizes, name)

    def both(value, *deps):
        return (value, cores(value, *deps))

    so_piece = moves.quarter(space_out, 0)
    out_piece = moves.quarter(time_out, 0)
    out_piece = out_piece.reshape(PAIR, -1, PAIR).transpose(1, 0, 2).reshape(1, -1, PAIR)
    time_piece = jnp.concatenate([moves.quarter(time_qkv, 2), out_piece])
    cot_packed = pack_grid(after(pick(cot_a), so_piece, time_piece), pick(cot_b))
    so_x = swap(so_piece, "tp", sizes)
    time_x = swap(time_piece, "tp", sizes)
    cot_moved = exchange(cot_packed)
    token = pause(tokens, so_piece, time_piece, cot_packed)
    cot_moved = after(cot_moved, token)
    (partner_heads,) = space_heads(
        after(1 - clip, token),
        frames_a, frames_b, shifts, gain_space, space_qkv, space_groups, False,
    )
    heads_other = swap(partner_heads, "tp", sizes)
    so_y = from_y(so_x, partner_heads)
    heads_own, proj_own, logs_own, started, normed_space = space_heads(
        after(clip, partner_heads), frames_a, frames_b, shifts, gain_space, space_qkv, space_groups, True
    )
    so_x, so_y = after(so_x, heads_own), after(so_y, heads_own)
    so_slots = (so_x, cores(so_x), so_y, cores(so_y))
    up_piece = moves.quarter(ffn_up, 1)
    down_piece = moves.quarter(ffn_down, 0)
    up_x = swap(after(up_piece, heads_other), "tp", sizes)
    token = pause(tokens, heads_other, up_piece, down_piece)
    middle = space_mix(moves.bits, after(started, token), heads_own, heads_other, space_out, so_slots)
    packed = pack_grid(middle[:rows_a], middle[rows_a:])
    middle_moved = exchange(after(packed, cot_moved))
    time_x = after(time_x, packed)
    time_y = swap(time_x, "clip", sizes)
    time_x_core = cores(time_x)
    token = pause(tokens, packed)

    up_x = after(up_x, token)
    up_y = swap(up_x, "clip", sizes)
    up_x_core = cores(up_x)
    down_x = swap(after(down_piece, up_x), "tp", sizes)
    token = pause(tokens, up_x)
    time_y = after(time_y, token)
    time_slots = (time_x, time_x_core, time_y, cores(time_y))
    down_x = after(down_x, token)
    down_y = swap(down_x, "clip", sizes)
    down_x_core = cores(down_x)
    sq_x = swap(after(moves.quarter(space_qkv, 2), down_x), "tp", sizes)
    token = pause(tokens, time_y, down_x)
    middle = unpack_grid(after(middle_moved, token))
    latest, normed_time, heads_time, proj_time, logs_time = time_forward(
        middle, gain_time, time_qkv, time_out, time_slots, time_groups
    )
    cot = unpack_grid(after(cot_moved, latest))
    width = ffn_up.shape[1] // 4
    normed_ffn, hidden_own, total_ffn, d_sum_ffn = feed_forward(latest, cot, gain_ffn, (ffn_up, ffn_down), width)
    up_y, down_y = after(up_y, hidden_own), after(down_y, hidden_own)
    up_slots = (up_x, up_x_core, up_y, cores(up_y))
    down_slots = (down_x, down_x_core, down_y, cores(down_y))
    out, d_latest, hidden_rest, d_gain_ffn = feed_forward(
        latest, cot, gain_ffn, (*up_slots, *down_slots), width, (normed_ffn, total_ffn, d_sum_ffn)
    )

    out_packed = pack_frames(out)
    out_moved = exchange(out_packed)
    normed_time2, heads_time2 = both(normed_time, latest), both(heads_time[:, None], latest)
    cot2, normed_ffn2, hidden2 = both(cot, latest), both(normed_ffn, latest), both(hidden_own)
    hidden_rest2 = both(hidden_rest)
    partial_time, d_proj_own = branch_back(
        "time_back", after(d_latest, out_packed), proj_time, logs_time, 0,
        (time_qkv, time_out), time_groups,
    )
    own = (both(d_proj_own), 0)
    d_latest2 = both(d_latest, partial_time)
    sq_x = after(sq_x, partial_time)
    sq_y = swap(sq_x, "clip", sizes)
    chunk = ffn_up.shape[1] // 4
    up = product(
        [(after(normed_ffn2[0], partial_time), normed_ffn2[1])],
        [(0, (hidden2, 0), (hidden_rest2, 0), 1, 1)], chunk, False, "grad_up",
    )
    up = moves.reduction(up, False)
    sq_x, sq_y = after(sq_x, up.keep), after(sq_y, up.keep, d_latest2[1])
    sq_slots = (sq_x, cores(sq_x), sq_y, cores(sq_y))
    down = product(
        [(after(cot2[0], up.keep), cot2[1])], [(0, (hidden2, 0), (hidden_rest2, 0), 0, 1)], chunk, True, "grad_down"
    )
    down = moves.reduction(down, True)
    out_rows = unpack_frames(after(out_moved, down.keep))
    out_partner = swap(out_rows, "tp", sizes)
    d_middle, d_proj_rest, d_gain_time, _ = branch_back(
        "time_back_end", d_latest, proj_time, logs_time, 2, (time_slots,), time_groups,
        (middle, gain_time, after(partial_time, out_rows)), ((0, rows),),
    )
    rest = (both(d_proj_rest), 0)
    packed = pack_frames(d_middle)
    d_middle = exchange(packed)
    gate = up.third(packed)
    time_one = product(
        [(after(normed_time, gate), normed_time2[1])], [(0, own, rest, 0, 2)], PAIR, False, "time_one"
    )
    time_one = moves.reduction(time_one, False)
    time_two = product(
        [(normed_time, normed_time2[1]), (after(d_latest, time_one.keep), d_latest2[1])],
        [(0, own, rest, 2, 1), (1, (heads_time2, 0), (heads_time2, 1), 0, 1)],
        PAIR, True, "time_two",
    )
    time_two = moves.reduction(time_two, True)
    gate = down.third(time_two.keep)
    out_a, out_b = both_clips(out_rows, after(out_partner, gate))
    heads_rest, proj_rest, logs_rest = space_rest(
        after(normed_space, gate, out_a, out_b), sq_slots, space_groups
    )
    heads_rest2 = both(heads_rest[:, None])
    heads_own2, normed_space2 = both(heads_own[:, None], heads_rest), both(normed_space, heads_rest)
    gate = time_one.third(heads_rest)
    d_middle = unpack_frames(after(d_middle, gate))
    d_middle2 = both(d_middle)
    partial_space, d_proj_own = branch_back(
        "space_back", d_middle, proj_own, logs_own, 0, (space_qkv, space_out), space_groups
    )
    own = (both(d_proj_own), 0)
    ffn, time = Pair(moves, up, down), Pair(moves, time_one, time_two)
    gates = [up.sum(partial_space), down.sum(partial_space)]
    ffn.fourth()
    gates += [time_two.third(gates[1])]
    token = pause(tokens, *gates)
    segments = tuple((i * grid_a, grid_a) for i in range(n_frames)) + tuple(
        (rows_a + i * grid_b, grid_b) for i in range(n_frames)
    )
    d_started, d_proj_rest, d_gain_space, frame_sums = branch_back(
        "space_back_end", d_middle, proj_rest, logs_rest, 0, (sq_slots, so_slots), space_groups,
        (started, gain_space, after(partial_space, token)), segments, True,
    )
    rest = (both(d_proj_rest), 0)
    started_partner = swap(d_started, "tp", sizes)
    d_table = jnp.einsum(
        "fa,fd->ad", pick(one_hot), frame_sums[: 2 * n_frames], precision=lax.Precision.HIGHEST
    )
    small, small_other = moves.small_first(jnp.concatenate([d_table, d_gain_space, d_gain_time, d_gain_ffn]))
    gates = [time_one.sum(d_started), time_two.sum(d_started)]
    time.fourth()
    space_two = product(
        [(after(normed_space, small, *gates), normed_space2[1]), d_middle2],
        [(0, own, rest, 2, 1), (1, (heads_own2, 0), (heads_rest2, 0), 0, 1)],
        PAIR, True, "space_two",
    )
    space_two = moves.reduction(space_two, True)
    small = small + after(small_other, space_two.keep)
    small_other = swap(small, "tp", sizes)
    space_one = product(
        [(after(normed_space, space_two.keep, small), normed_space2[1])], [(0, own, rest, 0, 2)], PAIR, False, "space_one"
    )
    space_one = moves.reduction(space_one, False)
    token = pause(tokens, space_one.keep)
    small = small + after(small_other, token)
    small_other = small
    step = 1
    while step < sizes["clip"]:
        small_other = swap(small, "clip", sizes, step)
        if 2 * step < sizes["clip"]:
            small = small + small_other
        step *= 2
    d_frames_a, d_frames_b = both_clips(d_started, after(started_partner, small))
    gate = space_two.third(d_frames_a, d_frames_b)
    gate2 = space_one.third(gate)
    gate3 = ffn.fifth(gate2)
    token = pause(tokens, gate, gate2, gate3)
    small = small + after(small_other, token)
    gates = [space_two.sum(token), space_one.sum(token)]
    space = Pair(moves, space_one, space_two)
    space.fourth()
    small = moves.small_last(after(small, *gates))
    gates += [time.fifth(gates[1])]
    token = pause(tokens, *gates)
    gate = space.fifth(token)
    token = pause(tokens, gate)
    ffn.arrived, time.arrived = after(ffn.arrived, gates[0]), after(time.arrived, token)
    space.arrived = after(space.arrived, token)

    small = small + sum(tokens)[:1, :1]

    def qkv(pair):
        return jnp.stack([pair.halves(0, 0, 2), pair.halves(0, 1, 2), pair.halves(1, 0, 2)])

    return (
        out_a,
        out_b,
        d_frames_a,
        d_frames_b,
        small[:n_codes],
        small[n_codes],
        qkv(space),
        space.halves(1, 1, 2).T,
        small[n_codes + 1],
        qkv(time),
        time.halves(1, 1, 2).T,
        small[n_codes + 2],
        ffn.halves(0, 0, 1),
        ffn.halves(1, 0, 1).T,
    )


def solution(mesh):
    sizes = dict(mesh.shape)
    return jax.shard_map(
        partial(per_device, sizes),
        mesh=mesh,
        in_specs=(
            P("clip", "wide", None, None),
            P("clip", "wide", None, None),
            P("clip", "wide"),
            P("clip", "wide"),
            P(),
            P(),
            P(None, None, "tp"),
            P("tp", None),
            P(),
            P(None, None, "tp"),
            P("tp", None),
            P(),
            P(None, "tp"),
            P("tp", None),
            P("clip", "wide", None, None),
            P("clip", "wide", None, None),
        ),
        out_specs=(
            P("clip", "wide", None, None),
            P("clip", "wide", None, None),
            P("clip", "wide", None, None),
            P("clip", "wide", None, None),
            P(None, "wide"),
            P("wide"),
            P(None, "wide", "tp"),
            P("tp", "wide"),
            P("wide"),
            P(None, "wide", "tp"),
            P("tp", "wide"),
            P("wide"),
            P("wide", "tp"),
            P("tp", "wide"),
        ),
        check_vma=False,
    )
```

```python
from functools import partial

import jax
import jax.numpy as jnp
from jax import lax
from jax.experimental import pallas as pl
from jax.experimental.pallas import tpu as pltpu
from jax.sharding import PartitionSpec as P

HEAD = 64
PAIR = 2 * HEAD
BLOCK = 2 * PAIR
BATCH = 2**30
BF = jnp.bfloat16
F32 = jnp.float32
LIMIT = 60 * 2**20


def dot_n(a, b):
    return lax.dot_general(a, b, (((1,), (0,)), ((), ())), preferred_element_type=F32)


def dot_t(a, b):
    return lax.dot_general(a, b, (((1,), (1,)), ((), ())), preferred_element_type=F32)


def shape_of(*dims, dtype=BF):
    return jax.ShapeDtypeStruct(dims, dtype)


def whole(*dims):
    return pl.BlockSpec(dims, lambda *_: (0,) * len(dims))


def any_spec():
    return pl.BlockSpec(memory_space=pl.ANY)


def params():
    return pltpu.CompilerParams(vmem_limit_bytes=LIMIT)


MICROS = {'space_partner': 8, 'space_own': 8, 'space_mix': 8, 'space_rest': 1.031, 'time_forward': 44.8106, 'feed_forward': 15.1219, 'time_back': 11.3339, 'time_back_end': 0.852, 'space_back': 6.0811, 'space_back_end': 30.4331, 'grad_up': 12.841, 'grad_down': 0.5749, 'time_one': 0.1151, 'time_two': 0.6269, 'space_two': 0.3517, 'space_one': 1.624, 'pause0': 1, 'pause1': 0.02, 'pause2': 12, 'pause3': 5.3533, 'pause4': 12, 'pause5': 5.9164, 'pause6': 3.5109, 'pause7': 2.6464, 'pause8': 12.3069, 'pause9': 160.0718, 'pause10': 0.8432, 'feed_forward_end': 15.1219}


def cost(name):
    return pl.CostEstimate(flops=int(MICROS[name] * 1e9), bytes_accessed=2**20, transcendentals=0)


def group_mask(kind, length):
    if kind is None:
        return None
    name, size, inner = kind
    key = lax.broadcasted_iota(jnp.int32, (length, length), 0)
    query = lax.broadcasted_iota(jnp.int32, (length, length), 1)
    if name == "block":
        shift = size.bit_length() - 1
        return (query >> shift) == (key >> shift)
    shift = inner.bit_length() - 1
    return ((query & (inner - 1)) == (key & (inner - 1))) & ((key >> shift) <= (query >> shift))


def head_masks(value):
    lane = lax.broadcasted_iota(jnp.int32, (1, PAIR), 1)
    return (
        jnp.where(lane < HEAD, value, 0.0).astype(BF),
        jnp.where(lane < HEAD, 0.0, value).astype(BF),
    )


def batches(groups):
    result, area = [], 0
    for group in groups:
        size = group[1] * group[1]
        if result and area + size <= BATCH:
            result[-1].append(group)
            area += size
        else:
            result.append([group])
            area = size
    return result


def attend_block(groups, proj_ref, heads_ref, logs_ref):
    scaled = head_masks(HEAD**-0.5)
    masks = {kind: group_mask(kind, length) for _, length, kind in groups}
    for batch in batches([(*group, pair) for pair in range(2) for group in groups]):
        if True:
            places = [slice(start, start + length) for start, length, _, _ in batch]
            spots = [slice(group[3] * PAIR, (group[3] + 1) * PAIR) for group in batch]
            items = [(g, h) for g in range(len(batch)) for h in range(2)]
            scores = [
                dot_t(proj_ref[1, places[g], spots[g]] * scaled[h], proj_ref[0, places[g], spots[g]]) for g, h in items
            ]
            scores = [
                scores[n] if batch[g][2] is None else jnp.where(masks[batch[g][2]], scores[n], -1e30)
                for n, (g, h) in enumerate(items)
            ]
            largest = [jnp.max(v, 0, keepdims=True) for v in scores]
            shifted = [jnp.exp(v - m) for v, m in zip(scores, largest)]
            totals = [jnp.sum(v, 0, keepdims=True) for v in shifted]
            values_t = [proj_ref[2, rows, cols].T for rows, cols in zip(places, spots)]
            outs = [
                dot_n(values_t[g][h * HEAD : (h + 1) * HEAD], shifted[n].astype(BF)) * (1.0 / totals[n])
                for n, (g, h) in enumerate(items)
            ]
            for n, (g, h) in enumerate(items):
                if logs_ref is not None:
                    logs_ref[2 * batch[g][3] + h : 2 * batch[g][3] + h + 1, places[g]] = largest[n] + jnp.log(totals[n])
            for g, (rows, cols) in enumerate(zip(places, spots)):
                heads_ref[rows, cols] = jnp.concatenate(outs[2 * g : 2 * g + 2], 0).T.astype(BF)


def attend_back_block(groups, proj_ref, d_ref, logs_ref, o_ref):
    scale = HEAD**-0.5
    scaled = head_masks(scale)
    parts = head_masks(1.0)
    masks = {kind: group_mask(kind, length) for _, length, kind in groups}
    for batch in batches([(*group, pair) for pair in range(2) for group in groups]):
        if True:
            places = [slice(start, start + length) for start, length, _, _ in batch]
            spots = [slice(group[3] * PAIR, (group[3] + 1) * PAIR) for group in batch]
            items = [(g, h) for g in range(len(batch)) for h in range(2)]
            scores = [
                dot_t(proj_ref[1, places[g], spots[g]] * scaled[h], proj_ref[0, places[g], spots[g]]) for g, h in items
            ]
            d_soft = [dot_t(proj_ref[2, places[g], spots[g]] * parts[h], d_ref[places[g], spots[g]]) for g, h in items]
            soft = [
                jnp.exp(scores[n] - logs_ref[2 * batch[g][3] + h : 2 * batch[g][3] + h + 1, places[g]])
                for n, (g, h) in enumerate(items)
            ]
            soft = [
                soft[n] if batch[g][2] is None else jnp.where(masks[batch[g][2]], soft[n], 0.0)
                for n, (g, h) in enumerate(items)
            ]
            row_dots = [jnp.sum(p * d, 0, keepdims=True) for p, d in zip(soft, d_soft)]
            d_scores = [(p * (d - r)).astype(BF) for p, d, r in zip(soft, d_soft, row_dots)]
            soft = [p.astype(BF) for p in soft]
            keys_t = [proj_ref[1, rows, cols].T for rows, cols in zip(places, spots)]
            d_query = [
                dot_n(keys_t[g][h * HEAD : (h + 1) * HEAD], d_scores[n]) for n, (g, h) in enumerate(items)
            ]
            d_key = [dot_n(d_scores[n], proj_ref[0, places[g], spots[g]] * parts[h]) for n, (g, h) in enumerate(items)]
            d_value = [dot_n(soft[n], d_ref[places[g], spots[g]] * parts[h]) for n, (g, h) in enumerate(items)]
            for g, (rows, cols) in enumerate(zip(places, spots)):
                o_ref[0, rows, cols] = (jnp.concatenate(d_query[2 * g : 2 * g + 2], 0).T * scale).astype(BF)
                o_ref[1, rows, cols] = ((d_key[2 * g] + d_key[2 * g + 1]) * scale).astype(BF)
                o_ref[2, rows, cols] = (d_value[2 * g] + d_value[2 * g + 1]).astype(BF)


def row_chunks(rows, size=64):
    return [slice(i, i + size) for i in range(0, rows, size)]


def norm_parts(values):
    centered = values - jnp.mean(values, -1, keepdims=True)
    inverse = lax.rsqrt(jnp.mean(centered * centered, -1, keepdims=True) + 1e-05)
    return centered * inverse, inverse


def project_block(normed_ref, weight, proj_ref):
    for i in range(3):
        proj_ref[i] = dot_n(normed_ref[...], weight(i)).astype(BF)


def space_kernel(groups, full, _, fa_ref, fb_ref, shift_ref, gain_ref, w_ref, *refs):
    if full:
        heads_ref, proj_ref, logs_ref, started_ref, normed_ref = refs
        proj, logs = proj_ref.at[0], logs_ref.at[0]
    else:
        heads_ref, proj, normed_ref = refs
        logs = None
    _, frames, grid_a, _ = fa_ref.shape
    grid_b = fb_ref.shape[2]

    @pl.when(pl.program_id(0) == 0)
    def _():
        gain = gain_ref[...]
        base = 0
        for frame_ref, grid, first in ((fa_ref, grid_a, 0), (fb_ref, grid_b, frames)):
            for f in range(frames):
                move = shift_ref[0, first + f : first + f + 1, :]
                for rows in row_chunks(grid):
                    values = frame_ref[0, f, rows, :].astype(F32) + move
                    out = slice(base + rows.start, base + rows.stop)
                    if full:
                        started_ref[out, :] = values
                    normed_ref[out, :] = (norm_parts(values)[0] * gain).astype(BF)
                base += grid

    project_block(normed_ref, lambda i: w_ref[i], proj)
    attend_block(groups, proj, heads_ref.at[0], logs)


def space_heads(clip, frames_a, frames_b, shifts, gain, qkv, groups, full):
    _, frames, grid_a, depth = frames_a.shape
    grid_b = frames_b.shape[2]
    rows = frames * (grid_a + grid_b)
    blocks = qkv.shape[2] // BLOCK

    def chosen(*dims):
        return pl.BlockSpec((1, *dims), lambda s, c: (c[0],) + (0,) * len(dims))

    heads = (pl.BlockSpec((1, rows, BLOCK), lambda s, c: (s, 0, 0)), shape_of(blocks, rows, BLOCK))
    if full:
        outs = [
            heads,
            (pl.BlockSpec((1, 3, rows, BLOCK), lambda s, c: (s, 0, 0, 0)), shape_of(blocks, 3, rows, BLOCK)),
            (pl.BlockSpec((1, 8, rows), lambda s, c: (s, 0, 0)), shape_of(blocks, 8, rows, dtype=F32)),
            (whole(rows, depth), shape_of(rows, depth, dtype=F32)),
            (whole(rows, depth), shape_of(rows, depth)),
        ]
        scratch = []
    else:
        outs = [heads]
        scratch = [pltpu.VMEM((3, rows, BLOCK), BF), pltpu.VMEM((rows, depth), BF)]
    return pl.pallas_call(
        partial(space_kernel, groups, full),
        grid_spec=pltpu.PrefetchScalarGridSpec(
            num_scalar_prefetch=1,
            grid=(blocks,),
            in_specs=[
                chosen(frames, grid_a, depth),
                chosen(frames, grid_b, depth),
                chosen(2 * frames, depth),
                whole(1, depth),
                pl.BlockSpec((3, depth, BLOCK), lambda s, c: (0, 0, s)),
            ],
            out_specs=[o[0] for o in outs],
            scratch_shapes=scratch,
        ),
        out_shape=[o[1] for o in outs],
        compiler_params=params(),
        cost_estimate=cost("space_own" if full else "space_partner"),
        name="space_own" if full else "space_partner",
    )(clip, frames_a, frames_b, shifts, gain, qkv)


def stream_weights(own_qkv, own_out, qkv_slots, out_slots, wq, wo, sems, step, steps, first=0):
    def start(index, slot):
        for s in range(steps):

            @pl.when(index == s)
            def _(s=s):
                if s + first < 2:
                    cols = pl.ds((s + first) * BLOCK, BLOCK)
                    pltpu.make_async_copy(own_qkv.at[:, :, cols], wq.at[slot], sems.at[slot, 0]).start()
                    if wo is not None:
                        pltpu.make_async_copy(own_out.at[cols, :], wo.at[slot], sems.at[slot, 1]).start()
                else:
                    for i in range(2):
                        part = 2 * (s + first - 2) + i
                        cols = pl.ds(i * PAIR, PAIR)
                        pltpu.make_async_copy(
                            qkv_slots[part].at[0:3], wq.at[slot, :, :, cols], sems.at[slot, 0]
                        ).start()
                        if wo is None:
                            continue
                        if out_slots is not None:
                            pltpu.make_async_copy(
                                out_slots[part], wo.at[slot, cols, :], sems.at[slot, 1]
                            ).start()
                            continue
                        for j in range(wo.shape[2] // PAIR):
                            place = pl.ds(j * PAIR, PAIR)
                            pltpu.make_async_copy(
                                qkv_slots[part].at[3, place, :], wo.at[slot, cols, place], sems.at[slot, 1]
                            ).start()

    slot = step % 2

    @pl.when(step == 0)
    def _():
        start(step, slot)

    @pl.when(step + 1 < steps)
    def _():
        start(step + 1, 1 - slot)

    pltpu.make_async_copy(wq.at[slot], wq.at[slot], sems.at[slot, 0]).wait()
    if wo is not None:
        pltpu.make_async_copy(wo.at[slot], wo.at[slot], sems.at[slot, 1]).wait()
    return slot


def rest_kernel(groups, normed_ref, q0, q1, q2, q3, heads_ref, proj_ref, logs_ref, wq, sems):
    slot = stream_weights(None, None, (q0, q1, q2, q3), None, wq, None, sems, pl.program_id(0), 2, 2)
    project_block(normed_ref, lambda i: wq[slot, i], proj_ref.at[0])
    attend_block(groups, proj_ref.at[0], heads_ref.at[0], logs_ref.at[0])


def space_rest(normed, qkv_slots, groups):
    rows, depth = normed.shape
    return pl.pallas_call(
        partial(rest_kernel, groups),
        grid=(2,),
        in_specs=[whole(rows, depth)] + [any_spec()] * 4,
        out_specs=[
            pl.BlockSpec((1, rows, BLOCK), lambda s: (s, 0, 0)),
            pl.BlockSpec((1, 3, rows, BLOCK), lambda s: (s, 0, 0, 0)),
            pl.BlockSpec((1, 8, rows), lambda s: (s, 0, 0)),
        ],
        out_shape=[
            shape_of(2, rows, BLOCK),
            shape_of(2, 3, rows, BLOCK),
            shape_of(2, 8, rows, dtype=F32),
        ],
        scratch_shapes=[pltpu.VMEM((2, 3, depth, BLOCK), BF), pltpu.SemaphoreType.DMA((2, 2))],
        compiler_params=params(),
        cost_estimate=cost("space_rest"),
        name="space_rest",
    )(normed, *qkv_slots)


def out_kernel(bits_ref, stream_ref, own_ref, other_ref, w_ref, o0, o1, o2, o3, mid_ref, assembled):
    clip_bit, core_bit = bits_ref[0], bits_ref[1]
    for i, piece in enumerate((o0, o1, o2, o3)):
        place = 2 * (clip_bit if i < 2 else 1 - clip_bit) + (core_bit if i % 2 == 0 else 1 - core_bit)
        assembled[pl.ds(pl.multiple_of(place * PAIR, PAIR), PAIR), :] = piece[...]
    total = stream_ref[...]
    for b in range(own_ref.shape[0]):
        cols = slice(b * BLOCK, (b + 1) * BLOCK)
        total = total + dot_n(own_ref[b], w_ref[cols, :]) + dot_n(other_ref[b], assembled[cols, :])
    mid_ref[...] = total.astype(BF)


def space_mix(bits, started, own, other, weight, out_slots):
    rows, depth = started.shape
    half = weight.shape[0]
    return pl.pallas_call(
        out_kernel,
        grid_spec=pltpu.PrefetchScalarGridSpec(
            num_scalar_prefetch=1,
            grid=(1,),
            in_specs=[whole(rows, depth), whole(*own.shape), whole(*other.shape), whole(half, depth)]
            + [whole(half // 4, depth)] * 4,
            out_specs=whole(rows, depth),
            scratch_shapes=[pltpu.VMEM((half, depth), BF)],
        ),
        out_shape=shape_of(rows, depth),
        compiler_params=params(),
        cost_estimate=cost("space_mix"),
        name="space_mix",
    )(bits, started, own, other, weight, *out_slots)


def time_kernel(groups, mid_ref, gain_ref, wq_any, wo_any, q0, q1, q2, q3,
                late_ref, normed_ref, heads_ref, proj_ref, logs_ref, acc, wq, wo, sems):
    step = pl.program_id(0)
    rows = mid_ref.shape[0]

    @pl.when(step == 0)
    def _():
        gain = gain_ref[...]
        for chunk in row_chunks(rows):
            values = mid_ref[chunk, :].astype(F32)
            acc[chunk, :] = values
            normed_ref[chunk, :] = (norm_parts(values)[0] * gain).astype(BF)

    slot = stream_weights(wq_any, wo_any, (q0, q1, q2, q3), None, wq, wo, sems, step, 4)
    project_block(normed_ref, lambda i: wq[slot, i], proj_ref.at[0])
    attend_block(groups, proj_ref.at[0], heads_ref.at[0], logs_ref.at[0])
    acc[...] += dot_n(heads_ref[0], wo[slot])

    @pl.when(step == 3)
    def _():
        late_ref[...] = acc[...].astype(BF)


def time_forward(middle, gain, qkv, out, slots, groups):
    rows, depth = middle.shape
    return pl.pallas_call(
        partial(time_kernel, groups),
        grid=(4,),
        in_specs=[whole(rows, depth), whole(1, depth)] + [any_spec()] * 6,
        out_specs=[
            whole(rows, depth),
            whole(rows, depth),
            pl.BlockSpec((1, rows, BLOCK), lambda s: (s, 0, 0)),
            pl.BlockSpec((1, 3, rows, BLOCK), lambda s: (s, 0, 0, 0)),
            pl.BlockSpec((1, 8, rows), lambda s: (s, 0, 0)),
        ],
        out_shape=[
            shape_of(rows, depth),
            shape_of(rows, depth),
            shape_of(4, rows, BLOCK),
            shape_of(4, 3, rows, BLOCK),
            shape_of(4, 8, rows, dtype=F32),
        ],
        scratch_shapes=[
            pltpu.VMEM((rows, depth), F32),
            pltpu.VMEM((2, 3, depth, BLOCK), BF),
            pltpu.VMEM((2, BLOCK, depth), BF),
            pltpu.SemaphoreType.DMA((2, 2)),
        ],
        compiler_params=params(),
        cost_estimate=cost("time_forward"),
        name="time_forward",
    )(middle, gain, qkv, out, *slots)


def gelu_parts(hidden):
    root = 0.7978845608028654
    square = hidden * hidden
    curve = jnp.tanh(hidden * (root + (root * 0.044715) * square))
    half = 0.5 + 0.5 * curve
    slope = half + hidden * (half * (1.0 - curve)) * (root + (3 * 0.044715 * root) * square)
    return hidden * half, slope


def norm_back_rows(values, gain, d_normed):
    normal, inverse = norm_parts(values)
    scaled = d_normed * gain
    mean_first = jnp.mean(scaled, -1, keepdims=True)
    mean_second = jnp.mean(scaled * normal, -1, keepdims=True)
    return (scaled - mean_first - normal * mean_second) * inverse, d_normed * normal


def ffn_kernel(final, late_ref, cot_ref, gain_ref, *refs):
    if final:
        normed_ref, total_in, d_normed_in, u0, u1, u2, u3, d0, d1, d2, d3 = refs[:11]
        out_ref, d_late_ref, hidden_ref, d_gain_ref, total, d_normed, wu, wd, sems = refs[11:]
    else:
        up_any, down_any, normed_ref, hidden_ref, total, d_normed, wu, wd, sems = refs
    step = pl.program_id(0)
    rows = late_ref.shape[0]
    width = wu.shape[2]
    steps = 4

    @pl.when(step == 0)
    def _():
        if final:
            total[...] = total_in[...]
            d_normed[...] = d_normed_in[...]
            return
        gain = gain_ref[...]
        for chunk in row_chunks(rows):
            values = late_ref[chunk, :].astype(F32)
            total[chunk, :] = values
            d_normed[chunk, :] = jnp.zeros_like(values)
            normed_ref[chunk, :] = (norm_parts(values)[0] * gain).astype(BF)

    def start(index, slot):
        for s in range(steps):

            @pl.when(index == s)
            def _(s=s):
                cols = pl.ds(s * width, width)
                up = (u0, u1, u2, u3)[s] if final else up_any.at[:, cols]
                down = (d0, d1, d2, d3)[s] if final else down_any.at[cols, :]
                pltpu.make_async_copy(up, wu.at[slot], sems.at[slot, 0]).start()
                pltpu.make_async_copy(down, wd.at[slot], sems.at[slot, 1]).start()

    slot = step % 2

    @pl.when(step == 0)
    def _():
        start(step, slot)

    @pl.when(step + 1 < steps)
    def _():
        start(step + 1, 1 - slot)

    pltpu.make_async_copy(wu.at[slot], wu.at[slot], sems.at[slot, 0]).wait()
    pltpu.make_async_copy(wd.at[slot], wd.at[slot], sems.at[slot, 1]).wait()
    for chunk in row_chunks(rows, rows):
        gelu, slope = gelu_parts(dot_n(normed_ref[chunk, :], wu[slot]))
        gelu = gelu.astype(BF)
        hidden_ref[0, 0, chunk, :] = gelu
        d_hidden = (dot_t(cot_ref[chunk, :], wd[slot]) * slope).astype(BF)
        hidden_ref[0, 1, chunk, :] = d_hidden
        total[chunk, :] += dot_n(gelu, wd[slot])
        d_normed[chunk, :] += dot_t(d_hidden, wu[slot])

    if not final:
        return

    @pl.when(step == steps - 1)
    def _():
        gain = gain_ref[...]
        d_gain = jnp.zeros_like(gain)
        for chunk in row_chunks(rows):
            out_ref[chunk, :] = total[chunk, :].astype(BF)
            back, d_gain_rows = norm_back_rows(late_ref[chunk, :].astype(F32), gain, d_normed[chunk, :])
            d_late_ref[chunk, :] = (cot_ref[chunk, :].astype(F32) + back).astype(BF)
            d_gain = d_gain + jnp.sum(d_gain_rows, 0, keepdims=True)
        d_gain_ref[...] = d_gain


def feed_forward(latest, cot, gain, weights, width, tail=None):
    rows, depth = latest.shape
    stream = (pl.BlockSpec((1, 2, rows, width), lambda s: (s, 0, 0, 0)), shape_of(4, 2, rows, width))
    plain = (whole(rows, depth), shape_of(rows, depth))
    sums = (whole(rows, depth), shape_of(rows, depth, dtype=F32))
    final = tail is not None
    if final:
        outs = [plain, plain, stream, (whole(1, depth), shape_of(1, depth, dtype=F32))]
        scratch = [pltpu.VMEM((rows, depth), F32)] * 2
    else:
        outs = [plain, stream, sums, sums]
        scratch = []
    return pl.pallas_call(
        partial(ffn_kernel, final),
        grid=(4,),
        in_specs=[whole(rows, depth), whole(rows, depth), whole(1, depth)]
        + [whole(rows, depth)] * (3 if final else 0)
        + [any_spec()] * len(weights),
        out_specs=[o[0] for o in outs],
        out_shape=[o[1] for o in outs],
        scratch_shapes=scratch
        + [
            pltpu.VMEM((2, depth, width), BF),
            pltpu.VMEM((2, width, depth), BF),
            pltpu.SemaphoreType.DMA((2, 2)),
        ],
        compiler_params=params(),
        cost_estimate=cost("feed_forward_end" if final else "feed_forward"),
        name="feed_forward_end" if final else "feed_forward",
    )(latest, cot, gain, *(tail or ()), *weights)


def back_kernel(groups, segments, sums, final, packed, offset, dy_ref, proj_any, logs_any, *refs):
    if final:
        stream_ref, gain_ref, partial_ref, q0, q1, q2, q3 = refs[:7]
        refs = refs[7:]
        out_slots = None
        if not packed:
            out_slots, refs = refs[:4], refs[4:]
        own, slots = (None, None), ((q0, q1, q2, q3), out_slots)
        d_stream_ref, d_proj_ref, d_gain_ref, sums_ref, d_normed = refs[:5]
        first = 2
    else:
        own, slots = refs[:2], (None, None)
        d_normed, d_proj_ref = refs[2:4]
        first = 0
    d_heads, proj, logs, wq, wo, sems, more = refs[-7:]
    step = pl.program_id(0)

    def start(index, slot):
        pltpu.make_async_copy(proj_any.at[index + offset], proj.at[slot], more.at[slot, 0]).start()
        pltpu.make_async_copy(logs_any.at[index + offset], logs.at[slot], more.at[slot, 1]).start()

    slot = step % 2

    @pl.when(step == 0)
    def _():
        start(step, slot)
        start(step + 1, 1 - slot)

    slot = stream_weights(*own, *slots, wq, wo, sems, step, 2, first)
    d_heads[...] = dot_t(dy_ref[...], wo[slot]).astype(BF)
    pltpu.make_async_copy(proj.at[slot], proj.at[slot], more.at[slot, 0]).wait()
    pltpu.make_async_copy(logs.at[slot], logs.at[slot], more.at[slot, 1]).wait()
    attend_back_block(groups, proj.at[slot], d_heads, logs.at[slot], d_proj_ref.at[0])
    term = (
        dot_t(d_proj_ref[0, 0], wq[slot, 0])
        + dot_t(d_proj_ref[0, 1], wq[slot, 1])
        + dot_t(d_proj_ref[0, 2], wq[slot, 2])
    )

    @pl.when(step == 0)
    def _():
        d_normed[...] = term + partial_ref[...] if final else term

    @pl.when(step > 0)
    def _():
        d_normed[...] += term

    if not final:
        return

    @pl.when(step == 1)
    def _():
        gain = gain_ref[...]
        d_gain = jnp.zeros_like(gain)
        for index, (begin, count) in enumerate(segments):
            summed = jnp.zeros_like(gain)
            for piece in row_chunks(count):
                chunk = slice(begin + piece.start, begin + piece.stop)
                back, d_gain_rows = norm_back_rows(stream_ref[chunk, :].astype(F32), gain, d_normed[chunk, :])
                d_values = dy_ref[chunk, :].astype(F32) + back
                d_stream_ref[chunk, :] = d_values.astype(BF)
                d_gain = d_gain + jnp.sum(d_gain_rows, 0, keepdims=True)
                if sums:
                    summed = summed + jnp.sum(d_values, 0, keepdims=True)
            if sums:
                sums_ref[index : index + 1, :] = summed
        d_gain_ref[...] = d_gain
        if not sums:
            sums_ref[...] = jnp.zeros_like(sums_ref)


def branch_back(name, dy, proj, logs, offset, weights, groups, tail=None, segments=(), sums=False):
    rows, depth = dy.shape
    final = tail is not None
    if final:
        slots = [piece for group in weights for piece in group]
        others = [*tail, *slots]
        specs = [whole(rows, depth), whole(1, depth), whole(rows, depth)] + [any_spec()] * len(slots)
        outs = [
            (whole(rows, depth), shape_of(rows, depth)),
            (pl.BlockSpec((1, 3, rows, BLOCK), lambda s: (s, 0, 0, 0)), shape_of(2, 3, rows, BLOCK)),
            (whole(1, depth), shape_of(1, depth, dtype=F32)),
            (whole(8, depth), shape_of(8, depth, dtype=F32)),
        ]
        scratch = [pltpu.VMEM((rows, depth), F32)]
    else:
        others = list(weights)
        specs = [any_spec()] * 2
        outs = [
            (whole(rows, depth), shape_of(rows, depth, dtype=F32)),
            (pl.BlockSpec((1, 3, rows, BLOCK), lambda s: (s, 0, 0, 0)), shape_of(2, 3, rows, BLOCK)),
        ]
        scratch = []
    return pl.pallas_call(
        partial(back_kernel, groups, segments, sums, final, len(weights) == 1, offset),
        grid=(2,),
        in_specs=[whole(rows, depth), any_spec(), any_spec()] + specs,
        out_specs=[o[0] for o in outs],
        out_shape=[o[1] for o in outs],
        scratch_shapes=scratch
        + [
            pltpu.VMEM((rows, BLOCK), BF),
            pltpu.VMEM((2, 3, rows, BLOCK), BF),
            pltpu.VMEM((2, 8, rows), F32),
            pltpu.VMEM((2, 3, depth, BLOCK), BF),
            pltpu.VMEM((2, BLOCK, depth), BF),
            pltpu.SemaphoreType.DMA((2, 2)),
            pltpu.SemaphoreType.DMA((2, 2)),
        ],
        compiler_params=params(),
        cost_estimate=cost(name),
        name=name,
    )(dy, proj, logs, *others)


def grad_kernel(chunk, y_first, lefts, bits_ref, *refs):
    count = len(lefts)
    n_left = max(lefts) + 1
    left_refs, refs = refs[: 2 * n_left], refs[2 * n_left :]
    own_refs, other_refs = refs[: 2 * count], refs[2 * count : 4 * count]
    keep_ref, leave_ref, turned = refs[4 * count :]
    step = pl.program_id(0)
    core_bit, z_index = bits_ref[1], bits_ref[2]
    _, stacks, cut, _ = keep_ref.shape
    rows = left_refs[0].shape[0]

    @pl.when(step == 0)
    def _():
        for n, left_ref in enumerate(left_refs):
            columns = slice(n % 2 * rows, (n % 2 + 1) * rows)
            for j in range(stacks):
                place = slice(j * cut, (j + 1) * cut)
                start = pl.multiple_of((z_index ^ j) * 2 * cut, 2 * cut)
                if cut % 128 == 0:
                    start = pl.multiple_of(start + core_bit * cut, cut)
                    turned[n // 2, place, columns] = left_ref[:, pl.ds(start, cut)].T
                    continue
                both = left_ref[:, pl.ds(start, 2 * cut)].T
                for core in range(2):

                    @pl.when(core_bit == core)
                    def _(core=core, both=both, place=place, n=n, columns=columns):
                        turned[n // 2, place, columns] = both[core * cut : (core + 1) * cut]

    def fill(half, out_ref):
        matrix = 0
        for term, n in enumerate(lefts):
            mine_ref, partner_ref = (own_refs if half == 0 else other_refs)[2 * term : 2 * term + 2]
            blocks, parts, _, span = mine_ref.shape
            for t in range(parts):
                for b in range(blocks):
                    mine = mine_ref[b, t]
                    if half == 0:
                        partner = partner_ref[b, t]
                    elif span == chunk:
                        partner = partner_ref[1 - b, t]
                    else:
                        partner = partner_ref[b, t]
                        partner = jnp.concatenate([partner[:, chunk:], partner[:, :chunk]], 1)
                    block = dot_n(turned[n], jnp.concatenate([mine, partner], 0)).astype(BF)
                    for i in range(span // chunk):
                        index = b * (span // chunk) + i
                        if half == 1:
                            index = index ^ core_bit
                        lanes = pl.ds(pl.multiple_of((2 * matrix + index) * chunk, chunk), chunk)
                        for j in range(stacks):
                            out_ref[0, j, :, lanes] = block[
                                j * cut : (j + 1) * cut, i * chunk : (i + 1) * chunk
                            ]
                matrix += 1

    for g in range(4):

        @pl.when(step == g)
        def _(g=g):
            first, second = 1 - g // 2, g % 2
            fill(second if y_first else first, leave_ref if first == 1 else keep_ref)


def grad_product(bits, left_arrays, terms, chunk, y_first, sizes, name):
    rows, depth = left_arrays[0][0].shape
    stacks = sizes["wide"] // 2
    cut = depth // sizes["wide"]
    columns = 2 * sum(term[4] for term in terms) * chunk

    def flip(g, half):
        if y_first:
            return 1 - g // 2
        return jnp.where(1 - g // 2 == half, g % 2, 1 - half)

    def half_spec(value, half, first_part, parts):
        arrays, at = value
        shape = arrays[0].shape
        lead = 2 * chunk // shape[3]

        def index(g, b):
            y = flip(g, half)
            return (2 * at + ((b[0] ^ y) if half == 0 else y), first_part // parts, 0, 0)

        return [pl.BlockSpec((lead, parts, *shape[2:]), index)] * 2

    block = (1, stacks, cut, columns)
    return pl.pallas_call(
        partial(grad_kernel, chunk, y_first, [term[0] for term in terms]),
        grid_spec=pltpu.PrefetchScalarGridSpec(
            num_scalar_prefetch=1,
            grid=(4,),
            in_specs=[whole(rows, depth)] * (2 * len(left_arrays))
            + [spec for term in terms for spec in half_spec(term[1], 0, *term[3:])]
            + [spec for term in terms for spec in half_spec(term[2], 1, *term[3:])],
            out_specs=[
                pl.BlockSpec(block, lambda g, b: (jnp.maximum(g - 2, 0), 0, 0, 0)),
                pl.BlockSpec(block, lambda g, b: (jnp.minimum(g, 1), 0, 0, 0)),
            ],
            scratch_shapes=[pltpu.VMEM((len(left_arrays), stacks * cut, 2 * rows), BF)],
        ),
        out_shape=[shape_of(2, stacks, cut, columns)] * 2,
        compiler_params=params(),
        cost_estimate=cost(name),
        name="grad_product",
    )(
        bits,
        *[array for pair in left_arrays for array in pair],
        *[array for term in terms for array in term[1][0]],
        *[array for term in terms for array in term[2][0]],
    )


def swap(value, axis, sizes, step=1):
    return lax.ppermute(value, axis, [(i, i ^ step) for i in range(sizes[axis])])


def after(value, *others):
    return lax.optimization_barrier((value, *others))[0]


def pause_kernel(x_ref, o_ref):
    o_ref[...] = x_ref[...]


def pause(tokens, *deps):
    token = after(jnp.zeros((8, 128), F32), *deps)
    tokens.append(pl.pallas_call(
        pause_kernel,
        out_shape=shape_of(8, 128, dtype=F32),
        cost_estimate=cost("pause%d" % len(tokens)),
        name="pause",
    )(token))
    return tokens[-1]


def wide(value):
    return value.astype(F32)


class Moves:
    def __init__(self, sizes):
        self.sizes = sizes
        self.tp = lax.axis_index("tp")
        self.clip = lax.axis_index("clip")
        self.clip_bit = self.clip % 2
        place = lax.axis_index("wide")
        self.core_bit = place % 2
        self.z = place // 2
        self.bits = jnp.stack([self.clip_bit, self.core_bit, self.z]).astype(jnp.int32)

    def quarter(self, weight, axis):
        size = weight.shape[axis] // 4
        return lax.dynamic_slice_in_dim(weight, (2 * self.clip_bit + self.core_bit) * size, size, axis)

    def spread(self, from_x):
        from_y = swap(from_x, "clip", self.sizes)
        return (from_x, swap(from_x, "wide", self.sizes), from_y, swap(from_y, "wide", self.sizes))

    def spread_core(self, from_x, from_y):
        return (from_x, swap(from_x, "wide", self.sizes), from_y, swap(from_y, "wide", self.sizes))

    def reduction(self, product, y_first):
        return Reduction(self, *product, y_first)

    def take(self, value, index, axis):
        return lax.dynamic_index_in_dim(value, index, axis, keepdims=False)

    def small_first(self, rows):
        count, depth = rows.shape
        wide_size = self.sizes["wide"]
        blocks = rows.reshape(count, wide_size // 2, 2, depth // wide_size).transpose(1, 2, 0, 3)
        other = swap(self.take(blocks, 1 - self.core_bit, 1), "wide", self.sizes)
        return self.take(blocks, self.core_bit, 1), other

    def small_last(self, total):
        result = self.take(total, self.z, 0)
        for j in range(1, self.sizes["wide"] // 2):
            result = result + swap(self.take(total, self.z ^ j, 0), "wide", self.sizes, 2 * j)
        return result


class Reduction:
    def __init__(self, moves, keep, leaving, y_first):
        self.moves, self.sizes, self.keep = moves, moves.sizes, keep
        self.axes = ("clip", "tp") if y_first else ("tp", "clip")
        self.leaving = leaving
        self.arrived = swap(leaving, self.axes[0], self.sizes)

    def third(self, *deps):
        keep = after(self.keep, *deps) if deps else self.keep
        total = wide(keep) + wide(self.arrived)
        self.leaving = total[1].astype(BF)
        self.mine = total[0].astype(BF)
        self.arrived = swap(self.leaving, self.axes[1], self.sizes)
        return self.leaving

    def sum(self, *deps):
        if deps:
            self.mine = after(self.mine, *deps)
        total = wide(self.mine) + wide(self.arrived)
        step = 2
        while step < self.sizes["clip"]:
            total = total + wide(swap(total.astype(BF), "clip", self.sizes, step))
            step *= 2
        self.total = total.astype(BF)
        return self.total


class Pair:
    def __init__(self, moves, one, two):
        self.moves, self.sizes, self.one, self.two = moves, moves.sizes, one, two

    def fourth(self, *deps):
        one, two = self.one.total, self.two.total
        if deps:
            one = after(one, *deps)
        low = jnp.stack([one, two], 1)
        self.mine = low[0]
        self.pieces = [swap(low[j], "wide", self.sizes, 2 * j) for j in range(1, low.shape[0])]
        return low

    def fifth(self, *deps):
        result = wide(after(self.mine, *deps) if deps else self.mine)
        for piece in self.pieces:
            result = result + wide(piece)
        self.mine = result.astype(BF)
        self.arrived = swap(self.mine, "clip", self.sizes)
        return self.mine

    def halves(self, which, matrix, count):
        first = self.moves.clip_bit == 0
        columns = self.mine.shape[2] // count
        part = slice(matrix * columns, (matrix + 1) * columns)
        mine, arrived = self.mine[which, :, part], self.arrived[which, :, part]
        return jnp.concatenate(
            [wide(jnp.where(first, mine, arrived)), wide(jnp.where(first, arrived, mine))], -1
        )


def frame_groups(frames, grid_a, grid_b):
    groups = [(i * grid_a, grid_a, None) for i in range(frames)]
    base = frames * grid_a
    if frames % 2 == 0:
        groups += [(base + i * grid_b, 2 * grid_b, ("block", grid_b, 1)) for i in range(0, frames, 2)]
    else:
        groups += [(base + i * grid_b, grid_b, None) for i in range(frames)]
    return tuple(groups)


def per_device(
    sizes,
    frames_a,
    frames_b,
    actions_a,
    actions_b,
    action_table,
    gain_space,
    space_qkv,
    space_out,
    gain_time,
    time_qkv,
    time_out,
    gain_ffn,
    ffn_up,
    ffn_down,
    cot_a,
    cot_b,
):
    moves = Moves(sizes)
    n_wide = sizes["wide"]
    _, n_frames, grid_a, depth = frames_a.shape
    grid_b = frames_b.shape[2]
    rows_a, rows_b = n_frames * grid_a, n_frames * grid_b
    rows = rows_a + rows_b
    spots_a, spots_b = grid_a // n_wide, grid_b // n_wide
    spots = spots_a + spots_b
    all_frames = n_frames * n_wide
    inner = 8 if spots % 8 == 0 else 4
    gain_space, gain_time, gain_ffn = (g[None] for g in (gain_space, gain_time, gain_ffn))

    def exchange(packed):
        return lax.all_to_all(packed, "wide", split_axis=0, concat_axis=0, tiled=True)

    def pack_grid(first, second):
        first = first.reshape(n_frames, n_wide, spots_a, depth)
        second = second.reshape(n_frames, n_wide, spots_b, depth)
        return jnp.concatenate([first, second], 2).transpose(1, 0, 2, 3)

    def unpack_grid(moved):
        moved = moved.reshape(all_frames, spots // inner, inner, depth)
        return moved.transpose(1, 0, 2, 3).reshape(rows, depth)

    def pack_frames(rows_in):
        packed = rows_in.reshape(spots // inner, n_wide, n_frames, inner, depth)
        return packed.transpose(1, 2, 0, 3, 4).reshape(n_wide, n_frames, spots, depth)

    def unpack_frames(moved):
        first = moved[:, :, :spots_a].transpose(1, 0, 2, 3).reshape(rows_a, depth)
        second = moved[:, :, spots_a:].transpose(1, 0, 2, 3).reshape(rows_b, depth)
        return jnp.concatenate([first, second])

    def both_clips(mine, partner):
        low = moves.tp == 0
        pair = jnp.stack([jnp.where(low, mine, partner), jnp.where(low, partner, mine)])
        return (
            pair[:, :rows_a].reshape(2, n_frames, grid_a, depth),
            pair[:, rows_a:].reshape(2, n_frames, grid_b, depth),
        )

    def pick(value):
        return lax.dynamic_index_in_dim(value, moves.tp, 0, keepdims=False)

    space_groups = frame_groups(n_frames, grid_a, grid_b)
    group = inner * all_frames
    time_groups = tuple((i, group, ("causal", all_frames, inner)) for i in range(0, rows, group))
    codes = jnp.arange(action_table.shape[0])
    acts = jnp.concatenate([actions_a, actions_b], 1)
    one_hot = (acts[:, :, None] == codes).astype(F32)
    shifts = jnp.einsum("cfa,ad->cfd", one_hot, action_table.astype(F32), precision=lax.Precision.HIGHEST)

    clip = moves.tp[None].astype(jnp.int32)
    n_codes = action_table.shape[0]

    def from_x(weight, axis, *deps):
        piece = moves.quarter(weight, axis)
        return swap(after(piece, *deps) if deps else piece, "tp", sizes)

    def from_y(value, *deps):
        return swap(after(value, *deps) if deps else value, "clip", sizes)

    def cores(value, *deps):
        return swap(after(value, *deps) if deps else value, "wide", sizes)

    tokens = []

    def product(left_arrays, terms, chunk, y_first, name):
        return grad_product(moves.bits, left_arrays, terms, chunk, y_first, sizes, name)

    def both(value, *deps):
        return (value, cores(value, *deps))

    so_piece = moves.quarter(space_out, 0)
    out_piece = moves.quarter(time_out, 0)
    out_piece = out_piece.reshape(PAIR, -1, PAIR).transpose(1, 0, 2).reshape(1, -1, PAIR)
    time_piece = jnp.concatenate([moves.quarter(time_qkv, 2), out_piece])
    cot_packed = pack_grid(after(pick(cot_a), so_piece, time_piece), pick(cot_b))
    so_x = swap(so_piece, "tp", sizes)
    time_x = swap(time_piece, "tp", sizes)
    cot_moved = exchange(cot_packed)
    token = pause(tokens, so_piece, time_piece, cot_packed)
    cot_moved = after(cot_moved, token)
    (partner_heads,) = space_heads(
        after(1 - clip, token),
        frames_a, frames_b, shifts, gain_space, space_qkv, space_groups, False,
    )
    heads_other = swap(partner_heads, "tp", sizes)
    so_y = from_y(so_x, partner_heads)
    heads_own, proj_own, logs_own, started, normed_space = space_heads(
        after(clip, partner_heads), frames_a, frames_b, shifts, gain_space, space_qkv, space_groups, True
    )
    so_x, so_y = after(so_x, heads_own), after(so_y, heads_own)
    so_slots = (so_x, cores(so_x), so_y, cores(so_y))
    up_piece = moves.quarter(ffn_up, 1)
    down_piece = moves.quarter(ffn_down, 0)
    up_x = swap(after(up_piece, heads_other), "tp", sizes)
    token = pause(tokens, heads_other, up_piece, down_piece)
    middle = space_mix(moves.bits, after(started, token), heads_own, heads_other, space_out, so_slots)
    packed = pack_grid(middle[:rows_a], middle[rows_a:])
    middle_moved = exchange(after(packed, cot_moved))
    time_x = after(time_x, packed)
    time_y = swap(time_x, "clip", sizes)
    time_x_core = cores(time_x)
    token = pause(tokens, packed)

    up_x = after(up_x, token)
    up_y = swap(up_x, "clip", sizes)
    up_x_core = cores(up_x)
    down_x = swap(after(down_piece, up_x), "tp", sizes)
    token = pause(tokens, up_x)
    time_y = after(time_y, token)
    time_slots = (time_x, time_x_core, time_y, cores(time_y))
    down_x = after(down_x, token)
    down_y = swap(down_x, "clip", sizes)
    down_x_core = cores(down_x)
    sq_x = swap(after(moves.quarter(space_qkv, 2), down_x), "tp", sizes)
    token = pause(tokens, time_y, down_x)
    middle = unpack_grid(after(middle_moved, token))
    latest, normed_time, heads_time, proj_time, logs_time = time_forward(
        middle, gain_time, time_qkv, time_out, time_slots, time_groups
    )
    cot = unpack_grid(after(cot_moved, latest))
    width = ffn_up.shape[1] // 4
    normed_ffn, hidden_own, total_ffn, d_sum_ffn = feed_forward(latest, cot, gain_ffn, (ffn_up, ffn_down), width)
    up_y, down_y = after(up_y, hidden_own), after(down_y, hidden_own)
    up_slots = (up_x, up_x_core, up_y, cores(up_y))
    down_slots = (down_x, down_x_core, down_y, cores(down_y))
    out, d_latest, hidden_rest, d_gain_ffn = feed_forward(
        latest, cot, gain_ffn, (*up_slots, *down_slots), width, (normed_ffn, total_ffn, d_sum_ffn)
    )

    out_packed = pack_frames(out)
    out_moved = exchange(out_packed)
    normed_time2, heads_time2 = both(normed_time, latest), both(heads_time[:, None], latest)
    cot2, normed_ffn2, hidden2 = both(cot, latest), both(normed_ffn, latest), both(hidden_own)
    hidden_rest2 = both(hidden_rest)
    partial_time, d_proj_own = branch_back(
        "time_back", after(d_latest, out_packed), proj_time, logs_time, 0,
        (time_qkv, time_out), time_groups,
    )
    own = (both(d_proj_own), 0)
    d_latest2 = both(d_latest, partial_time)
    sq_x = after(sq_x, partial_time)
    sq_y = swap(sq_x, "clip", sizes)
    chunk = ffn_up.shape[1] // 4
    up = product(
        [(after(normed_ffn2[0], partial_time), normed_ffn2[1])],
        [(0, (hidden2, 0), (hidden_rest2, 0), 1, 1)], chunk, False, "grad_up",
    )
    up = moves.reduction(up, False)
    sq_x, sq_y = after(sq_x, up.keep), after(sq_y, up.keep, d_latest2[1])
    sq_slots = (sq_x, cores(sq_x), sq_y, cores(sq_y))
    down = product(
        [(after(cot2[0], up.keep), cot2[1])], [(0, (hidden2, 0), (hidden_rest2, 0), 0, 1)], chunk, True, "grad_down"
    )
    down = moves.reduction(down, True)
    out_rows = unpack_frames(after(out_moved, down.keep))
    out_partner = swap(out_rows, "tp", sizes)
    d_middle, d_proj_rest, d_gain_time, _ = branch_back(
        "time_back_end", d_latest, proj_time, logs_time, 2, (time_slots,), time_groups,
        (middle, gain_time, after(partial_time, out_rows)), ((0, rows),),
    )
    rest = (both(d_proj_rest), 0)
    packed = pack_frames(d_middle)
    d_middle = exchange(packed)
    gate = up.third(packed)
    time_one = product(
        [(after(normed_time, gate), normed_time2[1])], [(0, own, rest, 0, 2)], PAIR, False, "time_one"
    )
    time_one = moves.reduction(time_one, False)
    time_two = product(
        [(normed_time, normed_time2[1]), (after(d_latest, time_one.keep), d_latest2[1])],
        [(0, own, rest, 2, 1), (1, (heads_time2, 0), (heads_time2, 1), 0, 1)],
        PAIR, True, "time_two",
    )
    time_two = moves.reduction(time_two, True)
    gate = down.third(time_two.keep)
    out_a, out_b = both_clips(out_rows, after(out_partner, gate))
    heads_rest, proj_rest, logs_rest = space_rest(
        after(normed_space, gate, out_a, out_b), sq_slots, space_groups
    )
    heads_rest2 = both(heads_rest[:, None])
    heads_own2, normed_space2 = both(heads_own[:, None], heads_rest), both(normed_space, heads_rest)
    gate = time_one.third(heads_rest)
    d_middle = unpack_frames(after(d_middle, gate))
    d_middle2 = both(d_middle)
    partial_space, d_proj_own = branch_back(
        "space_back", d_middle, proj_own, logs_own, 0, (space_qkv, space_out), space_groups
    )
    own = (both(d_proj_own), 0)
    ffn, time = Pair(moves, up, down), Pair(moves, time_one, time_two)
    gates = [time_two.third(partial_space)]
    gates += [up.sum(gates[0]), down.sum(gates[0])]
    ffn.fourth()
    token = pause(tokens, *gates)
    segments = tuple((i * grid_a, grid_a) for i in range(n_frames)) + tuple(
        (rows_a + i * grid_b, grid_b) for i in range(n_frames)
    )
    d_started, d_proj_rest, d_gain_space, frame_sums = branch_back(
        "space_back_end", d_middle, proj_rest, logs_rest, 0, (sq_slots, so_slots), space_groups,
        (started, gain_space, after(partial_space, token)), segments, True,
    )
    rest = (both(d_proj_rest), 0)
    started_partner = swap(d_started, "tp", sizes)
    d_table = jnp.einsum(
        "fa,fd->ad", pick(one_hot), frame_sums[: 2 * n_frames], precision=lax.Precision.HIGHEST
    )
    small, small_other = moves.small_first(jnp.concatenate([d_table, d_gain_space, d_gain_time, d_gain_ffn]))
    gates = [time_one.sum(d_started), time_two.sum(d_started)]
    time.fourth()
    space_two = product(
        [(after(normed_space, small, *gates), normed_space2[1]), d_middle2],
        [(0, own, rest, 2, 1), (1, (heads_own2, 0), (heads_rest2, 0), 0, 1)],
        PAIR, True, "space_two",
    )
    space_two = moves.reduction(space_two, True)
    small = small + after(small_other, space_two.keep)
    small_other = swap(small, "tp", sizes)
    space_one = product(
        [(after(normed_space, space_two.keep, small), normed_space2[1])], [(0, own, rest, 0, 2)], PAIR, False, "space_one"
    )
    space_one = moves.reduction(space_one, False)
    token = pause(tokens, space_one.keep)
    small = small + after(small_other, token)
    small_other = small
    step = 1
    while step < sizes["clip"]:
        small_other = swap(small, "clip", sizes, step)
        if 2 * step < sizes["clip"]:
            small = small + small_other
        step *= 2
    d_frames_a, d_frames_b = both_clips(d_started, after(started_partner, small))
    gate = space_two.third(d_frames_a, d_frames_b)
    gate2 = space_one.third(gate)
    gate3 = ffn.fifth(gate2)
    token = pause(tokens, gate, gate2, gate3)
    small = small + after(small_other, token)
    gates = [space_two.sum(token), space_one.sum(token)]
    space = Pair(moves, space_one, space_two)
    space.fourth()
    small = moves.small_last(after(small, *gates))
    gates += [time.fifth(gates[1])]
    token = pause(tokens, *gates)
    gate = space.fifth(token)
    token = pause(tokens, gate)
    ffn.arrived, time.arrived = after(ffn.arrived, gates[0]), after(time.arrived, token)
    space.arrived = after(space.arrived, token)

    small = small + sum(tokens)[:1, :1]

    def qkv(pair):
        return jnp.stack([pair.halves(0, 0, 2), pair.halves(0, 1, 2), pair.halves(1, 0, 2)])

    return (
        out_a,
        out_b,
        d_frames_a,
        d_frames_b,
        small[:n_codes],
        small[n_codes],
        qkv(space),
        space.halves(1, 1, 2).T,
        small[n_codes + 1],
        qkv(time),
        time.halves(1, 1, 2).T,
        small[n_codes + 2],
        ffn.halves(0, 0, 1),
        ffn.halves(1, 0, 1).T,
    )


def solution(mesh):
    sizes = dict(mesh.shape)
    return jax.shard_map(
        partial(per_device, sizes),
        mesh=mesh,
        in_specs=(
            P("clip", "wide", None, None),
            P("clip", "wide", None, None),
            P("clip", "wide"),
            P("clip", "wide"),
            P(),
            P(),
            P(None, None, "tp"),
            P("tp", None),
            P(),
            P(None, None, "tp"),
            P("tp", None),
            P(),
            P(None, "tp"),
            P("tp", None),
            P("clip", "wide", None, None),
            P("clip", "wide", None, None),
        ),
        out_specs=(
            P("clip", "wide", None, None),
            P("clip", "wide", None, None),
            P("clip", "wide", None, None),
            P("clip", "wide", None, None),
            P(None, "wide"),
            P("wide"),
            P(None, "wide", "tp"),
            P("tp", "wide"),
            P("wide"),
            P(None, "wide", "tp"),
            P("tp", "wide"),
            P("wide"),
            P("wide", "tp"),
            P("tp", "wide"),
        ),
        check_vma=False,
    )
```

```python
from functools import partial

import jax
import jax.numpy as jnp
from jax import lax
from jax.experimental import pallas as pl
from jax.experimental.pallas import tpu as pltpu
from jax.sharding import PartitionSpec as P

HEAD = 64
PAIR = 2 * HEAD
BLOCK = 2 * PAIR
BATCH = 2**30
BF = jnp.bfloat16
F32 = jnp.float32
LIMIT = 60 * 2**20


def dot_n(a, b):
    return lax.dot_general(a, b, (((1,), (0,)), ((), ())), preferred_element_type=F32)


def dot_t(a, b):
    return lax.dot_general(a, b, (((1,), (1,)), ((), ())), preferred_element_type=F32)


def shape_of(*dims, dtype=BF):
    return jax.ShapeDtypeStruct(dims, dtype)


def whole(*dims):
    return pl.BlockSpec(dims, lambda *_: (0,) * len(dims))


def any_spec():
    return pl.BlockSpec(memory_space=pl.ANY)


def params():
    return pltpu.CompilerParams(vmem_limit_bytes=LIMIT)


MICROS = {'space_partner': 8, 'space_own': 8, 'space_mix': 8, 'space_rest': 1.031, 'time_forward': 44.8106, 'feed_forward': 15.1219, 'time_back': 11.3339, 'time_back_end': 0.852, 'space_back': 6.0811, 'space_back_end': 30.4331, 'grad_up': 12.841, 'grad_down': 0.5749, 'time_one': 0.1151, 'time_two': 0.6269, 'space_two': 0.3517, 'space_one': 1.624, 'pause0': 1, 'pause1': 0.02, 'pause2': 12, 'pause3': 5.3533, 'pause4': 12, 'pause5': 5.9164, 'pause6': 3.5109, 'pause7': 2.6464, 'pause8': 12.3069, 'pause9': 160.0718, 'pause10': 0.8432, 'feed_forward_end': 15.1219}


def cost(name):
    return pl.CostEstimate(flops=int(MICROS[name] * 1e9), bytes_accessed=2**20, transcendentals=0)


def group_mask(kind, length):
    if kind is None:
        return None
    name, size, inner = kind
    key = lax.broadcasted_iota(jnp.int32, (length, length), 0)
    query = lax.broadcasted_iota(jnp.int32, (length, length), 1)
    if name == "block":
        shift = size.bit_length() - 1
        return (query >> shift) == (key >> shift)
    shift = inner.bit_length() - 1
    return ((query & (inner - 1)) == (key & (inner - 1))) & ((key >> shift) <= (query >> shift))


def head_masks(value):
    lane = lax.broadcasted_iota(jnp.int32, (1, PAIR), 1)
    return (
        jnp.where(lane < HEAD, value, 0.0).astype(BF),
        jnp.where(lane < HEAD, 0.0, value).astype(BF),
    )


def batches(groups):
    result, area = [], 0
    for group in groups:
        size = group[1] * group[1]
        if result and area + size <= BATCH:
            result[-1].append(group)
            area += size
        else:
            result.append([group])
            area = size
    return result


def attend_block(groups, proj_ref, heads_ref, logs_ref):
    scaled = head_masks(HEAD**-0.5)
    masks = {kind: group_mask(kind, length) for _, length, kind in groups}
    for batch in batches([(*group, pair) for pair in range(2) for group in groups]):
        if True:
            places = [slice(start, start + length) for start, length, _, _ in batch]
            spots = [slice(group[3] * PAIR, (group[3] + 1) * PAIR) for group in batch]
            items = [(g, h) for g in range(len(batch)) for h in range(2)]
            scores = [
                dot_t(proj_ref[1, places[g], spots[g]] * scaled[h], proj_ref[0, places[g], spots[g]]) for g, h in items
            ]
            scores = [
                scores[n] if batch[g][2] is None else jnp.where(masks[batch[g][2]], scores[n], -1e30)
                for n, (g, h) in enumerate(items)
            ]
            largest = [jnp.max(v, 0, keepdims=True) for v in scores]
            shifted = [jnp.exp(v - m) for v, m in zip(scores, largest)]
            totals = [jnp.sum(v, 0, keepdims=True) for v in shifted]
            values_t = [proj_ref[2, rows, cols].T for rows, cols in zip(places, spots)]
            outs = [
                dot_n(values_t[g][h * HEAD : (h + 1) * HEAD], shifted[n].astype(BF)) * (1.0 / totals[n])
                for n, (g, h) in enumerate(items)
            ]
            for n, (g, h) in enumerate(items):
                if logs_ref is not None:
                    logs_ref[2 * batch[g][3] + h : 2 * batch[g][3] + h + 1, places[g]] = largest[n] + jnp.log(totals[n])
            for g, (rows, cols) in enumerate(zip(places, spots)):
                heads_ref[rows, cols] = jnp.concatenate(outs[2 * g : 2 * g + 2], 0).T.astype(BF)


def attend_back_block(groups, proj_ref, d_ref, logs_ref, o_ref):
    scale = HEAD**-0.5
    scaled = head_masks(scale)
    parts = head_masks(1.0)
    masks = {kind: group_mask(kind, length) for _, length, kind in groups}
    for batch in batches([(*group, pair) for pair in range(2) for group in groups]):
        if True:
            places = [slice(start, start + length) for start, length, _, _ in batch]
            spots = [slice(group[3] * PAIR, (group[3] + 1) * PAIR) for group in batch]
            items = [(g, h) for g in range(len(batch)) for h in range(2)]
            scores = [
                dot_t(proj_ref[1, places[g], spots[g]] * scaled[h], proj_ref[0, places[g], spots[g]]) for g, h in items
            ]
            d_soft = [dot_t(proj_ref[2, places[g], spots[g]] * parts[h], d_ref[places[g], spots[g]]) for g, h in items]
            soft = [
                jnp.exp(scores[n] - logs_ref[2 * batch[g][3] + h : 2 * batch[g][3] + h + 1, places[g]])
                for n, (g, h) in enumerate(items)
            ]
            soft = [
                soft[n] if batch[g][2] is None else jnp.where(masks[batch[g][2]], soft[n], 0.0)
                for n, (g, h) in enumerate(items)
            ]
            row_dots = [jnp.sum(p * d, 0, keepdims=True) for p, d in zip(soft, d_soft)]
            d_scores = [(p * (d - r)).astype(BF) for p, d, r in zip(soft, d_soft, row_dots)]
            soft = [p.astype(BF) for p in soft]
            keys_t = [proj_ref[1, rows, cols].T for rows, cols in zip(places, spots)]
            d_query = [
                dot_n(keys_t[g][h * HEAD : (h + 1) * HEAD], d_scores[n]) for n, (g, h) in enumerate(items)
            ]
            d_key = [dot_n(d_scores[n], proj_ref[0, places[g], spots[g]] * parts[h]) for n, (g, h) in enumerate(items)]
            d_value = [dot_n(soft[n], d_ref[places[g], spots[g]] * parts[h]) for n, (g, h) in enumerate(items)]
            for g, (rows, cols) in enumerate(zip(places, spots)):
                o_ref[0, rows, cols] = (jnp.concatenate(d_query[2 * g : 2 * g + 2], 0).T * scale).astype(BF)
                o_ref[1, rows, cols] = ((d_key[2 * g] + d_key[2 * g + 1]) * scale).astype(BF)
                o_ref[2, rows, cols] = (d_value[2 * g] + d_value[2 * g + 1]).astype(BF)


def row_chunks(rows, size=64):
    return [slice(i, i + size) for i in range(0, rows, size)]


def norm_parts(values):
    centered = values - jnp.mean(values, -1, keepdims=True)
    inverse = lax.rsqrt(jnp.mean(centered * centered, -1, keepdims=True) + 1e-05)
    return centered * inverse, inverse


def project_block(normed_ref, weight, proj_ref):
    for i in range(3):
        proj_ref[i] = dot_n(normed_ref[...], weight(i)).astype(BF)


def space_kernel(groups, full, _, fa_ref, fb_ref, shift_ref, gain_ref, w_ref, *refs):
    if full:
        heads_ref, proj_ref, logs_ref, started_ref, normed_ref = refs
        proj, logs = proj_ref.at[0], logs_ref.at[0]
    else:
        heads_ref, proj, normed_ref = refs
        logs = None
    _, frames, grid_a, _ = fa_ref.shape
    grid_b = fb_ref.shape[2]

    @pl.when(pl.program_id(0) == 0)
    def _():
        gain = gain_ref[...]
        base = 0
        for frame_ref, grid, first in ((fa_ref, grid_a, 0), (fb_ref, grid_b, frames)):
            for f in range(frames):
                move = shift_ref[0, first + f : first + f + 1, :]
                for rows in row_chunks(grid):
                    values = frame_ref[0, f, rows, :].astype(F32) + move
                    out = slice(base + rows.start, base + rows.stop)
                    if full:
                        started_ref[out, :] = values
                    normed_ref[out, :] = (norm_parts(values)[0] * gain).astype(BF)
                base += grid

    project_block(normed_ref, lambda i: w_ref[i], proj)
    attend_block(groups, proj, heads_ref.at[0], logs)


def space_heads(clip, frames_a, frames_b, shifts, gain, qkv, groups, full):
    _, frames, grid_a, depth = frames_a.shape
    grid_b = frames_b.shape[2]
    rows = frames * (grid_a + grid_b)
    blocks = qkv.shape[2] // BLOCK

    def chosen(*dims):
        return pl.BlockSpec((1, *dims), lambda s, c: (c[0],) + (0,) * len(dims))

    heads = (pl.BlockSpec((1, rows, BLOCK), lambda s, c: (s, 0, 0)), shape_of(blocks, rows, BLOCK))
    if full:
        outs = [
            heads,
            (pl.BlockSpec((1, 3, rows, BLOCK), lambda s, c: (s, 0, 0, 0)), shape_of(blocks, 3, rows, BLOCK)),
            (pl.BlockSpec((1, 8, rows), lambda s, c: (s, 0, 0)), shape_of(blocks, 8, rows, dtype=F32)),
            (whole(rows, depth), shape_of(rows, depth, dtype=F32)),
            (whole(rows, depth), shape_of(rows, depth)),
        ]
        scratch = []
    else:
        outs = [heads]
        scratch = [pltpu.VMEM((3, rows, BLOCK), BF), pltpu.VMEM((rows, depth), BF)]
    return pl.pallas_call(
        partial(space_kernel, groups, full),
        grid_spec=pltpu.PrefetchScalarGridSpec(
            num_scalar_prefetch=1,
            grid=(blocks,),
            in_specs=[
                chosen(frames, grid_a, depth),
                chosen(frames, grid_b, depth),
                chosen(2 * frames, depth),
                whole(1, depth),
                pl.BlockSpec((3, depth, BLOCK), lambda s, c: (0, 0, s)),
            ],
            out_specs=[o[0] for o in outs],
            scratch_shapes=scratch,
        ),
        out_shape=[o[1] for o in outs],
        compiler_params=params(),
        cost_estimate=cost("space_own" if full else "space_partner"),
        name="space_own" if full else "space_partner",
    )(clip, frames_a, frames_b, shifts, gain, qkv)


def stream_weights(own_qkv, own_out, qkv_slots, out_slots, wq, wo, sems, step, steps, first=0):
    def out_at(slot, index):
        return slot if wo.shape[0] == 2 else index

    def start(index, slot):
        for s in range(steps):

            @pl.when(index == s)
            def _(s=s):
                if s + first < 2:
                    cols = pl.ds((s + first) * BLOCK, BLOCK)
                    pltpu.make_async_copy(own_qkv.at[:, :, cols], wq.at[slot], sems.at[slot, 0]).start()
                    if wo is not None:
                        pltpu.make_async_copy(own_out.at[cols, :], wo.at[out_at(slot, s)], sems.at[slot, 1]).start()
                else:
                    for i in range(2):
                        part = 2 * (s + first - 2) + i
                        cols = pl.ds(i * PAIR, PAIR)
                        pltpu.make_async_copy(
                            qkv_slots[part].at[0:3], wq.at[slot, :, :, cols], sems.at[slot, 0]
                        ).start()
                        if wo is None:
                            continue
                        if out_slots is not None:
                            pltpu.make_async_copy(
                                out_slots[part], wo.at[out_at(slot, s), cols, :], sems.at[slot, 1]
                            ).start()
                            continue
                        for j in range(wo.shape[2] // PAIR):
                            place = pl.ds(j * PAIR, PAIR)
                            pltpu.make_async_copy(
                                qkv_slots[part].at[3, place, :], wo.at[out_at(slot, s), cols, place], sems.at[slot, 1]
                            ).start()

    slot = step % 2

    @pl.when(step == 0)
    def _():
        start(step, slot)

    @pl.when(step + 1 < steps)
    def _():
        start(step + 1, 1 - slot)

    pltpu.make_async_copy(wq.at[slot], wq.at[slot], sems.at[slot, 0]).wait()
    if wo is not None:
        pltpu.make_async_copy(wo.at[0], wo.at[0], sems.at[slot, 1]).wait()
    return slot


def rest_kernel(groups, normed_ref, q0, q1, q2, q3, heads_ref, proj_ref, logs_ref, wq, sems):
    slot = stream_weights(None, None, (q0, q1, q2, q3), None, wq, None, sems, pl.program_id(0), 2, 2)
    project_block(normed_ref, lambda i: wq[slot, i], proj_ref.at[0])
    attend_block(groups, proj_ref.at[0], heads_ref.at[0], logs_ref.at[0])


def space_rest(normed, qkv_slots, groups):
    rows, depth = normed.shape
    return pl.pallas_call(
        partial(rest_kernel, groups),
        grid=(2,),
        in_specs=[whole(rows, depth)] + [any_spec()] * 4,
        out_specs=[
            pl.BlockSpec((1, rows, BLOCK), lambda s: (s, 0, 0)),
            pl.BlockSpec((1, 3, rows, BLOCK), lambda s: (s, 0, 0, 0)),
            pl.BlockSpec((1, 8, rows), lambda s: (s, 0, 0)),
        ],
        out_shape=[
            shape_of(2, rows, BLOCK),
            shape_of(2, 3, rows, BLOCK),
            shape_of(2, 8, rows, dtype=F32),
        ],
        scratch_shapes=[pltpu.VMEM((2, 3, depth, BLOCK), BF), pltpu.SemaphoreType.DMA((2, 2))],
        compiler_params=params(),
        cost_estimate=cost("space_rest"),
        name="space_rest",
    )(normed, *qkv_slots)


def out_kernel(bits_ref, stream_ref, own_ref, other_ref, w_ref, o0, o1, o2, o3, mid_ref, assembled):
    clip_bit, core_bit = bits_ref[0], bits_ref[1]
    for i, piece in enumerate((o0, o1, o2, o3)):
        place = 2 * (clip_bit if i < 2 else 1 - clip_bit) + (core_bit if i % 2 == 0 else 1 - core_bit)
        assembled[pl.ds(pl.multiple_of(place * PAIR, PAIR), PAIR), :] = piece[...]
    total = stream_ref[...]
    for b in range(own_ref.shape[0]):
        cols = slice(b * BLOCK, (b + 1) * BLOCK)
        total = total + dot_n(own_ref[b], w_ref[cols, :]) + dot_n(other_ref[b], assembled[cols, :])
    mid_ref[...] = total.astype(BF)


def space_mix(bits, started, own, other, weight, out_slots):
    rows, depth = started.shape
    half = weight.shape[0]
    return pl.pallas_call(
        out_kernel,
        grid_spec=pltpu.PrefetchScalarGridSpec(
            num_scalar_prefetch=1,
            grid=(1,),
            in_specs=[whole(rows, depth), whole(*own.shape), whole(*other.shape), whole(half, depth)]
            + [whole(half // 4, depth)] * 4,
            out_specs=whole(rows, depth),
            scratch_shapes=[pltpu.VMEM((half, depth), BF)],
        ),
        out_shape=shape_of(rows, depth),
        compiler_params=params(),
        cost_estimate=cost("space_mix"),
        name="space_mix",
    )(bits, started, own, other, weight, *out_slots)


def time_kernel(groups, mid_ref, gain_ref, wq_any, wo_any, q0, q1, q2, q3,
                late_ref, normed_ref, heads_ref, proj_ref, logs_ref, acc, wq, wo, sems, joined):
    step = pl.program_id(0)
    rows = mid_ref.shape[0]

    @pl.when(step == 0)
    def _():
        gain = gain_ref[...]
        for chunk in row_chunks(rows):
            values = mid_ref[chunk, :].astype(F32)
            acc[chunk, :] = values
            normed_ref[chunk, :] = (norm_parts(values)[0] * gain).astype(BF)

    slot = stream_weights(wq_any, wo_any, (q0, q1, q2, q3), None, wq, wo, sems, step, 4)
    project_block(normed_ref, lambda i: wq[slot, i], proj_ref.at[0])
    attend_block(groups, proj_ref.at[0], heads_ref.at[0], logs_ref.at[0])
    for s in range(4):

        @pl.when(step == s)
        def _(s=s):
            joined[:, s * BLOCK : (s + 1) * BLOCK] = heads_ref[0]

    @pl.when(step == 3)
    def _():
        weight = wo[...].reshape(4 * BLOCK, wo.shape[2])
        late_ref[...] = (acc[...] + dot_n(joined[...], weight)).astype(BF)


def time_forward(middle, gain, qkv, out, slots, groups):
    rows, depth = middle.shape
    return pl.pallas_call(
        partial(time_kernel, groups),
        grid=(4,),
        in_specs=[whole(rows, depth), whole(1, depth)] + [any_spec()] * 6,
        out_specs=[
            whole(rows, depth),
            whole(rows, depth),
            pl.BlockSpec((1, rows, BLOCK), lambda s: (s, 0, 0)),
            pl.BlockSpec((1, 3, rows, BLOCK), lambda s: (s, 0, 0, 0)),
            pl.BlockSpec((1, 8, rows), lambda s: (s, 0, 0)),
        ],
        out_shape=[
            shape_of(rows, depth),
            shape_of(rows, depth),
            shape_of(4, rows, BLOCK),
            shape_of(4, 3, rows, BLOCK),
            shape_of(4, 8, rows, dtype=F32),
        ],
        scratch_shapes=[
            pltpu.VMEM((rows, depth), F32),
            pltpu.VMEM((2, 3, depth, BLOCK), BF),
            pltpu.VMEM((4, BLOCK, depth), BF),
            pltpu.SemaphoreType.DMA((2, 2)),
            pltpu.VMEM((rows, 4 * BLOCK), BF),
        ],
        compiler_params=params(),
        cost_estimate=cost("time_forward"),
        name="time_forward",
    )(middle, gain, qkv, out, *slots)


def gelu_parts(hidden):
    root = 0.7978845608028654
    square = hidden * hidden
    curve = jnp.tanh(hidden * (root + (root * 0.044715) * square))
    half = 0.5 + 0.5 * curve
    slope = half + hidden * (half * (1.0 - curve)) * (root + (3 * 0.044715 * root) * square)
    return hidden * half, slope


def norm_back_rows(values, gain, d_normed):
    normal, inverse = norm_parts(values)
    scaled = d_normed * gain
    mean_first = jnp.mean(scaled, -1, keepdims=True)
    mean_second = jnp.mean(scaled * normal, -1, keepdims=True)
    return (scaled - mean_first - normal * mean_second) * inverse, d_normed * normal


def ffn_kernel(final, late_ref, cot_ref, gain_ref, *refs):
    if final:
        normed_ref, total_in, d_normed_in, u0, u1, u2, u3, d0, d1, d2, d3 = refs[:11]
        out_ref, d_late_ref, hidden_ref, d_gain_ref, total, d_normed, wu, wd, sems = refs[11:]
    else:
        up_any, down_any, normed_ref, hidden_ref, total, d_normed, wu, wd, sems = refs
    step = pl.program_id(0)
    rows = late_ref.shape[0]
    width = wu.shape[2]
    steps = 4

    @pl.when(step == 0)
    def _():
        if final:
            total[...] = total_in[...]
            d_normed[...] = d_normed_in[...]
            return
        gain = gain_ref[...]
        for chunk in row_chunks(rows):
            values = late_ref[chunk, :].astype(F32)
            total[chunk, :] = values
            d_normed[chunk, :] = jnp.zeros_like(values)
            normed_ref[chunk, :] = (norm_parts(values)[0] * gain).astype(BF)

    def start(index, slot):
        for s in range(steps):

            @pl.when(index == s)
            def _(s=s):
                cols = pl.ds(s * width, width)
                up = (u0, u1, u2, u3)[s] if final else up_any.at[:, cols]
                down = (d0, d1, d2, d3)[s] if final else down_any.at[cols, :]
                pltpu.make_async_copy(up, wu.at[slot], sems.at[slot, 0]).start()
                pltpu.make_async_copy(down, wd.at[slot], sems.at[slot, 1]).start()

    slot = step % 2

    @pl.when(step == 0)
    def _():
        start(step, slot)

    @pl.when(step + 1 < steps)
    def _():
        start(step + 1, 1 - slot)

    pltpu.make_async_copy(wu.at[slot], wu.at[slot], sems.at[slot, 0]).wait()
    pltpu.make_async_copy(wd.at[slot], wd.at[slot], sems.at[slot, 1]).wait()
    for chunk in row_chunks(rows, rows):
        gelu, slope = gelu_parts(dot_n(normed_ref[chunk, :], wu[slot]))
        gelu = gelu.astype(BF)
        hidden_ref[0, 0, chunk, :] = gelu
        d_hidden = (dot_t(cot_ref[chunk, :], wd[slot]) * slope).astype(BF)
        hidden_ref[0, 1, chunk, :] = d_hidden
        total[chunk, :] += dot_n(gelu, wd[slot])
        d_normed[chunk, :] += dot_t(d_hidden, wu[slot])

    if not final:
        return

    @pl.when(step == steps - 1)
    def _():
        gain = gain_ref[...]
        d_gain = jnp.zeros_like(gain)
        for chunk in row_chunks(rows):
            out_ref[chunk, :] = total[chunk, :].astype(BF)
            back, d_gain_rows = norm_back_rows(late_ref[chunk, :].astype(F32), gain, d_normed[chunk, :])
            d_late_ref[chunk, :] = (cot_ref[chunk, :].astype(F32) + back).astype(BF)
            d_gain = d_gain + jnp.sum(d_gain_rows, 0, keepdims=True)
        d_gain_ref[...] = d_gain


def feed_forward(latest, cot, gain, weights, width, tail=None):
    rows, depth = latest.shape
    stream = (pl.BlockSpec((1, 2, rows, width), lambda s: (s, 0, 0, 0)), shape_of(4, 2, rows, width))
    plain = (whole(rows, depth), shape_of(rows, depth))
    sums = (whole(rows, depth), shape_of(rows, depth, dtype=F32))
    final = tail is not None
    if final:
        outs = [plain, plain, stream, (whole(1, depth), shape_of(1, depth, dtype=F32))]
        scratch = [pltpu.VMEM((rows, depth), F32)] * 2
    else:
        outs = [plain, stream, sums, sums]
        scratch = []
    return pl.pallas_call(
        partial(ffn_kernel, final),
        grid=(4,),
        in_specs=[whole(rows, depth), whole(rows, depth), whole(1, depth)]
        + [whole(rows, depth)] * (3 if final else 0)
        + [any_spec()] * len(weights),
        out_specs=[o[0] for o in outs],
        out_shape=[o[1] for o in outs],
        scratch_shapes=scratch
        + [
            pltpu.VMEM((2, depth, width), BF),
            pltpu.VMEM((2, width, depth), BF),
            pltpu.SemaphoreType.DMA((2, 2)),
        ],
        compiler_params=params(),
        cost_estimate=cost("feed_forward_end" if final else "feed_forward"),
        name="feed_forward_end" if final else "feed_forward",
    )(latest, cot, gain, *(tail or ()), *weights)


def back_kernel(groups, segments, sums, final, packed, offset, dy_ref, proj_any, logs_any, *refs):
    if final:
        stream_ref, gain_ref, partial_ref, q0, q1, q2, q3 = refs[:7]
        refs = refs[7:]
        out_slots = None
        if not packed:
            out_slots, refs = refs[:4], refs[4:]
        own, slots = (None, None), ((q0, q1, q2, q3), out_slots)
        d_stream_ref, d_proj_ref, d_gain_ref, sums_ref, d_normed = refs[:5]
        first = 2
    else:
        own, slots = refs[:2], (None, None)
        d_normed, d_proj_ref = refs[2:4]
        first = 0
    d_heads, proj, logs, wq, wo, sems, more = refs[-7:]
    step = pl.program_id(0)

    def start(index, slot):
        pltpu.make_async_copy(proj_any.at[index + offset], proj.at[slot], more.at[slot, 0]).start()
        pltpu.make_async_copy(logs_any.at[index + offset], logs.at[slot], more.at[slot, 1]).start()

    slot = step % 2

    @pl.when(step == 0)
    def _():
        start(step, slot)
        start(step + 1, 1 - slot)

    slot = stream_weights(*own, *slots, wq, wo, sems, step, 2, first)
    d_heads[...] = dot_t(dy_ref[...], wo[slot]).astype(BF)
    pltpu.make_async_copy(proj.at[slot], proj.at[slot], more.at[slot, 0]).wait()
    pltpu.make_async_copy(logs.at[slot], logs.at[slot], more.at[slot, 1]).wait()
    attend_back_block(groups, proj.at[slot], d_heads, logs.at[slot], d_proj_ref.at[0])
    term = (
        dot_t(d_proj_ref[0, 0], wq[slot, 0])
        + dot_t(d_proj_ref[0, 1], wq[slot, 1])
        + dot_t(d_proj_ref[0, 2], wq[slot, 2])
    )

    @pl.when(step == 0)
    def _():
        d_normed[...] = term + partial_ref[...] if final else term

    @pl.when(step > 0)
    def _():
        d_normed[...] += term

    if not final:
        return

    @pl.when(step == 1)
    def _():
        gain = gain_ref[...]
        d_gain = jnp.zeros_like(gain)
        for index, (begin, count) in enumerate(segments):
            summed = jnp.zeros_like(gain)
            for piece in row_chunks(count):
                chunk = slice(begin + piece.start, begin + piece.stop)
                back, d_gain_rows = norm_back_rows(stream_ref[chunk, :].astype(F32), gain, d_normed[chunk, :])
                d_values = dy_ref[chunk, :].astype(F32) + back
                d_stream_ref[chunk, :] = d_values.astype(BF)
                d_gain = d_gain + jnp.sum(d_gain_rows, 0, keepdims=True)
                if sums:
                    summed = summed + jnp.sum(d_values, 0, keepdims=True)
            if sums:
                sums_ref[index : index + 1, :] = summed
        d_gain_ref[...] = d_gain
        if not sums:
            sums_ref[...] = jnp.zeros_like(sums_ref)


def branch_back(name, dy, proj, logs, offset, weights, groups, tail=None, segments=(), sums=False):
    rows, depth = dy.shape
    final = tail is not None
    if final:
        slots = [piece for group in weights for piece in group]
        others = [*tail, *slots]
        specs = [whole(rows, depth), whole(1, depth), whole(rows, depth)] + [any_spec()] * len(slots)
        outs = [
            (whole(rows, depth), shape_of(rows, depth)),
            (pl.BlockSpec((1, 3, rows, BLOCK), lambda s: (s, 0, 0, 0)), shape_of(2, 3, rows, BLOCK)),
            (whole(1, depth), shape_of(1, depth, dtype=F32)),
            (whole(8, depth), shape_of(8, depth, dtype=F32)),
        ]
        scratch = [pltpu.VMEM((rows, depth), F32)]
    else:
        others = list(weights)
        specs = [any_spec()] * 2
        outs = [
            (whole(rows, depth), shape_of(rows, depth, dtype=F32)),
            (pl.BlockSpec((1, 3, rows, BLOCK), lambda s: (s, 0, 0, 0)), shape_of(2, 3, rows, BLOCK)),
        ]
        scratch = []
    return pl.pallas_call(
        partial(back_kernel, groups, segments, sums, final, len(weights) == 1, offset),
        grid=(2,),
        in_specs=[whole(rows, depth), any_spec(), any_spec()] + specs,
        out_specs=[o[0] for o in outs],
        out_shape=[o[1] for o in outs],
        scratch_shapes=scratch
        + [
            pltpu.VMEM((rows, BLOCK), BF),
            pltpu.VMEM((2, 3, rows, BLOCK), BF),
            pltpu.VMEM((2, 8, rows), F32),
            pltpu.VMEM((2, 3, depth, BLOCK), BF),
            pltpu.VMEM((2, BLOCK, depth), BF),
            pltpu.SemaphoreType.DMA((2, 2)),
            pltpu.SemaphoreType.DMA((2, 2)),
        ],
        compiler_params=params(),
        cost_estimate=cost(name),
        name=name,
    )(dy, proj, logs, *others)


def grad_kernel(chunk, y_first, lefts, bits_ref, *refs):
    count = len(lefts)
    n_left = max(lefts) + 1
    left_refs, refs = refs[: 2 * n_left], refs[2 * n_left :]
    own_refs, other_refs = refs[: 2 * count], refs[2 * count : 4 * count]
    keep_ref, leave_ref, turned = refs[4 * count :]
    step = pl.program_id(0)
    core_bit, z_index = bits_ref[1], bits_ref[2]
    _, stacks, cut, _ = keep_ref.shape
    rows = left_refs[0].shape[0]

    @pl.when(step == 0)
    def _():
        for n, left_ref in enumerate(left_refs):
            columns = slice(n % 2 * rows, (n % 2 + 1) * rows)
            for j in range(stacks):
                place = slice(j * cut, (j + 1) * cut)
                start = pl.multiple_of((z_index ^ j) * 2 * cut, 2 * cut)
                if cut % 128 == 0:
                    start = pl.multiple_of(start + core_bit * cut, cut)
                    turned[n // 2, place, columns] = left_ref[:, pl.ds(start, cut)].T
                    continue
                both = left_ref[:, pl.ds(start, 2 * cut)].T
                for core in range(2):

                    @pl.when(core_bit == core)
                    def _(core=core, both=both, place=place, n=n, columns=columns):
                        turned[n // 2, place, columns] = both[core * cut : (core + 1) * cut]

    def fill(half, out_ref):
        matrix = 0
        for term, n in enumerate(lefts):
            mine_ref, partner_ref = (own_refs if half == 0 else other_refs)[2 * term : 2 * term + 2]
            blocks, parts, _, span = mine_ref.shape
            for t in range(parts):
                for b in range(blocks):
                    mine = mine_ref[b, t]
                    if half == 0:
                        partner = partner_ref[b, t]
                    elif span == chunk:
                        partner = partner_ref[1 - b, t]
                    else:
                        partner = partner_ref[b, t]
                        partner = jnp.concatenate([partner[:, chunk:], partner[:, :chunk]], 1)
                    block = dot_n(turned[n], jnp.concatenate([mine, partner], 0)).astype(BF)
                    for i in range(span // chunk):
                        index = b * (span // chunk) + i
                        if half == 1:
                            index = index ^ core_bit
                        lanes = pl.ds(pl.multiple_of((2 * matrix + index) * chunk, chunk), chunk)
                        for j in range(stacks):
                            out_ref[0, j, :, lanes] = block[
                                j * cut : (j + 1) * cut, i * chunk : (i + 1) * chunk
                            ]
                matrix += 1

    for g in range(4):

        @pl.when(step == g)
        def _(g=g):
            first, second = 1 - g // 2, g % 2
            fill(second if y_first else first, leave_ref if first == 1 else keep_ref)


def grad_product(bits, left_arrays, terms, chunk, y_first, sizes, name):
    rows, depth = left_arrays[0][0].shape
    stacks = sizes["wide"] // 2
    cut = depth // sizes["wide"]
    columns = 2 * sum(term[4] for term in terms) * chunk

    def flip(g, half):
        if y_first:
            return 1 - g // 2
        return jnp.where(1 - g // 2 == half, g % 2, 1 - half)

    def half_spec(value, half, first_part, parts):
        arrays, at = value
        shape = arrays[0].shape
        lead = 2 * chunk // shape[3]

        def index(g, b):
            y = flip(g, half)
            return (2 * at + ((b[0] ^ y) if half == 0 else y), first_part // parts, 0, 0)

        return [pl.BlockSpec((lead, parts, *shape[2:]), index)] * 2

    block = (1, stacks, cut, columns)
    return pl.pallas_call(
        partial(grad_kernel, chunk, y_first, [term[0] for term in terms]),
        grid_spec=pltpu.PrefetchScalarGridSpec(
            num_scalar_prefetch=1,
            grid=(4,),
            in_specs=[whole(rows, depth)] * (2 * len(left_arrays))
            + [spec for term in terms for spec in half_spec(term[1], 0, *term[3:])]
            + [spec for term in terms for spec in half_spec(term[2], 1, *term[3:])],
            out_specs=[
                pl.BlockSpec(block, lambda g, b: (jnp.maximum(g - 2, 0), 0, 0, 0)),
                pl.BlockSpec(block, lambda g, b: (jnp.minimum(g, 1), 0, 0, 0)),
            ],
            scratch_shapes=[pltpu.VMEM((len(left_arrays), stacks * cut, 2 * rows), BF)],
        ),
        out_shape=[shape_of(2, stacks, cut, columns)] * 2,
        compiler_params=params(),
        cost_estimate=cost(name),
        name="grad_product",
    )(
        bits,
        *[array for pair in left_arrays for array in pair],
        *[array for term in terms for array in term[1][0]],
        *[array for term in terms for array in term[2][0]],
    )


def swap(value, axis, sizes, step=1):
    return lax.ppermute(value, axis, [(i, i ^ step) for i in range(sizes[axis])])


def after(value, *others):
    return lax.optimization_barrier((value, *others))[0]


def pause_kernel(x_ref, o_ref):
    o_ref[...] = x_ref[...]


def pause(tokens, *deps):
    token = after(jnp.zeros((8, 128), F32), *deps)
    tokens.append(pl.pallas_call(
        pause_kernel,
        out_shape=shape_of(8, 128, dtype=F32),
        cost_estimate=cost("pause%d" % len(tokens)),
        name="pause",
    )(token))
    return tokens[-1]


def wide(value):
    return value.astype(F32)


class Moves:
    def __init__(self, sizes):
        self.sizes = sizes
        self.tp = lax.axis_index("tp")
        self.clip = lax.axis_index("clip")
        self.clip_bit = self.clip % 2
        place = lax.axis_index("wide")
        self.core_bit = place % 2
        self.z = place // 2
        self.bits = jnp.stack([self.clip_bit, self.core_bit, self.z]).astype(jnp.int32)

    def quarter(self, weight, axis):
        size = weight.shape[axis] // 4
        return lax.dynamic_slice_in_dim(weight, (2 * self.clip_bit + self.core_bit) * size, size, axis)

    def spread(self, from_x):
        from_y = swap(from_x, "clip", self.sizes)
        return (from_x, swap(from_x, "wide", self.sizes), from_y, swap(from_y, "wide", self.sizes))

    def spread_core(self, from_x, from_y):
        return (from_x, swap(from_x, "wide", self.sizes), from_y, swap(from_y, "wide", self.sizes))

    def reduction(self, product, y_first):
        return Reduction(self, *product, y_first)

    def take(self, value, index, axis):
        return lax.dynamic_index_in_dim(value, index, axis, keepdims=False)

    def small_first(self, rows):
        count, depth = rows.shape
        wide_size = self.sizes["wide"]
        blocks = rows.reshape(count, wide_size // 2, 2, depth // wide_size).transpose(1, 2, 0, 3)
        other = swap(self.take(blocks, 1 - self.core_bit, 1), "wide", self.sizes)
        return self.take(blocks, self.core_bit, 1), other

    def small_last(self, total):
        result = self.take(total, self.z, 0)
        for j in range(1, self.sizes["wide"] // 2):
            result = result + swap(self.take(total, self.z ^ j, 0), "wide", self.sizes, 2 * j)
        return result


class Reduction:
    def __init__(self, moves, keep, leaving, y_first):
        self.moves, self.sizes, self.keep = moves, moves.sizes, keep
        self.axes = ("clip", "tp") if y_first else ("tp", "clip")
        self.leaving = leaving
        self.arrived = swap(leaving, self.axes[0], self.sizes)

    def third(self, *deps):
        keep = after(self.keep, *deps) if deps else self.keep
        total = wide(keep) + wide(self.arrived)
        self.leaving = total[1].astype(BF)
        self.mine = total[0].astype(BF)
        self.arrived = swap(self.leaving, self.axes[1], self.sizes)
        return self.leaving

    def sum(self, *deps):
        if deps:
            self.mine = after(self.mine, *deps)
        total = wide(self.mine) + wide(self.arrived)
        step = 2
        while step < self.sizes["clip"]:
            total = total + wide(swap(total.astype(BF), "clip", self.sizes, step))
            step *= 2
        self.total = total.astype(BF)
        return self.total


class Pair:
    def __init__(self, moves, one, two):
        self.moves, self.sizes, self.one, self.two = moves, moves.sizes, one, two

    def fourth(self, *deps):
        one, two = self.one.total, self.two.total
        if deps:
            one = after(one, *deps)
        low = jnp.stack([one, two], 1)
        self.mine = low[0]
        self.pieces = [swap(low[j], "wide", self.sizes, 2 * j) for j in range(1, low.shape[0])]
        return low

    def fifth(self, *deps):
        result = wide(after(self.mine, *deps) if deps else self.mine)
        for piece in self.pieces:
            result = result + wide(piece)
        self.mine = result.astype(BF)
        self.arrived = swap(self.mine, "clip", self.sizes)
        return self.mine

    def halves(self, which, matrix, count):
        first = self.moves.clip_bit == 0
        columns = self.mine.shape[2] // count
        part = slice(matrix * columns, (matrix + 1) * columns)
        mine, arrived = self.mine[which, :, part], self.arrived[which, :, part]
        return jnp.concatenate(
            [wide(jnp.where(first, mine, arrived)), wide(jnp.where(first, arrived, mine))], -1
        )


def frame_groups(frames, grid_a, grid_b):
    groups = [(i * grid_a, grid_a, None) for i in range(frames)]
    base = frames * grid_a
    if frames % 2 == 0:
        groups += [(base + i * grid_b, 2 * grid_b, ("block", grid_b, 1)) for i in range(0, frames, 2)]
    else:
        groups += [(base + i * grid_b, grid_b, None) for i in range(frames)]
    return tuple(groups)


def per_device(
    sizes,
    frames_a,
    frames_b,
    actions_a,
    actions_b,
    action_table,
    gain_space,
    space_qkv,
    space_out,
    gain_time,
    time_qkv,
    time_out,
    gain_ffn,
    ffn_up,
    ffn_down,
    cot_a,
    cot_b,
):
    moves = Moves(sizes)
    n_wide = sizes["wide"]
    _, n_frames, grid_a, depth = frames_a.shape
    grid_b = frames_b.shape[2]
    rows_a, rows_b = n_frames * grid_a, n_frames * grid_b
    rows = rows_a + rows_b
    spots_a, spots_b = grid_a // n_wide, grid_b // n_wide
    spots = spots_a + spots_b
    all_frames = n_frames * n_wide
    inner = 8 if spots % 8 == 0 else 4
    gain_space, gain_time, gain_ffn = (g[None] for g in (gain_space, gain_time, gain_ffn))

    def exchange(packed):
        return lax.all_to_all(packed, "wide", split_axis=0, concat_axis=0, tiled=True)

    def pack_grid(first, second):
        first = first.reshape(n_frames, n_wide, spots_a, depth)
        second = second.reshape(n_frames, n_wide, spots_b, depth)
        return jnp.concatenate([first, second], 2).transpose(1, 0, 2, 3)

    def unpack_grid(moved):
        moved = moved.reshape(all_frames, spots // inner, inner, depth)
        return moved.transpose(1, 0, 2, 3).reshape(rows, depth)

    def pack_frames(rows_in):
        packed = rows_in.reshape(spots // inner, n_wide, n_frames, inner, depth)
        return packed.transpose(1, 2, 0, 3, 4).reshape(n_wide, n_frames, spots, depth)

    def unpack_frames(moved):
        first = moved[:, :, :spots_a].transpose(1, 0, 2, 3).reshape(rows_a, depth)
        second = moved[:, :, spots_a:].transpose(1, 0, 2, 3).reshape(rows_b, depth)
        return jnp.concatenate([first, second])

    def both_clips(mine, partner):
        low = moves.tp == 0
        pair = jnp.stack([jnp.where(low, mine, partner), jnp.where(low, partner, mine)])
        return (
            pair[:, :rows_a].reshape(2, n_frames, grid_a, depth),
            pair[:, rows_a:].reshape(2, n_frames, grid_b, depth),
        )

    def pick(value):
        return lax.dynamic_index_in_dim(value, moves.tp, 0, keepdims=False)

    space_groups = frame_groups(n_frames, grid_a, grid_b)
    group = inner * all_frames
    time_groups = tuple((i, group, ("causal", all_frames, inner)) for i in range(0, rows, group))
    codes = jnp.arange(action_table.shape[0])
    acts = jnp.concatenate([actions_a, actions_b], 1)
    one_hot = (acts[:, :, None] == codes).astype(F32)
    shifts = jnp.einsum("cfa,ad->cfd", one_hot, action_table.astype(F32), precision=lax.Precision.HIGHEST)

    clip = moves.tp[None].astype(jnp.int32)
    n_codes = action_table.shape[0]

    def from_x(weight, axis, *deps):
        piece = moves.quarter(weight, axis)
        return swap(after(piece, *deps) if deps else piece, "tp", sizes)

    def from_y(value, *deps):
        return swap(after(value, *deps) if deps else value, "clip", sizes)

    def cores(value, *deps):
        return swap(after(value, *deps) if deps else value, "wide", sizes)

    tokens = []

    def product(left_arrays, terms, chunk, y_first, name):
        return grad_product(moves.bits, left_arrays, terms, chunk, y_first, sizes, name)

    def both(value, *deps):
        return (value, cores(value, *deps))

    so_piece = moves.quarter(space_out, 0)
    out_piece = moves.quarter(time_out, 0)
    out_piece = out_piece.reshape(PAIR, -1, PAIR).transpose(1, 0, 2).reshape(1, -1, PAIR)
    time_piece = jnp.concatenate([moves.quarter(time_qkv, 2), out_piece])
    cot_packed = pack_grid(after(pick(cot_a), so_piece, time_piece), pick(cot_b))
    so_x = swap(so_piece, "tp", sizes)
    time_x = swap(time_piece, "tp", sizes)
    cot_moved = exchange(cot_packed)
    token = pause(tokens, so_piece, time_piece, cot_packed)
    cot_moved = after(cot_moved, token)
    (partner_heads,) = space_heads(
        after(1 - clip, token),
        frames_a, frames_b, shifts, gain_space, space_qkv, space_groups, False,
    )
    heads_other = swap(partner_heads, "tp", sizes)
    so_y = from_y(so_x, partner_heads)
    heads_own, proj_own, logs_own, started, normed_space = space_heads(
        after(clip, partner_heads), frames_a, frames_b, shifts, gain_space, space_qkv, space_groups, True
    )
    so_x, so_y = after(so_x, heads_own), after(so_y, heads_own)
    so_slots = (so_x, cores(so_x), so_y, cores(so_y))
    up_piece = moves.quarter(ffn_up, 1)
    down_piece = moves.quarter(ffn_down, 0)
    up_x = swap(after(up_piece, heads_other), "tp", sizes)
    token = pause(tokens, heads_other, up_piece, down_piece)
    middle = space_mix(moves.bits, after(started, token), heads_own, heads_other, space_out, so_slots)
    packed = pack_grid(middle[:rows_a], middle[rows_a:])
    middle_moved = exchange(after(packed, cot_moved))
    time_x = after(time_x, packed)
    time_y = swap(time_x, "clip", sizes)
    time_x_core = cores(time_x)
    token = pause(tokens, packed)

    up_x = after(up_x, token)
    up_y = swap(up_x, "clip", sizes)
    up_x_core = cores(up_x)
    down_x = swap(after(down_piece, up_x), "tp", sizes)
    token = pause(tokens, up_x)
    time_y = after(time_y, token)
    time_slots = (time_x, time_x_core, time_y, cores(time_y))
    down_x = after(down_x, token)
    down_y = swap(down_x, "clip", sizes)
    down_x_core = cores(down_x)
    sq_x = swap(after(moves.quarter(space_qkv, 2), down_x), "tp", sizes)
    token = pause(tokens, time_y, down_x)
    middle = unpack_grid(after(middle_moved, token))
    latest, normed_time, heads_time, proj_time, logs_time = time_forward(
        middle, gain_time, time_qkv, time_out, time_slots, time_groups
    )
    cot = unpack_grid(after(cot_moved, latest))
    width = ffn_up.shape[1] // 4
    normed_ffn, hidden_own, total_ffn, d_sum_ffn = feed_forward(latest, cot, gain_ffn, (ffn_up, ffn_down), width)
    up_y, down_y = after(up_y, hidden_own), after(down_y, hidden_own)
    up_slots = (up_x, up_x_core, up_y, cores(up_y))
    down_slots = (down_x, down_x_core, down_y, cores(down_y))
    out, d_latest, hidden_rest, d_gain_ffn = feed_forward(
        latest, cot, gain_ffn, (*up_slots, *down_slots), width, (normed_ffn, total_ffn, d_sum_ffn)
    )

    out_packed = pack_frames(out)
    out_moved = exchange(out_packed)
    normed_time2, heads_time2 = both(normed_time, latest), both(heads_time[:, None], latest)
    cot2, normed_ffn2, hidden2 = both(cot, latest), both(normed_ffn, latest), both(hidden_own)
    hidden_rest2 = both(hidden_rest)
    partial_time, d_proj_own = branch_back(
        "time_back", after(d_latest, out_packed), proj_time, logs_time, 0,
        (time_qkv, time_out), time_groups,
    )
    own = (both(d_proj_own), 0)
    d_latest2 = both(d_latest, partial_time)
    sq_x = after(sq_x, partial_time)
    sq_y = swap(sq_x, "clip", sizes)
    chunk = ffn_up.shape[1] // 4
    up = product(
        [(after(normed_ffn2[0], partial_time), normed_ffn2[1])],
        [(0, (hidden2, 0), (hidden_rest2, 0), 1, 1)], chunk, False, "grad_up",
    )
    up = moves.reduction(up, False)
    sq_x, sq_y = after(sq_x, up.keep), after(sq_y, up.keep, d_latest2[1])
    sq_slots = (sq_x, cores(sq_x), sq_y, cores(sq_y))
    down = product(
        [(after(cot2[0], up.keep), cot2[1])], [(0, (hidden2, 0), (hidden_rest2, 0), 0, 1)], chunk, True, "grad_down"
    )
    down = moves.reduction(down, True)
    out_rows = unpack_frames(after(out_moved, down.keep))
    out_partner = swap(out_rows, "tp", sizes)
    d_middle, d_proj_rest, d_gain_time, _ = branch_back(
        "time_back_end", d_latest, proj_time, logs_time, 2, (time_slots,), time_groups,
        (middle, gain_time, after(partial_time, out_rows)), ((0, rows),),
    )
    rest = (both(d_proj_rest), 0)
    packed = pack_frames(d_middle)
    d_middle = exchange(packed)
    gate = up.third(packed)
    time_one = product(
        [(after(normed_time, gate), normed_time2[1])], [(0, own, rest, 0, 2)], PAIR, False, "time_one"
    )
    time_one = moves.reduction(time_one, False)
    time_two = product(
        [(normed_time, normed_time2[1]), (after(d_latest, time_one.keep), d_latest2[1])],
        [(0, own, rest, 2, 1), (1, (heads_time2, 0), (heads_time2, 1), 0, 1)],
        PAIR, True, "time_two",
    )
    time_two = moves.reduction(time_two, True)
    gate = down.third(time_two.keep)
    out_a, out_b = both_clips(out_rows, after(out_partner, gate))
    heads_rest, proj_rest, logs_rest = space_rest(
        after(normed_space, gate, out_a, out_b), sq_slots, space_groups
    )
    heads_rest2 = both(heads_rest[:, None])
    heads_own2, normed_space2 = both(heads_own[:, None], heads_rest), both(normed_space, heads_rest)
    gate = time_one.third(heads_rest)
    d_middle = unpack_frames(after(d_middle, gate))
    d_middle2 = both(d_middle)
    partial_space, d_proj_own = branch_back(
        "space_back", d_middle, proj_own, logs_own, 0, (space_qkv, space_out), space_groups
    )
    own = (both(d_proj_own), 0)
    ffn, time = Pair(moves, up, down), Pair(moves, time_one, time_two)
    gates = [time_two.third(partial_space)]
    gates += [up.sum(gates[0]), down.sum(gates[0])]
    ffn.fourth()
    token = pause(tokens, *gates)
    segments = tuple((i * grid_a, grid_a) for i in range(n_frames)) + tuple(
        (rows_a + i * grid_b, grid_b) for i in range(n_frames)
    )
    d_started, d_proj_rest, d_gain_space, frame_sums = branch_back(
        "space_back_end", d_middle, proj_rest, logs_rest, 0, (sq_slots, so_slots), space_groups,
        (started, gain_space, after(partial_space, token)), segments, True,
    )
    rest = (both(d_proj_rest), 0)
    started_partner = swap(d_started, "tp", sizes)
    d_table = jnp.einsum(
        "fa,fd->ad", pick(one_hot), frame_sums[: 2 * n_frames], precision=lax.Precision.HIGHEST
    )
    small, small_other = moves.small_first(jnp.concatenate([d_table, d_gain_space, d_gain_time, d_gain_ffn]))
    gates = [time_one.sum(d_started), time_two.sum(d_started)]
    time.fourth()
    space_two = product(
        [(after(normed_space, small, *gates), normed_space2[1]), d_middle2],
        [(0, own, rest, 2, 1), (1, (heads_own2, 0), (heads_rest2, 0), 0, 1)],
        PAIR, True, "space_two",
    )
    space_two = moves.reduction(space_two, True)
    small = small + after(small_other, space_two.keep)
    small_other = swap(small, "tp", sizes)
    space_one = product(
        [(after(normed_space, space_two.keep, small), normed_space2[1])], [(0, own, rest, 0, 2)], PAIR, False, "space_one"
    )
    space_one = moves.reduction(space_one, False)
    token = pause(tokens, space_one.keep)
    small = small + after(small_other, token)
    small_other = small
    step = 1
    while step < sizes["clip"]:
        small_other = swap(small, "clip", sizes, step)
        if 2 * step < sizes["clip"]:
            small = small + small_other
        step *= 2
    d_frames_a, d_frames_b = both_clips(d_started, after(started_partner, small))
    gate = space_two.third(d_frames_a, d_frames_b)
    gate2 = space_one.third(gate)
    gate3 = ffn.fifth(gate2)
    token = pause(tokens, gate, gate2, gate3)
    small = small + after(small_other, token)
    gates = [space_two.sum(token), space_one.sum(token)]
    space = Pair(moves, space_one, space_two)
    space.fourth()
    small = moves.small_last(after(small, *gates))
    gates += [time.fifth(gates[1])]
    token = pause(tokens, *gates)
    gate = space.fifth(token)
    token = pause(tokens, gate)
    ffn.arrived, time.arrived = after(ffn.arrived, gates[0]), after(time.arrived, token)
    space.arrived = after(space.arrived, token)

    small = small + sum(tokens)[:1, :1]

    def qkv(pair):
        return jnp.stack([pair.halves(0, 0, 2), pair.halves(0, 1, 2), pair.halves(1, 0, 2)])

    return (
        out_a,
        out_b,
        d_frames_a,
        d_frames_b,
        small[:n_codes],
        small[n_codes],
        qkv(space),
        space.halves(1, 1, 2).T,
        small[n_codes + 1],
        qkv(time),
        time.halves(1, 1, 2).T,
        small[n_codes + 2],
        ffn.halves(0, 0, 1),
        ffn.halves(1, 0, 1).T,
    )


def solution(mesh):
    sizes = dict(mesh.shape)
    return jax.shard_map(
        partial(per_device, sizes),
        mesh=mesh,
        in_specs=(
            P("clip", "wide", None, None),
            P("clip", "wide", None, None),
            P("clip", "wide"),
            P("clip", "wide"),
            P(),
            P(),
            P(None, None, "tp"),
            P("tp", None),
            P(),
            P(None, None, "tp"),
            P("tp", None),
            P(),
            P(None, "tp"),
            P("tp", None),
            P("clip", "wide", None, None),
            P("clip", "wide", None, None),
        ),
        out_specs=(
            P("clip", "wide", None, None),
            P("clip", "wide", None, None),
            P("clip", "wide", None, None),
            P("clip", "wide", None, None),
            P(None, "wide"),
            P("wide"),
            P(None, "wide", "tp"),
            P("tp", "wide"),
            P("wide"),
            P(None, "wide", "tp"),
            P("tp", "wide"),
            P("wide"),
            P("wide", "tp"),
            P("tp", "wide"),
        ),
        check_vma=False,
    )
```
